32 devices in a mesh: seq: 16 (over z, y, x), fsdp: 2 (over core).
Axes of the slice: x: 2, y: 2, z: 4, core: 2. Of those that a mesh axis runs over, the one named last changes fastest.
Arguments:
- inputs: bfloat16 [2, 2048, 1536], P('fsdp', 'seq'), may hold values from -6 to 6
- segment_ids: int32 [2, 2048], P('fsdp', 'seq'), may hold values from 0 to 3, never falling along the last dimension, each value on 1 to 1024 neighbouring positions
- cotangent: bfloat16 [2, 2048, 1536], P('fsdp', 'seq'), may hold values from -6 to 6
- norm_mixer: bfloat16 [1536], P(('seq', 'fsdp')), may hold values from 0.5 to 1.5
- in_proj: bfloat16 [1536, 6144], P(('seq', 'fsdp')), may hold values from -0.15625 to 0.15625
- conv_weight: bfloat16 [4, 3072], P(None, ('seq', 'fsdp')), may hold values from -3 to 3
- conv_bias: bfloat16 [3072], P(('seq', 'fsdp')), may hold values from -3 to 3
- state_proj: bfloat16 [3072, 128], P(('seq', 'fsdp')), may hold values from -0.109375 to 0.109375
- step_proj: bfloat16 [96, 3072], P(None, ('seq', 'fsdp')), may hold values from -0.625 to 0.625
- step_bias: bfloat16 [3072], P(('seq', 'fsdp')), may hold values from -5 to -1
- decay_log: bfloat16 [3072, 16], P(('seq', 'fsdp')), may hold values from -7 to 0.5
- skip_gain: bfloat16 [3072], P(('seq', 'fsdp')), may hold values from 0.5 to 1.5
- mixer_out: bfloat16 [3072, 1536], P(('seq', 'fsdp')), may hold values from -0.109375 to 0.109375
- norm_ffn_one: bfloat16 [1536], P(('seq', 'fsdp')), may hold values from 0.5 to 1.5
- gate_up_one: bfloat16 [1536, 8192], P(('seq', 'fsdp')), may hold values from -0.15625 to 0.15625
- down_one: bfloat16 [4096, 1536], P(('seq', 'fsdp')), may hold values from -0.09375 to 0.09375
- norm_attn: bfloat16 [1536], P(('seq', 'fsdp')), may hold values from 0.5 to 1.5
- qkv_proj: bfloat16 [1536, 4608], P(('seq', 'fsdp')), may hold values from -0.15625 to 0.15625
- attn_out: bfloat16 [1536, 1536], P(('seq', 'fsdp')), may hold values from -1.25 to 1.25
- norm_ffn_two: bfloat16 [1536], P(('seq', 'fsdp')), may hold values from 0.5 to 1.5
- gate_up_two: bfloat16 [1536, 8192], P(('seq', 'fsdp')), may hold values from -0.15625 to 0.15625
- down_two: bfloat16 [4096, 1536], P(('seq', 'fsdp')), may hold values from -0.09375 to 0.09375
Outputs:
- outputs: bfloat16 [2, 2048, 1536], P('fsdp', 'seq')
- grad_inputs: float32 [2, 2048, 1536], P('fsdp', 'seq')
- grad_norm_mixer: float32 [1536], P(('seq', 'fsdp'))
- grad_in_proj: float32 [1536, 6144], P(('seq', 'fsdp'))
- grad_conv_weight: float32 [4, 3072], P(None, ('seq', 'fsdp'))
- grad_conv_bias: float32 [3072], P(('seq', 'fsdp'))
- grad_state_proj: float32 [3072, 128], P(('seq', 'fsdp'))
- grad_step_proj: float32 [96, 3072], P(None, ('seq', 'fsdp'))
- grad_step_bias: float32 [3072], P(('seq', 'fsdp'))
- grad_decay_log: float32 [3072, 16], P(('seq', 'fsdp'))
- grad_skip_gain: float32 [3072], P(('seq', 'fsdp'))
- grad_mixer_out: float32 [3072, 1536], P(('seq', 'fsdp'))
- grad_norm_ffn_one: float32 [1536], P(('seq', 'fsdp'))
- grad_gate_up_one: float32 [1536, 8192], P(('seq', 'fsdp'))
- grad_down_one: float32 [4096, 1536], P(('seq', 'fsdp'))
- grad_norm_attn: float32 [1536], P(('seq', 'fsdp'))
- grad_qkv_proj: float32 [1536, 4608], P(('seq', 'fsdp'))
- grad_attn_out: float32 [1536, 1536], P(('seq', 'fsdp'))
- grad_norm_ffn_two: float32 [1536], P(('seq', 'fsdp'))
- grad_gate_up_two: float32 [1536, 8192], P(('seq', 'fsdp'))
- grad_down_two: float32 [4096, 1536], P(('seq', 'fsdp'))
The draws below stay inside these ranges and needn't reach their ends.
Inputs may be any that keep to these rules, and one draw needn't show every extreme that they name: `segment_ids`: along a stream the ids never fall; a document (one id within one sequence of 2048 tokens) holds at most 1024 tokens.
All inputs are finite; a program needn't handle non-finite values.
Results may differ from the reference program's by a relative error of at most 0.024.
Values may be sent and summed in bfloat16 or wider, within the bound.
A program may use at most 576 MiB of HBM per device.

```python
import math
import jax
import jax.numpy as jnp
import numpy as np
from jax import lax

D = 1536
DI = 3072
N = 16
K = 4
R = 96
FF = 4096
H = 12
HD = 128
WIN = 2048
STREAMS = 2
TOKENS = 2048
SEQ = 2048
SEG_COUNT = 4
SEG_MOST = 1024


def block_scale(rng, dims, split, least, largest):
    factor_of, own = 1.0, jax.random.fold_in(rng, 6)
    for position, blocks in split:
        draws = jnp.exp(jax.random.uniform(jax.random.fold_in(own, position), (blocks,), jnp.float32, least / len(split), largest / len(split)))
        factor_of = factor_of * jnp.repeat(draws, dims[position] // blocks).reshape([-1 if axis == position else 1 for axis in range(len(dims))])
    return factor_of


def profile(amount, total, bound, slope):
    loads = [(1 << 20) // math.isqrt(grade ** slope) + 1 for grade in range(2, amount + 1)]
    surplus, holding = total - bound - (amount - 1), [1] * (amount - 1)
    while surplus > 0:
        free = [i for i in range(amount - 1) if holding[i] < bound]
        whole, remaining = sum([loads[i] for i in free]), surplus
        for i in free:
            more = min(bound - holding[i], max(1, remaining * loads[i] // whole), surplus)
            holding[i] = holding[i] + more
            surplus = surplus - more
    return np.array([bound] + holding)


def ragged(stream_key, amount, total, reach, lean):
    if amount == 2:
        one = jax.random.randint(stream_key, (), max(1, total - reach), min(reach, total - 1) + 1)
        return jnp.stack([one, total - one])
    tallies = jnp.asarray(profile(amount, total, reach, lean), jnp.int32)
    twos = (amount - 1) // 2
    donor, taker = tallies[1:1 + 2 * twos:2], tallies[2:2 + 2 * twos:2]
    margin = jnp.minimum(donor - 1, reach - taker)
    moved = jax.random.randint(jax.random.fold_in(stream_key, 1), (twos,), 0, 1 << 20) % (margin + 1)
    tallies = tallies.at[1:1 + 2 * twos:2].set(donor - moved).at[2:2 + 2 * twos:2].set(taker + moved)
    return tallies[jax.random.permutation(jax.random.fold_in(stream_key, 2), amount)]


def noise(stream_key, dims, deviation, bound, pieces=(), kind=jnp.bfloat16):
    loudness = block_scale(stream_key, dims, pieces, -0.22, 0.18) if pieces else 1.0
    values = jax.random.normal(stream_key, dims, jnp.float32) * deviation * loudness
    return jnp.minimum(jnp.maximum(values, -bound), bound).astype(kind)


def setup_inputs(seed: int = 0) -> dict:
    key_list = jax.random.split(jax.random.key(seed), 23)
    return {
        "inputs": noise(key_list[0], (STREAMS, TOKENS, D), 1.0, 6.0, ((0, 2), (1, 16))),
        "segment_ids": jax.vmap(lambda own: jnp.searchsorted(jnp.cumsum(ragged(own, SEG_COUNT, TOKENS, SEG_MOST, 2)), jnp.arange(TOKENS), side="right"))(jax.random.split(key_list[1], STREAMS)).reshape((STREAMS, TOKENS)).astype(jnp.int32),
        "cotangent": noise(key_list[2], (STREAMS, TOKENS, D), 1.0, 6.0, ((0, 2), (1, 16))),
        "norm_mixer": jnp.clip(1.0 + 0.1 * jax.random.normal(key_list[3], (D,), jnp.float32), 0.5, 1.5).astype(jnp.bfloat16),
        "in_proj": noise(key_list[4], (D, 2 * DI), D ** -0.5, 0.15625, ((0, 32),)),
        "conv_weight": noise(key_list[5], (K, DI), K ** -0.5, 3.0, ((1, 32),)),
        "conv_bias": noise(key_list[6], (DI,), 0.5, 3.0, ((0, 32),)),
        "state_proj": noise(key_list[7], (DI, R + 2 * N), DI ** -0.5, 0.109375, ((0, 32),)),
        "step_proj": noise(key_list[8], (R, DI), R ** -0.5, 0.625, ((1, 32),)),
        "step_bias": jnp.clip(-5.0 + 4.0 * jax.random.uniform(key_list[9], (DI,), jnp.float32) ** block_scale(key_list[9], (DI,), ((0, 32),), -0.2, 0.2), -5.0, -1.0).astype(jnp.bfloat16),
        "decay_log": jnp.clip(-7.0 + 7.5 * jax.random.uniform(key_list[10], (DI, N), jnp.float32) ** block_scale(key_list[10], (DI, N), ((0, 32),), -0.2, 0.2), -7.0, 0.5).astype(jnp.bfloat16),
        "skip_gain": jnp.clip(0.5 + 1.0 * jax.random.uniform(key_list[11], (DI,), jnp.float32) ** block_scale(key_list[11], (DI,), ((0, 32),), -0.2, 0.2), 0.5, 1.5).astype(jnp.bfloat16),
        "mixer_out": noise(key_list[12], (DI, D), DI ** -0.5, 0.109375, ((0, 32),)),
        "norm_ffn_one": jnp.clip(1.0 + 0.1 * jax.random.normal(key_list[13], (D,), jnp.float32), 0.5, 1.5).astype(jnp.bfloat16),
        "gate_up_one": noise(key_list[14], (D, 2 * FF), D ** -0.5, 0.15625, ((0, 32),)),
        "down_one": noise(key_list[15], (FF, D), FF ** -0.5, 0.09375, ((0, 32),)),
        "norm_attn": jnp.clip(1.0 + 0.1 * jax.random.normal(key_list[16], (D,), jnp.float32), 0.5, 1.5).astype(jnp.bfloat16),
        "qkv_proj": noise(key_list[17], (D, 3 * D), D ** -0.5, 0.15625, ((0, 32),)),
        "attn_out": noise(key_list[18], (D, D), (D // 64) ** -0.5, 1.25, ((0, 32),)),
        "norm_ffn_two": jnp.clip(1.0 + 0.1 * jax.random.normal(key_list[19], (D,), jnp.float32), 0.5, 1.5).astype(jnp.bfloat16),
        "gate_up_two": noise(key_list[20], (D, 2 * FF), D ** -0.5, 0.15625, ((0, 32),)),
        "down_two": noise(key_list[21], (FF, D), FF ** -0.5, 0.09375, ((0, 32),)),
    }


EPS = 1e-05
HIGH = lax.Precision.HIGHEST
NEGATIVE = -1e+30

@jax.custom_vjp
def low(v):
    return lax.optimization_barrier(v.astype(jnp.bfloat16)).astype(jnp.float32)

@jax.custom_vjp
def low_back(v):
    return v

def low_keep(v):
    return (low(v), None)

def low_pass(kept, grad):
    return (grad,)

def back_keep(v):
    return (v, None)

def back_low(kept, grad):
    return (low(grad),)
low.defvjp(low_keep, low_pass)
low_back.defvjp(back_keep, back_low)

def matmul_high(left_side, right_side):
    return jnp.dot(left_side, right_side, precision=HIGH, preferred_element_type=jnp.float32)

def rms_norm(values, norm_gain):
    return values * lax.rsqrt(lax.optimization_barrier(jnp.mean(values * values, axis=-1, keepdims=True)) + EPS) * norm_gain

def rope_angles(positions):
    half_size = HD // 2
    inverse = jnp.exp(jnp.arange(half_size, dtype=jnp.float32) * (-math.log(10000.0) * 2.0 / HD))
    return positions.astype(jnp.float32)[:, None] * inverse[None, :]

def rotate(values, angles):
    half_size = values.shape[-1] // 2
    cosine = jnp.cos(angles)[:, None, :]
    sine_part = jnp.sin(angles)[:, None, :]
    first_half = values[..., :half_size]
    second_half = values[..., half_size:]
    return jnp.concatenate([first_half * cosine - second_half * sine_part, second_half * cosine + first_half * sine_part], axis=-1)

def scan_tokens(step_rate, u_values, in_mat, out_mat, keep_flag, decay_rate, block_size):
    tokens, inner_width = step_rate.shape

    def token_step(state_now, token_item):
        rate_now, input_now, in_now, out_now, keep_now = token_item
        state_now = jnp.exp(rate_now[:, None] * decay_rate) * keep_now * state_now + (rate_now * input_now)[:, None] * in_now[None, :]
        return (state_now, jnp.dot(state_now, out_now, precision=HIGH))

    def block_step(state_now, block_items):
        return lax.scan(token_step, state_now, block_items)
    blocked = tuple((member.reshape((tokens // block_size, block_size) + member.shape[1:]) for member in (step_rate, u_values, in_mat, out_mat, keep_flag)))
    state_now, outputs = lax.scan(jax.checkpoint(block_step), jnp.zeros_like(decay_rate), blocked)
    return (outputs.reshape(tokens, inner_width), state_now)

def feed_forward(layer_in, norm_gain, gate_up, down_proj):
    normed = low(rms_norm(layer_in, norm_gain))
    hidden_pre = low_back(matmul_high(normed, gate_up))
    hidden = low(jax.nn.silu(hidden_pre[:, :FF]) * hidden_pre[:, FF:])
    return layer_in + low_back(matmul_high(hidden, down_proj))

def attend(queries, keys_all, values_all, seg_ids, sequence_now):
    tokens = queries.shape[0]
    block_size = min(512, tokens)
    score_scale = HD ** (-0.5)
    pad_keys = jnp.concatenate([jnp.zeros((WIN, H, HD), jnp.float32), keys_all], axis=0)
    pad_values = jnp.concatenate([jnp.zeros((WIN, H, HD), jnp.float32), values_all], axis=0)
    pad_segs = jnp.concatenate([jnp.full((WIN,), -1, jnp.int32), seg_ids], axis=0)
    pad_seqs = jnp.concatenate([jnp.full((WIN,), -1, jnp.int32), sequence_now], axis=0)

    def one_block(start_row):
        query_blk = lax.dynamic_slice_in_dim(queries, start_row, block_size, 0)
        key_blk = lax.dynamic_slice_in_dim(pad_keys, start_row, block_size + WIN, 0)
        value_blk = lax.dynamic_slice_in_dim(pad_values, start_row, block_size + WIN, 0)
        qseg = lax.dynamic_slice_in_dim(seg_ids, start_row, block_size, 0)
        qseq = lax.dynamic_slice_in_dim(sequence_now, start_row, block_size, 0)
        kseg = lax.dynamic_slice_in_dim(pad_segs, start_row, block_size + WIN, 0)
        kseq = lax.dynamic_slice_in_dim(pad_seqs, start_row, block_size + WIN, 0)
        query_pos = start_row + jnp.arange(block_size, dtype=jnp.int32)
        key_pos = start_row - WIN + jnp.arange(block_size + WIN, dtype=jnp.int32)
        distance_back = query_pos[:, None] - key_pos[None, :]
        key_mask = (key_pos[None, :] >= 0) & (distance_back >= 0) & (distance_back < WIN) & (kseg[None, :] == qseg[:, None]) & (kseq[None, :] == qseq[:, None])
        scores = low_back(jnp.einsum('thd,shd->hts', query_blk, key_blk, precision=HIGH) * score_scale)
        masked = jnp.where(key_mask[None], scores, NEGATIVE)
        top_score = lax.optimization_barrier(jnp.max(masked, axis=-1, keepdims=True))
        exp_scores = jnp.exp(masked - top_score)
        soft_weights = exp_scores / lax.optimization_barrier(jnp.sum(exp_scores, axis=-1, keepdims=True))
        return jnp.einsum('hts,shd->thd', low(soft_weights), value_blk, precision=HIGH)
    starts = (jnp.arange(tokens // block_size, dtype=jnp.int32) * block_size).astype(jnp.int32)
    outputs = lax.map(jax.checkpoint(one_block), starts)
    return outputs.reshape(tokens, H, HD)

def stream_forward(layer_in, seg_ids, params):
    norm_mixer, in_proj, conv_weight, conv_bias, state_proj, step_proj, step_bias, decay_log, skip_gain, mixer_out, norm_ffn_one, gate_up_one, down_one, norm_attn, qkv_proj, attn_out, norm_ffn_two, gate_up_two, down_two = params
    tokens = layer_in.shape[0]
    positions = jnp.arange(tokens, dtype=jnp.int32)
    sequence_now = positions // SEQ
    normed = low(rms_norm(layer_in, norm_mixer))
    mixed_proj = low_back(matmul_high(normed, in_proj))
    stream_part = mixed_proj[:, :DI]
    gate_part = mixed_proj[:, DI:]
    conv_sum = jnp.broadcast_to(conv_bias[None, :], (tokens, DI))
    for offset in range(K):
        back_by = K - 1 - offset
        shifted = jnp.concatenate([jnp.zeros((back_by, DI), jnp.float32), stream_part[:tokens - back_by]], axis=0)
        seg_back = jnp.concatenate([jnp.full((back_by,), -1, jnp.int32), seg_ids[:tokens - back_by]], axis=0)
        seq_back = jnp.concatenate([jnp.full((back_by,), -1, jnp.int32), sequence_now[:tokens - back_by]], axis=0)
        valid = ((seg_back == seg_ids) & (seq_back == sequence_now)).astype(jnp.float32)
        conv_sum = conv_sum + conv_weight[offset] * shifted * valid[:, None]
    u_values = jax.nn.silu(conv_sum)
    projected = low_back(matmul_high(low(u_values), state_proj))
    dt_low = low(projected[:, :R])
    in_mat = projected[:, R:R + N]
    out_mat = projected[:, R + N:]
    step_rate = jax.nn.softplus(low_back(matmul_high(dt_low, step_proj)) + step_bias)
    decay_rate = -jnp.exp(decay_log)
    seg_prev = jnp.concatenate([jnp.full((1,), -1, jnp.int32), seg_ids[:-1]], axis=0)
    starts = (positions % SEQ == 0) | (seg_prev != seg_ids)
    keep_flag = jnp.where(starts, 0.0, 1.0).astype(jnp.float32)
    scanned, last_state = scan_tokens(step_rate, u_values, in_mat, out_mat, keep_flag, decay_rate, min(64, tokens))
    y_values = scanned + skip_gain * u_values
    gated_low = low(y_values * jax.nn.silu(gate_part))
    after_mixer = layer_in + low_back(matmul_high(gated_low, mixer_out))
    after_ffn = feed_forward(after_mixer, norm_ffn_one, gate_up_one, down_one)
    normed_attn = low(rms_norm(after_ffn, norm_attn))
    qkv_all = low_back(matmul_high(normed_attn, qkv_proj))
    angles = rope_angles(positions % SEQ)
    queries = low(rotate(qkv_all[:, :D].reshape(tokens, H, HD), angles))
    keys_all = low(rotate(qkv_all[:, D:2 * D].reshape(tokens, H, HD), angles))
    values_all = low(qkv_all[:, 2 * D:].reshape(tokens, H, HD))
    attended = attend(queries, keys_all, values_all, seg_ids, sequence_now)
    att_low = low(low_back(attended)).reshape(tokens, D)
    after_attn = after_ffn + low_back(matmul_high(att_low, attn_out))
    return feed_forward(after_attn, norm_ffn_two, gate_up_two, down_two)

def reference(inputs, segment_ids, cotangent, norm_mixer, in_proj, conv_weight, conv_bias, state_proj, step_proj, step_bias, decay_log, skip_gain, mixer_out, norm_ffn_one, gate_up_one, down_one, norm_attn, qkv_proj, attn_out, norm_ffn_two, gate_up_two, down_two):
    params = tuple((member.astype(jnp.float32) for member in (norm_mixer, in_proj, conv_weight, conv_bias, state_proj, step_proj, step_bias, decay_log, skip_gain, mixer_out, norm_ffn_one, gate_up_one, down_one, norm_attn, qkv_proj, attn_out, norm_ffn_two, gate_up_two, down_two)))
    layer_in = inputs.astype(jnp.float32)

    def forward(acts_in, params_in):
        return jnp.stack([stream_forward(acts_in[stream], segment_ids[stream], params_in) for stream in range(acts_in.shape[0])])
    final_out, pullback = jax.vjp(forward, layer_in, params)
    grad_in, grad_params = pullback(cotangent.astype(jnp.float32))
    g_norm_mixer, g_in_proj, g_conv_weight, g_conv_bias, g_state_proj, g_step_proj, g_step_bias, g_decay_log, g_skip_gain, g_mixer_out, g_norm_ffn_one, g_gate_up_one, g_down_one, g_norm_attn, g_qkv_proj, g_attn_out, g_norm_ffn_two, g_gate_up_two, g_down_two = grad_params
    return (final_out.astype(jnp.bfloat16), grad_in, g_norm_mixer, g_in_proj, g_conv_weight, g_conv_bias, g_state_proj, g_step_proj, g_step_bias, g_decay_log, g_skip_gain, g_mixer_out, g_norm_ffn_one, g_gate_up_one, g_down_one, g_norm_attn, g_qkv_proj, g_attn_out, g_norm_ffn_two, g_gate_up_two, g_down_two)
```

```python
import functools
import math

import jax
import jax.numpy as jnp
from jax import lax
from jax.experimental import pallas as pl
from jax.experimental.pallas import tpu as pltpu
from jax.sharding import Mesh
from jax.sharding import PartitionSpec as P

W = 4
H = 12
HD = 128
WIN = 2048
SEQ_MAX = 8192
EPS = 1e-05
NEG = -1e30
BIG = 1e30
LOG2E = 1.4426950408889634
BF = jnp.bfloat16
F32 = jnp.float32
MESH = pl.DeviceIdType.MESH
HALO = 16
SUB = 64
MIB = 1 << 20


def vmem():
    return pl.BlockSpec(memory_space=pltpu.VMEM)


def hbm():
    return pl.BlockSpec(memory_space=pl.ANY)


def smem():
    return pl.BlockSpec(memory_space=pltpu.SMEM)


def here():
    return lax.axis_index("t"), lax.axis_index("p"), lax.axis_index("c")


def greet(device):
    pl.semaphore_signal(
        pltpu.get_barrier_semaphore(), inc=1, device_id=device, device_id_type=MESH
    )


def arrive(count):
    pl.semaphore_wait(pltpu.get_barrier_semaphore(), count)


def arrive_some(count):
    @pl.when(count > 0)
    def _():
        arrive(count)


def remote(src, dst, send, recv, device):
    return pltpu.make_async_remote_copy(
        src_ref=src,
        dst_ref=dst,
        send_sem=send,
        recv_sem=recv,
        device_id=device,
        device_id_type=MESH,
    )


def flip(p, d):
    return lax.bitwise_xor(p, d)


def dma(*shape):
    return pltpu.SemaphoreType.DMA(shape)


def talk(cid, limit=40):
    return pltpu.CompilerParams(
        collective_id=cid, has_side_effects=True, vmem_limit_bytes=limit * MIB
    )


def alone(limit=56):
    return pltpu.CompilerParams(vmem_limit_bytes=limit * MIB)


def out(shape, dtype=F32):
    return jax.ShapeDtypeStruct(shape, dtype)


def unit(x):
    return x * lax.rsqrt(jnp.mean(x * x, axis=-1, keepdims=True) + EPS)


def start_body(
    T, x, seg, par, win, nh, seg_out, par_out, win_out, nbuf, zbuf,
    s_n, r_n, s_h, r_h, s_s, r_s, s_p, r_p, s_w, r_w, s_l,
):
    t, p, c = here()
    B = x.shape[0]
    count = 0
    for dt in range(T):
        tt = lax.rem(t + dt, T)
        for dp in range(W):
            pp = flip(p, dp)
            if dt or dp:
                greet((tt, pp, c))
                count += 1
            if dt == 0 or dp == 0:
                greet((tt, pp, 1 - c))
                count += 1
    nbuf[...] = unit(x[...].astype(F32)).astype(BF)
    zbuf[...] = jnp.zeros_like(zbuf)
    arrive(count)
    half = lax.div(p, 2)
    slot = lax.rem(p, 2) * 2 + c
    for q in range(W):
        mine = (p == q) & (half == c)

        @pl.when(jnp.logical_not(mine))
        def _():
            remote(win.at[q], win_out.at[slot], s_w.at[q], r_w.at[slot], (t, q, half)).start()

        @pl.when(mine)
        def _():
            pltpu.make_async_copy(win.at[q], win_out.at[slot], s_w.at[q]).start()

    rows = pl.ds(pl.multiple_of(HALO + p * B, HALO), B)
    copies = []
    for d in range(1, W):
        copies.append(remote(nbuf, nh.at[rows], s_n.at[d], r_n.at[d], (t, flip(p, d), c)))
    for dt in range(T):
        for dc in range(2):
            if dt or dc:
                copies.append(
                    remote(
                        par, par_out.at[t * 2 + c], s_p.at[dt, dc], r_p.at[dt, dc],
                        (lax.rem(t + dt, T), p, flip(c, dc)),
                    )
                )
    for dt in range(T):
        for dp in range(W):
            if dt or dp:
                copies.append(
                    remote(
                        seg, seg_out.at[t * W + p], s_s.at[dt, dp], r_s.at[dt, dp],
                        (lax.rem(t + dt, T), flip(p, dp), c),
                    )
                )
    for copy in copies:
        copy.start()
    last = (p == W - 1) & (t < T - 1)
    tail = nbuf.at[pl.ds(B - HALO, HALO)]
    head = nh.at[pl.ds(0, HALO)]

    def rim(q):
        return remote(tail, head, s_h.at[q], r_h, (lax.rem(t + 1, T), q, c))

    @pl.when(last)
    def _():
        for q in range(W):
            rim(q).start()

    local = [
        pltpu.make_async_copy(nbuf, nh.at[rows], s_l.at[0]),
        pltpu.make_async_copy(par, par_out.at[t * 2 + c], s_l.at[1]),
        pltpu.make_async_copy(seg, seg_out.at[t * W + p], s_l.at[2]),
    ]
    for copy in local:
        copy.start()

    @pl.when(t == 0)
    def _():
        clear = pltpu.make_async_copy(zbuf, head, s_l.at[3])
        clear.start()
        clear.wait()

    for copy in local:
        copy.wait()
    for copy in copies:
        copy.wait()

    @pl.when(last)
    def _():
        for q in range(W):
            rim(q).wait_send()

    @pl.when(t > 0)
    def _():
        rim(0).wait_recv()

    for q in range(W):
        mine = (p == q) & (half == c)

        @pl.when(jnp.logical_not(mine))
        def _():
            remote(win.at[q], win_out.at[slot], s_w.at[q], r_w.at[slot], (t, q, half)).wait_send()

        @pl.when(mine)
        def _():
            pltpu.make_async_copy(win.at[q], win_out.at[slot], s_w.at[q]).wait()

    for j in range(W):
        own = (half == c) & (slot == j)

        @pl.when(jnp.logical_not(own))
        def _():
            remote(win.at[0], win_out.at[j], s_w.at[0], r_w.at[j], (t, 0, half)).wait_recv()


def start_call(T, x, seg, par, win):
    B, D = x.shape
    return pl.pallas_call(
        functools.partial(start_body, T),
        out_shape=(
            out((HALO + W * B, D), BF),
            out((W * T,) + seg.shape, jnp.int32),
            out((2 * T,) + par.shape, BF),
            out(win.shape, BF),
        ),
        in_specs=[vmem(), hbm(), hbm(), hbm()],
        out_specs=(hbm(), hbm(), hbm(), hbm()),
        scratch_shapes=[
            pltpu.VMEM((B, D), BF),
            pltpu.VMEM((HALO, D), BF),
            dma(W), dma(W), dma(W), pltpu.SemaphoreType.DMA,
            dma(T, W), dma(T, W), dma(T, 2), dma(T, 2), dma(W), dma(W), dma(4),
        ],
        compiler_params=talk(0),
        name="start",
    )(x, seg, par, win)


def spread_body(n, back, *refs):
    srcs, dsts = refs[:n], refs[n : 2 * n]
    s_w, r_w = refs[2 * n :]
    t, p, c = here()
    half = lax.div(p, 2)
    pair = lax.rem(p, 2) * 2 + c
    both = half == c

    def there(q):
        if back:
            return (t, c * 2 + q // 2, jnp.int32(q % 2))
        return (t, jnp.int32(q), half)

    def comes(j):
        if back:
            return (t, jnp.int32(j), half)
        return (t, c * 2 + j // 2, jnp.int32(j % 2))

    slot = p if back else pair
    for q in range(W):
        to, source = there(q), comes(q)
        own = both & ((pair == q) if back else (p == q))
        from_me = both & ((p == q) if back else (pair == q))

        @pl.when(jnp.logical_not(from_me))
        def _():
            greet(source)

    arrive(W - both.astype(jnp.int32))
    for q in range(W):
        own = both & ((pair == q) if back else (p == q))
        for a in range(n):

            @pl.when(jnp.logical_not(own))
            def _():
                remote(
                    srcs[a].at[q], dsts[a].at[slot], s_w.at[a, q], r_w.at[a, slot], there(q)
                ).start()

            @pl.when(own)
            def _():
                pltpu.make_async_copy(srcs[a].at[q], dsts[a].at[slot], s_w.at[a, q]).start()

    for q in range(W):
        own = both & ((pair == q) if back else (p == q))
        from_me = both & ((p == q) if back else (pair == q))
        for a in range(n):

            @pl.when(jnp.logical_not(own))
            def _():
                remote(
                    srcs[a].at[q], dsts[a].at[slot], s_w.at[a, q], r_w.at[a, slot], there(q)
                ).wait_send()

            @pl.when(own)
            def _():
                pltpu.make_async_copy(srcs[a].at[q], dsts[a].at[slot], s_w.at[a, q]).wait()

            @pl.when(jnp.logical_not(from_me))
            def _():
                remote(
                    srcs[a].at[q], dsts[a].at[q], s_w.at[a, q], r_w.at[a, q], there(q)
                ).wait_recv()


def spread_call(cid, back, arrays):
    n = len(arrays)
    return pl.pallas_call(
        functools.partial(spread_body, n, back),
        out_shape=tuple(out(a.shape, a.dtype) for a in arrays),
        in_specs=[hbm()] * n,
        out_specs=(hbm(),) * n,
        scratch_shapes=[dma(n, W), dma(n, W)],
        compiler_params=talk(cid),
        name="spread%d" % cid,
    )(*arrays)


def plane_gather_body(x, o, ss, rs, ls):
    t, p, c = here()
    B = x.shape[0]
    for d in range(1, W):
        greet((t, flip(p, d), c))
    arrive(W - 1)
    rows = o.at[pl.ds(pl.multiple_of(p * B, B), B)]
    copies = [remote(x, rows, ss.at[d], rs.at[d], (t, flip(p, d), c)) for d in range(1, W)]
    local = pltpu.make_async_copy(x, rows, ls)
    for copy in copies + [local]:
        copy.start()
    for copy in copies + [local]:
        copy.wait()


def plane_gather(cid, x):
    return pl.pallas_call(
        plane_gather_body,
        out_shape=out((W * x.shape[0], x.shape[1]), x.dtype),
        in_specs=[hbm()],
        out_specs=hbm(),
        scratch_shapes=[dma(W), dma(W), pltpu.SemaphoreType.DMA],
        compiler_params=talk(cid),
        name="gather%d" % cid,
    )(x)


def plane_sum_body(x, o, sb, recv, ss, rs):
    t, p, c = here()
    for d in range(1, W):
        greet((t, flip(p, d), c))
    sb[...] = x[...].astype(BF)
    arrive(W - 1)
    copies = [
        remote(sb, recv.at[d - 1], ss.at[d - 1], rs.at[d - 1], (t, flip(p, d), c))
        for d in range(1, W)
    ]
    for copy in copies:
        copy.start()
    for copy in copies:
        copy.wait()
    total = x[...]
    for d in range(W - 1):
        total = total + recv[d].astype(F32)
    o[...] = total


def plane_sum(cid, x):
    return pl.pallas_call(
        plane_sum_body,
        out_shape=out(x.shape),
        in_specs=[vmem()],
        out_specs=vmem(),
        scratch_shapes=[
            pltpu.VMEM(x.shape, BF),
            pltpu.VMEM((W - 1,) + x.shape, BF),
            dma(W - 1),
            dma(W - 1),
        ],
        compiler_params=talk(cid),
        name="plane_sum%d" % cid,
    )(x)


def turn_body(back, gather, parts, *refs):
    refs = list(refs)
    part = refs.pop(0)
    x = refs.pop(0)
    g = refs.pop(0) if back else None
    o = refs.pop(0)
    gath = refs.pop(0) if gather else None
    own, recv, sbuf, ss, rs, ls, ss2, rs2, ls2 = refs
    t, p, c = here()
    B = x.shape[0]
    rows = B // parts
    for d in range(1, W):
        greet((t, flip(p, d), c))
    local = pltpu.make_async_copy(part.at[pl.ds(pl.multiple_of(p * B, B), B)], own, ls)
    local.start()
    arrive(W - 1)
    first = {}
    for k in range(parts):
        for d in range(1, W):
            q = flip(p, d)
            first[k, d] = remote(
                part.at[pl.ds(pl.multiple_of(q * B + k * rows, rows), rows)],
                recv.at[d - 1, pl.ds(k * rows, rows)],
                ss.at[d - 1, k],
                rs.at[d - 1, k],
                (t, q, c),
            )
            first[k, d].start()
    local.wait()
    later = []
    for k in range(parts):
        for d in range(1, W):
            first[k, d].wait_recv()
        cut = pl.ds(k * rows, rows)
        total = own[cut, :].astype(F32)
        for d in range(W - 1):
            total = total + recv[d, cut, :].astype(F32)
        value = x[cut, :]
        if back:
            r = lax.rsqrt(jnp.mean(value * value, axis=-1, keepdims=True) + EPS)
            hat = value * r
            new = g[cut, :] + r * (total - hat * jnp.mean(total * hat, axis=-1, keepdims=True))
        else:
            new = value + total
        o[cut, :] = new.astype(o.dtype)
        if gather:
            sbuf[cut, :] = (new if back else unit(new)).astype(BF)
            place = gath.at[pl.ds(pl.multiple_of(p * B + k * rows, rows), rows)]
            for d in range(1, W):
                later.append(
                    remote(sbuf.at[cut], place, ss2.at[d - 1, k], rs2.at[d - 1, k], (t, flip(p, d), c))
                )
            later.append(pltpu.make_async_copy(sbuf.at[cut], place, ls2.at[k]))
            for copy in later[-W:]:
                copy.start()
    for copy in first.values():
        copy.wait_send()
    for copy in later:
        copy.wait()


def turn(cid, part, x, g=None, gather=True, dtype=F32, parts=2):
    B, D = x.shape
    back = g is not None
    shapes = [out((B, D), dtype)]
    specs = [vmem()]
    if gather:
        shapes.append(out((W * B, D), BF))
        specs.append(hbm())
    args = (part, x) + ((g,) if back else ())
    return pl.pallas_call(
        functools.partial(turn_body, back, gather, parts),
        out_shape=tuple(shapes),
        in_specs=[hbm()] + [vmem()] * (len(args) - 1),
        out_specs=tuple(specs),
        scratch_shapes=[
            pltpu.VMEM((B, D), BF),
            pltpu.VMEM((W - 1, B, D), BF),
            pltpu.VMEM((B, D), BF),
            dma(W - 1, parts), dma(W - 1, parts), pltpu.SemaphoreType.DMA,
            dma(W - 1, parts), dma(W - 1, parts), dma(parts),
        ],
        compiler_params=talk(cid),
        name="turn%d" % cid,
    )(*args)


def chain_body(T, back, v, a2, h, recv, ss, rs):
    t, p, c = here()
    sign = -1 if back else 1
    for k in range(1, T):
        source = t - sign * k

        @pl.when((source >= 0) & (source < T))
        def _():
            greet((lax.rem(source + T, T), p, c))

    arrive_some(t if back else T - 1 - t)

    def send(k):
        to = lax.rem(t + sign * k + T, T)
        return remote(v, recv.at[k - 1], ss.at[k - 1], rs.at[k - 1], (to, p, c))

    for k in range(1, T):
        to = t + sign * k

        @pl.when((to >= 0) & (to < T))
        def _():
            send(k).start()

    h[...] = jnp.zeros_like(h)
    for k in range(T - 1, 0, -1):
        source = t - sign * k

        @pl.when((source >= 0) & (source < T))
        def _():
            send(k).wait_recv()
            decay = jnp.exp2(a2[...] * recv[k - 1, 16:17, :]) * recv[k - 1, 17:18, :]
            h[...] = recv[k - 1, 0:16, :] + decay * h[...]

    for k in range(1, T):
        to = t + sign * k

        @pl.when((to >= 0) & (to < T))
        def _():
            send(k).wait_send()


def chain(cid, T, back, v, a2):
    return pl.pallas_call(
        functools.partial(chain_body, T, back),
        out_shape=out(a2.shape),
        in_specs=[vmem(), vmem()],
        out_specs=vmem(),
        scratch_shapes=[pltpu.VMEM((T - 1,) + v.shape, F32), dma(T - 1), dma(T - 1)],
        compiler_params=talk(cid),
        name="chain%d" % cid,
    )(v, a2)


def rope(w, cosine, sine):
    return w * cosine + pltpu.roll(w, HD // 2, 1) * sine


def keys_body(T, hops, qkv, cosine, sine, q, k_all, v_all, ss, rs):
    t, p, c = here()
    CH = q.shape[0]
    width = q.shape[1]
    for d in range(1, hops + 1):

        @pl.when(t >= d)
        def _():
            greet((lax.rem(t - d + T, T), p, c))

    mine = pl.ds(hops * CH, CH)
    for h in range(width // HD):
        cols = pl.ds(h * HD, HD)
        q[:, cols] = rope(qkv[:, cols], cosine[...], sine[...]).astype(BF)
        k_all[mine, cols] = rope(
            qkv[:, pl.ds(width + h * HD, HD)], cosine[...], sine[...]
        ).astype(BF)
    v_all[mine, :] = qkv[:, pl.ds(2 * width, width)].astype(BF)
    arrive_some(jnp.minimum(hops, T - 1 - t))

    def send(a, d):
        ref = (k_all, v_all)[a]
        return remote(
            ref.at[mine],
            ref.at[pl.ds((hops - d) * CH, CH)],
            ss.at[a, d - 1],
            rs.at[a, d - 1],
            (lax.rem(t + d, T), p, c),
        )

    for d in range(1, hops + 1):

        @pl.when(t + d < T)
        def _():
            send(0, d).start()
            send(1, d).start()

    for d in range(1, hops + 1):

        @pl.when(t < d)
        def _():
            k_all[pl.ds((hops - d) * CH, CH), :] = jnp.zeros((CH, width), BF)
            v_all[pl.ds((hops - d) * CH, CH), :] = jnp.zeros((CH, width), BF)

        @pl.when(t >= d)
        def _():
            send(0, d).wait_recv()
            send(1, d).wait_recv()

        @pl.when(t + d < T)
        def _():
            send(0, d).wait_send()
            send(1, d).wait_send()


def keys_call(cid, T, hops, qkv, cosine, sine):
    CH = qkv.shape[0]
    width = qkv.shape[1] // 3
    return pl.pallas_call(
        functools.partial(keys_body, T, hops),
        out_shape=(
            out((CH, width), BF),
            out(((hops + 1) * CH, width), BF),
            out(((hops + 1) * CH, width), BF),
        ),
        in_specs=[vmem()] * 3,
        out_specs=(vmem(),) * 3,
        scratch_shapes=[dma(2, hops), dma(2, hops)],
        compiler_params=talk(cid),
        name="keys",
    )(qkv, cosine, sine)


def keys_back_body(T, hops, dq, dk, dv, cosine, sine, dqkv, sb, recv, ss, rs):
    t, p, c = here()
    CH = dq.shape[0]
    width = dq.shape[1]
    for d in range(1, hops + 1):

        @pl.when(t + d < T)
        def _():
            greet((lax.rem(t + d, T), p, c))

    for d in range(1, hops + 1):
        rows = pl.ds((hops - d) * CH, CH)
        sb[0, d - 1] = dk[rows, :].astype(BF)
        sb[1, d - 1] = dv[rows, :].astype(BF)
    arrive_some(jnp.minimum(hops, t))

    def send(a, d):
        return remote(
            sb.at[a, d - 1],
            recv.at[a, d - 1],
            ss.at[a, d - 1],
            rs.at[a, d - 1],
            (lax.rem(t - d + T, T), p, c),
        )

    for d in range(1, hops + 1):

        @pl.when(t >= d)
        def _():
            send(0, d).start()
            send(1, d).start()

    mine = pl.ds(hops * CH, CH)
    for h in range(width // HD):
        cols = pl.ds(h * HD, HD)
        dqkv[:, cols] = rope(dq[:, cols], cosine[...], -sine[...]).astype(BF)
    for d in range(1, hops + 1):

        @pl.when(t + d < T)
        def _():
            send(0, d).wait_recv()
            send(1, d).wait_recv()

        @pl.when(t + d >= T)
        def _():
            recv[0, d - 1] = jnp.zeros((CH, width), BF)
            recv[1, d - 1] = jnp.zeros((CH, width), BF)

        @pl.when(t >= d)
        def _():
            send(0, d).wait_send()
            send(1, d).wait_send()

    for h in range(width // HD):
        cols = pl.ds(h * HD, HD)
        k_sum = dk[mine, cols]
        v_sum = dv[mine, cols]
        for d in range(hops):
            k_sum = k_sum + recv[0, d, :, cols].astype(F32)
            v_sum = v_sum + recv[1, d, :, cols].astype(F32)
        dqkv[:, pl.ds(width + h * HD, HD)] = rope(k_sum, cosine[...], -sine[...]).astype(BF)
        dqkv[:, pl.ds(2 * width + h * HD, HD)] = v_sum.astype(BF)


def keys_back_call(cid, T, hops, dq, dk, dv, cosine, sine):
    CH, width = dq.shape
    return pl.pallas_call(
        functools.partial(keys_back_body, T, hops),
        out_shape=out((CH, 3 * width), BF),
        in_specs=[vmem()] * 5,
        out_specs=vmem(),
        scratch_shapes=[
            pltpu.VMEM((2, hops, CH, width), BF),
            pltpu.VMEM((2, hops, CH, width), BF),
            dma(2, hops),
            dma(2, hops),
        ],
        compiler_params=talk(cid, 48),
        name="keys_back",
    )(dq, dk, dv, cosine, sine)


def rim_body(T, x, o, recv, ss, rs):
    t, p, c = here()

    @pl.when(t < T - 1)
    def _():
        greet((lax.rem(t + 1, T), p, c))

    def send():
        return remote(x, recv, ss, rs, (lax.rem(t + T - 1, T), p, c))

    @pl.when(t > 0)
    def _():
        arrive(1)
        send().start()
        send().wait_send()

    o[...] = jnp.zeros_like(o)

    @pl.when(t < T - 1)
    def _():
        send().wait_recv()
        o[...] = recv[...]


def rim_back(cid, T, x):
    return pl.pallas_call(
        functools.partial(rim_body, T),
        out_shape=out(x.shape),
        in_specs=[vmem()],
        out_specs=vmem(),
        scratch_shapes=[pltpu.VMEM(x.shape, F32), pltpu.SemaphoreType.DMA, pltpu.SemaphoreType.DMA],
        compiler_params=talk(cid),
        name="rim_back",
    )(x)


def small_body(T, x, o, recv, ss, rs):
    t, p, c = here()
    peers = [(dt, dc) for dt in range(T) for dc in range(2) if dt or dc]

    def device(dt, dc):
        return lax.rem(t + dt, T), flip(c, dc)

    for dt, dc in peers:
        tt, cc = device(dt, dc)
        greet((tt, p, cc))
    arrive(len(peers))
    copies = []
    for i, (dt, dc) in enumerate(peers):
        tt, cc = device(dt, dc)
        copies.append(remote(x.at[tt * 2 + cc], recv.at[i], ss.at[i], rs.at[i], (tt, p, cc)))
        copies[-1].start()
    total = x[t * 2 + c].astype(F32)
    for i, copy in enumerate(copies):
        copy.wait()
        total = total + recv[i].astype(F32)
    o[...] = total


def small_sum(cid, T, x):
    n = x.shape[0] - 1
    return pl.pallas_call(
        functools.partial(small_body, T),
        out_shape=out(x.shape[1:]),
        in_specs=[vmem()],
        out_specs=vmem(),
        scratch_shapes=[pltpu.VMEM((n,) + x.shape[1:], x.dtype), dma(n), dma(n)],
        compiler_params=talk(cid),
        name="small_sum",
    )(x)


def conv_sum(xz, mask, taps, lo, size):
    width = taps.shape[1]
    total = jnp.broadcast_to(taps[4:5, :], (size, width))
    for j in range(4):
        rows = xz[pl.ds(lo + HALO - 3 + j, size), pl.ds(0, width)]
        total = total + taps[j : j + 1, :] * rows * mask[pl.ds(lo, size), j : j + 1]
    return total


def conv_body(xz, mask, taps, proj, u, u_low, part):
    CH = u.shape[0]
    step = min(CH, 128)
    for lo in range(0, CH, step):
        cut = pl.ds(lo, step)
        c = conv_sum(xz, mask, taps, lo, step)
        value = c / (1.0 + jnp.exp(-c))
        u[cut, :] = value
        low = value.astype(BF)
        u_low[cut, :] = low
        part[cut, :] = jnp.dot(low, proj[...], preferred_element_type=F32)


def conv_call(xz, mask, taps, proj):
    CH = mask.shape[0]
    width = taps.shape[1]
    return pl.pallas_call(
        conv_body,
        out_shape=(out((CH, width)), out((CH, width), BF), out((CH, proj.shape[1]))),
        in_specs=[vmem()] * 4,
        out_specs=(vmem(),) * 3,
        compiler_params=alone(),
        name="conv",
    )(xz, mask, taps, proj)


def conv_back_body(xz, mask, taps, du, dxs, grads):
    CH, width = du.shape
    step = min(CH, 128)
    dxs[...] = jnp.zeros_like(dxs)
    sums = [jnp.zeros((1, width), F32) for _ in range(5)]
    for lo in range(0, CH, step):
        c = conv_sum(xz, mask, taps, lo, step)
        s = 1.0 / (1.0 + jnp.exp(-c))
        dc = du[pl.ds(lo, step), :] * (s * (1.0 + c * (1.0 - s)))
        sums[4] = sums[4] + jnp.sum(dc, axis=0, keepdims=True)
        for j in range(4):
            rows = pl.ds(lo + HALO - 3 + j, step)
            live = dc * mask[pl.ds(lo, step), j : j + 1]
            sums[j] = sums[j] + jnp.sum(live * xz[rows, pl.ds(0, width)], axis=0, keepdims=True)
            dxs[rows, :] = dxs[rows, :] + live * taps[j : j + 1, :]
    grads[...] = jnp.zeros_like(grads)
    for j in range(5):
        grads[j : j + 1, :] = sums[j]


def conv_back_call(xz, mask, taps, du):
    CH, width = du.shape
    return pl.pallas_call(
        conv_back_body,
        out_shape=(out((HALO + CH, width)), out((8, width))),
        in_specs=[vmem()] * 4,
        out_specs=(vmem(),) * 2,
        compiler_params=alone(),
        name="conv_back",
    )(xz, mask, taps, du)


def wide(block, width):
    return jnp.concatenate([block] * (width // 128), axis=1) if width > 128 else block


def fold(block):
    total = block[:, 0:128]
    for lo in range(128, block.shape[1], 128):
        total = total + block[:, lo : lo + 128]
    return total


def scan_one_body(delta, u, a2, brep, first, end):
    CH, width = delta.shape
    decay = a2[...]

    def group(g, h):
        lo = pl.multiple_of(g * 8, 8)
        d8 = delta[pl.ds(lo, 8), :]
        du8 = d8 * u[pl.ds(lo, 8), :]
        for i in range(8):
            d = d8[i : i + 1, :] + first[lo + i]
            b = wide(brep[pl.ds(pl.multiple_of(g * 128 + i * 16, 16), 16), :], width)
            h = jnp.exp2(d * decay) * h + du8[i : i + 1, :] * b
        return h

    end[...] = lax.fori_loop(0, CH // 8, group, jnp.zeros(decay.shape, F32))


def scan_one(delta, u, a2, brep, first):
    return pl.pallas_call(
        scan_one_body,
        out_shape=out(a2.shape),
        in_specs=[vmem()] * 4 + [smem()],
        out_specs=vmem(),
        compiler_params=alone(),
        name="scan_one",
    )(delta, u, a2, brep, first)


def scan_two_body(delta, u, a2, brep, crep, first, h_in, y, marks):
    CH, width = delta.shape
    decay = a2[...]
    row = lax.broadcasted_iota(jnp.int32, (8, width), 0)

    def group(g, h):
        lo = pl.multiple_of(g * 8, 8)

        @pl.when(lax.rem(g, SUB // 8) == 0)
        def _():
            marks[pl.ds(pl.multiple_of(lax.div(g, SUB // 8) * 16, 16), 16), :] = h

        d8 = delta[pl.ds(lo, 8), :]
        du8 = d8 * u[pl.ds(lo, 8), :]
        y8 = jnp.zeros((8, width), F32)
        for i in range(8):
            at = pl.ds(pl.multiple_of(g * 128 + i * 16, 16), 16)
            d = d8[i : i + 1, :] + first[lo + i]
            h = jnp.exp2(d * decay) * h + du8[i : i + 1, :] * wide(brep[at, :], width)
            total = jnp.sum(h * wide(crep[at, :], width), axis=0, keepdims=True)
            y8 = jnp.where(row == i, total, y8)
        y[pl.ds(lo, 8), :] = y8
        return h

    lax.fori_loop(0, CH // 8, group, h_in[...])


def scan_two(delta, u, a2, brep, crep, first, h_in):
    CH, width = delta.shape
    return pl.pallas_call(
        scan_two_body,
        out_shape=(out((CH, width)), out((CH // SUB * 16, width))),
        in_specs=[vmem()] * 5 + [smem(), vmem()],
        out_specs=(vmem(),) * 2,
        compiler_params=alone(),
        name="scan_two",
    )(delta, u, a2, brep, crep, first, h_in)


def scan_three_body(delta, dy, a2, crep, first, start):
    CH, width = delta.shape
    decay = a2[...]

    def group(step, carry):
        g = CH // 8 - 1 - step
        lo = pl.multiple_of(g * 8, 8)
        d8 = delta[pl.ds(lo, 8), :]
        dy8 = dy[pl.ds(lo, 8), :]
        for i in range(7, -1, -1):
            at = pl.ds(pl.multiple_of(g * 128 + i * 16, 16), 16)
            d = d8[i : i + 1, :] + first[lo + i]
            lam = dy8[i : i + 1, :] * wide(crep[at, :], width) + carry
            carry = jnp.exp2(d * decay) * lam
        return carry

    start[...] = lax.fori_loop(0, CH // 8, group, jnp.zeros(decay.shape, F32))


def scan_three(delta, dy, a2, crep, first):
    return pl.pallas_call(
        scan_three_body,
        out_shape=out(a2.shape),
        in_specs=[vmem()] * 4 + [smem()],
        out_specs=vmem(),
        compiler_params=alone(),
        name="scan_three",
    )(delta, dy, a2, crep, first)


def scan_four_body(
    delta, u, dy, skip, a2, brep, crep, first, marks, g_in,
    ddelta, du_out, db, dc, ga, keep_a, keep_w,
):
    CH, width = delta.shape
    decay = a2[...]
    rate = decay * (1.0 / LOG2E)
    row = lax.broadcasted_iota(jnp.int32, (8, width), 0)
    per = SUB // 8

    def block(step, carried):
        blk = CH // SUB - 1 - step

        def forward(k, h):
            g = blk * per + k
            lo = pl.multiple_of(g * 8, 8)
            d8 = delta[pl.ds(lo, 8), :]
            du8 = d8 * u[pl.ds(lo, 8), :]
            for i in range(8):
                at = pl.ds(pl.multiple_of(g * 128 + i * 16, 16), 16)
                put = pl.ds(pl.multiple_of(k * 128 + i * 16, 16), 16)
                d = d8[i : i + 1, :] + first[lo + i]
                a = jnp.exp2(d * decay)
                keep_a[put, :] = a
                w = a * h
                keep_w[put, :] = w
                h = w + du8[i : i + 1, :] * wide(brep[at, :], width)
            return h

        lax.fori_loop(0, per, forward, marks[pl.ds(pl.multiple_of(blk * 16, 16), 16), :])

        def backward(back, state):
            carry, total_a = state
            k = per - 1 - back
            g = blk * per + k
            lo = pl.multiple_of(g * 8, 8)
            d8 = delta[pl.ds(lo, 8), :]
            u8 = u[pl.ds(lo, 8), :]
            du8 = d8 * u8
            dy8 = dy[pl.ds(lo, 8), :]
            s1 = jnp.zeros((8, width), F32)
            s2 = jnp.zeros((8, width), F32)
            for i in range(7, -1, -1):
                at = pl.ds(pl.multiple_of(g * 128 + i * 16, 16), 16)
                put = pl.ds(pl.multiple_of(k * 128 + i * 16, 16), 16)
                b = wide(brep[at, :], width)
                du = du8[i : i + 1, :]
                dyi = dy8[i : i + 1, :]
                w = keep_w[put, :]
                lam = dyi * wide(crep[at, :], width) + carry
                lw = lam * w
                s1 = jnp.where(row == i, jnp.sum(lam * b, axis=0, keepdims=True), s1)
                s2 = jnp.where(row == i, jnp.sum(lw * rate, axis=0, keepdims=True), s2)
                total_a = total_a + lw * d8[i : i + 1, :]
                dc[at, :] = fold((w + du * b) * dyi)
                db[at, :] = fold(lam * du)
                carry = keep_a[put, :] * lam
            ddelta[pl.ds(lo, 8), :] = s2 + u8 * s1
            du_out[pl.ds(lo, 8), :] = d8 * s1 + skip[0:1, :] * dy8
            return carry, total_a

        return lax.fori_loop(0, per, backward, carried)

    carry, total_a = lax.fori_loop(
        0, CH // SUB, block, (g_in[...], jnp.zeros(decay.shape, F32))
    )
    ga[...] = total_a * rate


def scan_four(delta, u, dy, skip, a2, brep, crep, first, marks, g_in):
    CH, width = delta.shape
    return pl.pallas_call(
        scan_four_body,
        out_shape=(
            out((CH, width)),
            out((CH, width)),
            out((CH * 16, 128)),
            out((CH * 16, 128)),
            out(a2.shape),
        ),
        in_specs=[vmem()] * 7 + [smem(), vmem(), vmem()],
        out_specs=(vmem(),) * 5,
        scratch_shapes=[pltpu.VMEM((SUB * 16, width), F32), pltpu.VMEM((SUB * 16, width), F32)],
        compiler_params=alone(),
        name="scan_four",
    )(delta, u, dy, skip, a2, brep, crep, first, marks, g_in)


def nt(a, b):
    return lax.dot_general(a, b, (((1,), (1,)), ((), ())), preferred_element_type=F32)


def tn(a, b):
    return lax.dot_general(a, b, (((0,), (0,)), ((), ())), preferred_element_type=F32)


def nn(a, b):
    return jnp.dot(a, b, preferred_element_type=F32)


def attend_body(q, k, v, bias, o, lse):
    s = nt(q[...], k[...]) * (HD**-0.5) + bias[...].astype(F32)
    top = jnp.max(s, axis=-1, keepdims=True)
    e = jnp.exp(s - top)
    total = jnp.sum(e, axis=-1, keepdims=True)
    o[...] = nn((e / total).astype(BF), v[...]).astype(BF)
    lse[...] = jnp.broadcast_to(top + jnp.log(total), lse.shape)


def attend(q, k, v, bias):
    CH, width = q.shape
    NK = k.shape[0]
    tq = min(CH, 256)
    return pl.pallas_call(
        attend_body,
        grid=(width // HD, CH // tq),
        out_shape=(out((CH, width), BF), out((CH, width))),
        in_specs=[
            pl.BlockSpec((tq, HD), lambda h, i: (i, h)),
            pl.BlockSpec((NK, HD), lambda h, i: (0, h)),
            pl.BlockSpec((NK, HD), lambda h, i: (0, h)),
            pl.BlockSpec((tq, NK), lambda h, i: (i, 0)),
        ],
        out_specs=(
            pl.BlockSpec((tq, HD), lambda h, i: (i, h)),
            pl.BlockSpec((tq, HD), lambda h, i: (i, h)),
        ),
        compiler_params=alone(),
        name="attend",
    )(q, k, v, bias)


def attend_back_body(q, k, v, bias, lse, do, dq, dk, dv):
    scale = HD**-0.5
    first = pl.program_id(1) == 0
    s = nt(q[...], k[...]) * scale + bias[...].astype(F32)
    prob = jnp.exp(s - lse[:, 0:1])
    dp = nt(do[...], v[...])
    rowdot = jnp.sum(prob * dp, axis=-1, keepdims=True)
    ds = (prob * (dp - rowdot)).astype(BF)
    dq[...] = nn(ds, k[...]) * scale
    add_k = tn(ds, q[...]) * scale
    add_v = tn(prob.astype(BF), do[...])

    @pl.when(first)
    def _():
        dk[...] = add_k
        dv[...] = add_v

    @pl.when(jnp.logical_not(first))
    def _():
        dk[...] += add_k
        dv[...] += add_v


def attend_back(q, k, v, bias, lse, do):
    CH, width = q.shape
    NK = k.shape[0]
    tq = min(CH, 256)
    rows = pl.BlockSpec((tq, HD), lambda h, i: (i, h))
    keys = pl.BlockSpec((NK, HD), lambda h, i: (0, h))
    return pl.pallas_call(
        attend_back_body,
        grid=(width // HD, CH // tq),
        out_shape=(out((CH, width)), out((NK, width)), out((NK, width))),
        in_specs=[rows, keys, keys, pl.BlockSpec((tq, NK), lambda h, i: (i, 0)), rows, rows],
        out_specs=(rows, keys, keys),
        compiler_params=alone(),
        name="attend_back",
    )(q, k, v, bias, lse, do)


def columns_out(weight, gain, groups, T, cols):
    rows = weight.shape[0]
    scaled = (weight.astype(F32) * gain.astype(F32)[:, None]).astype(BF)
    return scaled.reshape(rows, groups, T, W, cols).transpose(3, 0, 1, 2, 4).reshape(W, rows, -1)


def columns_back(blocks, groups, T, cols):
    rows = blocks.shape[1]
    wide_form = blocks.reshape(W, rows, groups, T, cols).transpose(1, 2, 3, 0, 4)
    return wide_form.reshape(rows, -1).astype(F32)


def gather_tc(x):
    return lax.all_gather(x.reshape(-1, x.shape[-1]), ("t", "c"), axis=0, tiled=True)


def scatter_tc(x):
    return lax.psum_scatter(x, ("t", "c"), scatter_dimension=0, tiled=True)


def swiglu(a):
    width = a.shape[1] // 2
    return jax.nn.silu(a[:, :width]) * a[:, width:]


def swiglu_back(a, dh):
    width = a.shape[1] // 2
    gate, up = a[:, :width], a[:, width:]
    s = jax.nn.sigmoid(gate)
    return jnp.concatenate([dh * up * (s * (1.0 + gate * (1.0 - s))), dh * gate * s], axis=1).astype(BF)


def local(
    inputs, segment_ids, cotangent, norm_mixer, in_proj, conv_weight, conv_bias, state_proj,
    step_proj, step_bias, decay_log, skip_gain, mixer_out, norm_ffn_one, gate_up_one, down_one,
    norm_attn, qkv_proj, attn_out, norm_ffn_two, gate_up_two, down_two,
):
    T = lax.axis_size("t")
    t, p, c = here()
    B, D = inputs.shape[1:]
    CH = W * B
    total = CH * T
    seq_len = min(SEQ_MAX, total)
    CB = conv_bias.shape[0]
    DI = CB * W * T * 2
    FB = down_one.shape[0]
    R = step_proj.shape[0]
    N = decay_log.shape[1]
    NR = state_proj.shape[1]
    width = CB * 2 * T
    heads = H // W * HD
    most = min(WIN, total // 2)
    hops = -(-(most - 1) // CH)

    par = jnp.concatenate(
        [
            state_proj, step_proj.T, decay_log, conv_weight.T,
            conv_bias[:, None], step_bias[:, None], skip_gain[:, None],
        ],
        axis=1,
    )
    used = par.shape[1]
    par = jnp.pad(par, ((0, 0), (0, 256 - used)))
    win_out = columns_out(in_proj, norm_mixer, 2, T, 2 * CB)
    seg8 = jnp.broadcast_to(segment_ids, (8, B))
    x0 = inputs[0].astype(F32)
    nh1_ext, seg_all, par_all, win_mine = start_call(T, inputs[0], seg8, par, win_out)
    w_in = gather_tc(win_mine)

    gu1_out = columns_out(gate_up_one, norm_ffn_one, 2, T, 2 * FB)
    qkv_out = columns_out(qkv_proj, norm_attn, 3, 1, heads)
    gu2_out = columns_out(gate_up_two, norm_ffn_two, 2, T, 2 * FB)
    gu1_mine, qkv_mine, gu2_mine = spread_call(1, False, (gu1_out, qkv_out, gu2_out))
    devices = 2 * W * T
    pairs = []
    for d in range(devices):
        rest = d % (2 * T)
        pairs.append((d, (rest // 2) * 2 * W + (d // (2 * T)) * 2 + rest % 2))
    ao_mine = lax.ppermute(attn_out, ("t", "p", "c"), pairs)
    w_mix = gather_tc(mixer_out)
    w_gu1 = gather_tc(gu1_mine)
    w_d1 = gather_tc(down_one)
    w_qkv = gather_tc(qkv_mine)
    w_ao = gather_tc(ao_mine)
    w_gu2 = gather_tc(gu2_mine)
    w_d2 = gather_tc(down_two)
    gl4 = plane_gather(2, cotangent[0])

    seg = seg_all[:, 0, :].reshape(total)
    pos = t * CH + jnp.arange(CH, dtype=jnp.int32)
    padded = jnp.pad(seg, (max(hops * CH, HALO), 0), constant_values=-1)
    lead = max(hops * CH, HALO)
    near = lax.dynamic_slice(padded, (t * CH + lead - HALO,), (CH + HALO,))
    own_seg = near[HALO:]
    conv_mask = jnp.stack(
        [
            (near[HALO - 3 + j : HALO - 3 + j + CH] == own_seg) & ((pos - 3 + j) // seq_len == pos // seq_len)
            & (pos - 3 + j >= 0)
            for j in range(4)
        ]
        + [jnp.zeros((CH,), jnp.bool_)] * 4,
        axis=1,
    ).astype(F32)
    starts = (pos % seq_len == 0) | (near[HALO - 1 : HALO - 1 + CH] != own_seg)
    first = jnp.where(starts, BIG, 0.0).astype(F32)
    alive = jnp.where(jnp.any(starts), 0.0, 1.0).astype(F32)
    NK = (hops + 1) * CH
    key_seg = lax.dynamic_slice(padded, (t * CH + lead - hops * CH,), (NK,))
    key_pos = t * CH - hops * CH + jnp.arange(NK, dtype=jnp.int32)
    away = pos[:, None] - key_pos[None, :]
    allowed = (
        (key_pos[None, :] >= 0) & (away >= 0) & (away < WIN) & (key_seg[None, :] == own_seg[:, None])
        & (key_pos[None, :] // seq_len == (pos // seq_len)[:, None])
    )
    bias = jnp.where(allowed, 0.0, NEG).astype(BF)
    half = HD // 2
    inverse = jnp.exp(jnp.arange(half, dtype=F32) * (-math.log(10000.0) * 2.0 / HD))
    angles = (pos % seq_len).astype(F32)[:, None] * inverse[None, :]
    cos_half, sin_half = jnp.cos(angles), jnp.sin(angles)
    cosine = jnp.concatenate([cos_half, cos_half], axis=1)
    sine = jnp.concatenate([-sin_half, sin_half], axis=1)

    par_all = par_all.reshape(width, 256)
    w_state = par_all[:, :NR]
    w_step = par_all[:, NR : NR + R].T
    side = par_all[:, NR + R : used].astype(F32).T
    a2 = -jnp.exp(side[:N]) * LOG2E
    taps = jnp.pad(side[N : N + 5], ((0, 3), (0, 0)))
    step_row = side[N + 5 : N + 6]
    skip_row = side[N + 6 : N + 7]

    xz = nn(nh1_ext, w_in)
    nh1 = nh1_ext[HALO:]
    u, u_low, part = conv_call(xz, conv_mask, taps, w_state)
    pr = plane_sum(3, part)
    dt_low = pr[:, :R].astype(BF)
    pre = nn(dt_low, w_step) + step_row
    delta = jax.nn.softplus(pre)

    def replicated(block):
        return jnp.broadcast_to(block[:, :, None], (CH, N, 128)).reshape(CH * N, 128)

    brep = replicated(pr[:, R : R + N])
    crep = replicated(pr[:, R + N :])
    sum_delta = jnp.sum(delta, axis=0, keepdims=True)

    def packed(state):
        return jnp.concatenate(
            [state, sum_delta, jnp.full((1, width), alive, F32), jnp.zeros((6, width), F32)], axis=0
        )

    end = scan_one(delta, u, a2, brep, first)
    h_in = chain(4, T, False, packed(end), a2)
    y_scan, marks = scan_two(delta, u, a2, brep, crep, first, h_in)
    y = y_scan + skip_row * u
    zg = xz[HALO:, width:]
    gate_s = jax.nn.sigmoid(zg)
    gated = (y * zg * gate_s).astype(BF)
    x1, nh2 = turn(5, nn(gated, w_mix).astype(BF), x0)

    a_one = nn(nh2, w_gu1)
    h_one = swiglu(a_one).astype(BF)
    x2, nh3 = turn(6, nn(h_one, w_d1).astype(BF), x1)

    qkv = nn(nh3, w_qkv)
    q, k_all, v_all = keys_call(7, T, hops, qkv, cosine, sine)
    o, lse = attend(q, k_all, v_all, bias)
    x3, nh4 = turn(8, nn(o, w_ao).astype(BF), x2)

    a_two = nn(nh4, w_gu2)
    h_two = swiglu(a_two).astype(BF)
    (final,) = turn(9, nn(h_two, w_d2).astype(BF), x3, gather=False, dtype=BF)

    g4 = cotangent[0].astype(F32)
    da_two = swiglu_back(a_two, nt(gl4, w_d2))
    g3, gl3 = turn(10, nt(da_two, w_gu2).astype(BF), x3, g4)
    grad_d2 = scatter_tc(tn(h_two, gl4).astype(BF))
    raw_gu2 = scatter_tc(tn(nh4, da_two).astype(BF))

    do = nt(gl3, w_ao).astype(BF)
    dq, dk, dv = attend_back(q, k_all, v_all, bias, lse, do)
    dqkv = keys_back_call(11, T, hops, dq, dk, dv, cosine, sine)
    g2, gl2 = turn(12, nt(dqkv, w_qkv).astype(BF), x2, g3)
    raw_ao = scatter_tc(tn(o, gl3).astype(BF))
    raw_qkv = scatter_tc(tn(nh3, dqkv).astype(BF))

    da_one = swiglu_back(a_one, nt(gl2, w_d1))
    g1, gl1 = turn(13, nt(da_one, w_gu1).astype(BF), x1, g2)
    grad_d1 = scatter_tc(tn(h_one, gl2).astype(BF))
    raw_gu1 = scatter_tc(tn(nh2, da_one).astype(BF))

    dgate = nt(gl1, w_mix)
    dy = dgate * zg * gate_s
    dz_low = (dgate * y * gate_s * (1.0 + zg * (1.0 - gate_s))).astype(BF)
    grad_mix = scatter_tc(tn(gated, gl1).astype(BF))
    begin = scan_three(delta, dy, a2, crep, first)
    g_in = chain(14, T, True, packed(begin), a2)
    ddelta, du_scan, db, dc_mat, ga = scan_four(
        delta, u, dy, skip_row, a2, brep, crep, first, marks, g_in
    )
    dpre = ddelta * jax.nn.sigmoid(pre)
    dpre_low = dpre.astype(BF)
    part_back = jnp.concatenate(
        [
            nt(dpre_low, w_step),
            jnp.sum(db, axis=1).reshape(CH, N),
            jnp.sum(dc_mat, axis=1).reshape(CH, N),
        ],
        axis=1,
    )
    dpr_low = plane_sum(15, part_back).astype(BF)
    du = du_scan + nt(dpr_low, w_state)
    dxs_ext, conv_grads = conv_back_call(xz, conv_mask, taps, du)
    rim = rim_back(16, T, dxs_ext[8:16])
    dxs_low = jnp.concatenate(
        [dxs_ext[HALO : HALO + CH - 8], dxs_ext[HALO + CH - 8 :] + rim], axis=0
    ).astype(BF)
    dxz = jnp.concatenate([dxs_low, dz_low], axis=1)
    raw_in = scatter_tc(tn(nh1, dxz).astype(BF))
    (grad_x,) = turn(17, nt(dxz, w_in).astype(BF), x0, g1, gather=False)

    small = jnp.concatenate(
        [
            tn(u_low, dpr_low),
            tn(dpre_low, dt_low),
            ga.T,
            conv_grads[:5].T,
            jnp.sum(dpre, axis=0)[:, None],
            jnp.sum(dy * u, axis=0)[:, None],
        ],
        axis=1,
    )
    small = jnp.pad(small, ((0, 0), (0, 256 - used))).astype(BF).reshape(2 * T, CB, 256)
    small = small_sum(18, T, small)

    def blocks(x):
        return x.reshape(W, x.shape[0] // W, x.shape[1])

    gu2_b, qkv_b, gu1_b = spread_call(19, True, (blocks(raw_gu2), blocks(raw_qkv), blocks(raw_gu1)))
    (in_b,) = spread_call(20, True, (blocks(raw_in),))
    grad_ao = lax.ppermute(raw_ao, ("t", "p", "c"), [(b, a) for a, b in pairs]).astype(F32)

    def finished(blocks_in, weight, gain, groups, groups_t, cols):
        raw = columns_back(blocks_in, groups, groups_t, cols)
        return (
            jnp.sum(weight.astype(F32) * raw, axis=1),
            raw * gain.astype(F32)[:, None],
        )

    grad_n1, grad_in = finished(in_b, in_proj, norm_mixer, 2, T, 2 * CB)
    grad_n2, grad_gu1 = finished(gu1_b, gate_up_one, norm_ffn_one, 2, T, 2 * FB)
    grad_n3, grad_qkv = finished(qkv_b, qkv_proj, norm_attn, 3, 1, heads)
    grad_n4, grad_gu2 = finished(gu2_b, gate_up_two, norm_ffn_two, 2, T, 2 * FB)
    at = NR + R + N
    return (
        final[None],
        grad_x[None],
        grad_n1,
        grad_in,
        small[:, at : at + 4].T,
        small[:, at + 4],
        small[:, :NR],
        small[:, NR : NR + R].T,
        small[:, at + 5],
        small[:, NR + R : at],
        small[:, at + 6],
        grad_mix.astype(F32),
        grad_n2,
        grad_gu1,
        grad_d1.astype(F32),
        grad_n3,
        grad_qkv,
        grad_ao,
        grad_n4,
        grad_gu2,
        grad_d2.astype(F32),
    )


def solution(mesh):
    chunks = mesh.shape["seq"] // W
    view = Mesh(mesh.devices.reshape(chunks, W, mesh.shape["fsdp"]), ("t", "p", "c"))
    every = ("t", "p", "c")
    tokens = P("c", ("t", "p"), None)
    vector, rows, cols = P(every), P(every, None), P(None, every)
    placed = (
        tokens, P("c", ("t", "p")), tokens,
        vector, rows, cols, vector, rows, cols, vector, rows, vector, rows,
        vector, rows, rows, vector, rows, rows, vector, rows, rows,
    )
    return jax.shard_map(
        local,
        mesh=view,
        in_specs=placed,
        out_specs=(tokens, tokens) + placed[3:],
        check_vma=False,
    )
```

```python
import functools
import math

import jax
import jax.numpy as jnp
from jax import lax
from jax.experimental import pallas as pl
from jax.experimental.pallas import tpu as pltpu
from jax.sharding import Mesh
from jax.sharding import PartitionSpec as P

W = 4
H = 12
HD = 128
WIN = 2048
SEQ_MAX = 8192
EPS = 1e-05
NEG = -1e30
BIG = 1e30
LOG2E = 1.4426950408889634
BF = jnp.bfloat16
F32 = jnp.float32
MESH = pl.DeviceIdType.MESH
HALO = 16
SUB = 64
MIB = 1 << 20


def vmem():
    return pl.BlockSpec(memory_space=pltpu.VMEM)


def hbm():
    return pl.BlockSpec(memory_space=pl.ANY)


def smem():
    return pl.BlockSpec(memory_space=pltpu.SMEM)


def here():
    return lax.axis_index("t"), lax.axis_index("p"), lax.axis_index("c")


def greet(device):
    pl.semaphore_signal(
        pltpu.get_barrier_semaphore(), inc=1, device_id=device, device_id_type=MESH
    )


def arrive(count):
    pl.semaphore_wait(pltpu.get_barrier_semaphore(), count)


def arrive_some(count):
    @pl.when(count > 0)
    def _():
        arrive(count)


def remote(src, dst, send, recv, device):
    return pltpu.make_async_remote_copy(
        src_ref=src,
        dst_ref=dst,
        send_sem=send,
        recv_sem=recv,
        device_id=device,
        device_id_type=MESH,
    )


def flip(p, d):
    return lax.bitwise_xor(p, d)


def dma(*shape):
    return pltpu.SemaphoreType.DMA(shape)


def talk(cid, limit=40):
    return pltpu.CompilerParams(
        collective_id=cid, has_side_effects=True, vmem_limit_bytes=limit * MIB
    )


def alone(limit=56):
    return pltpu.CompilerParams(vmem_limit_bytes=limit * MIB)


def out(shape, dtype=F32):
    return jax.ShapeDtypeStruct(shape, dtype)


def unit(x):
    return x * lax.rsqrt(jnp.mean(x * x, axis=-1, keepdims=True) + EPS)


def start_body(
    T, x, seg, par, ct, nh, seg_out, par_out, ct_out, nbuf, zbuf,
    s_n, r_n, s_h, r_h, s_s, r_s, s_p, r_p, s_c, r_c, s_l,
):
    t, p, c = here()
    B = x.shape[0]
    count = 0
    for dt in range(T):
        tt = lax.rem(t + dt, T)
        for dp in range(W):
            pp = flip(p, dp)
            if dt or dp:
                greet((tt, pp, c))
                count += 1
            if dp == 0:
                greet((tt, pp, 1 - c))
                count += 1
    nbuf[...] = unit(x[...].astype(F32)).astype(BF)
    zbuf[...] = jnp.zeros_like(zbuf)
    arrive(count)
    rows = pl.ds(pl.multiple_of(HALO + p * B, HALO), B)
    plain = pl.ds(pl.multiple_of(p * B, B), B)
    copies = []
    for dt in range(T):
        for dc in range(2):
            if dt or dc:
                copies.append(
                    remote(
                        par, par_out.at[t * 2 + c], s_p.at[dt, dc], r_p.at[dt, dc],
                        (lax.rem(t + dt, T), p, flip(c, dc)),
                    )
                )
    for d in range(1, W):
        copies.append(remote(nbuf, nh.at[rows], s_n.at[d], r_n.at[d], (t, flip(p, d), c)))
    for dt in range(T):
        for dp in range(W):
            if dt or dp:
                copies.append(
                    remote(
                        seg, seg_out.at[t * W + p], s_s.at[dt, dp], r_s.at[dt, dp],
                        (lax.rem(t + dt, T), flip(p, dp), c),
                    )
                )
    for d in range(1, W):
        copies.append(remote(ct, ct_out.at[plain], s_c.at[d], r_c.at[d], (t, flip(p, d), c)))
    for copy in copies:
        copy.start()
    last = (p == W - 1) & (t < T - 1)
    tail = nbuf.at[pl.ds(B - HALO, HALO)]
    head = nh.at[pl.ds(0, HALO)]

    def rim(q):
        return remote(tail, head, s_h.at[q], r_h, (lax.rem(t + 1, T), q, c))

    @pl.when(last)
    def _():
        for q in range(W):
            rim(q).start()

    local = [
        pltpu.make_async_copy(nbuf, nh.at[rows], s_l.at[0]),
        pltpu.make_async_copy(par, par_out.at[t * 2 + c], s_l.at[1]),
        pltpu.make_async_copy(seg, seg_out.at[t * W + p], s_l.at[2]),
        pltpu.make_async_copy(ct, ct_out.at[plain], s_l.at[4]),
    ]
    for copy in local:
        copy.start()

    @pl.when(t == 0)
    def _():
        clear = pltpu.make_async_copy(zbuf, head, s_l.at[3])
        clear.start()
        clear.wait()

    for copy in local:
        copy.wait()
    for copy in copies:
        copy.wait()

    @pl.when(last)
    def _():
        for q in range(W):
            rim(q).wait_send()

    @pl.when(t > 0)
    def _():
        rim(0).wait_recv()


def start_call(T, x, seg, par, ct):
    B, D = x.shape
    return pl.pallas_call(
        functools.partial(start_body, T),
        out_shape=(
            out((HALO + W * B, D), BF),
            out((W * T,) + seg.shape, jnp.int32),
            out((2 * T,) + par.shape, BF),
            out((W * B, D), BF),
        ),
        in_specs=[vmem(), hbm(), hbm(), hbm()],
        out_specs=(hbm(), hbm(), hbm(), hbm()),
        scratch_shapes=[
            pltpu.VMEM((B, D), BF),
            pltpu.VMEM((HALO, D), BF),
            dma(W), dma(W), dma(W), pltpu.SemaphoreType.DMA,
            dma(T, W), dma(T, W), dma(T, 2), dma(T, 2), dma(W), dma(W), dma(5),
        ],
        compiler_params=talk(0),
        name="start",
    )(x, seg, par, ct)


def spread_body(n, back, *refs):
    srcs, dsts = refs[:n], refs[n : 2 * n]
    s_w, r_w = refs[2 * n :]
    t, p, c = here()
    half = lax.div(p, 2)
    pair = lax.rem(p, 2) * 2 + c
    both = half == c

    def there(q):
        if back:
            return (t, c * 2 + q // 2, jnp.int32(q % 2))
        return (t, jnp.int32(q), half)

    def comes(j):
        if back:
            return (t, jnp.int32(j), half)
        return (t, c * 2 + j // 2, jnp.int32(j % 2))

    slot = p if back else pair
    for q in range(W):
        to, source = there(q), comes(q)
        own = both & ((pair == q) if back else (p == q))
        from_me = both & ((p == q) if back else (pair == q))

        @pl.when(jnp.logical_not(from_me))
        def _():
            greet(source)

    arrive(W - both.astype(jnp.int32))
    for q in range(W):
        own = both & ((pair == q) if back else (p == q))
        for a in range(n):

            @pl.when(jnp.logical_not(own))
            def _():
                remote(
                    srcs[a].at[q], dsts[a].at[slot], s_w.at[a, q], r_w.at[a, slot], there(q)
                ).start()

            @pl.when(own)
            def _():
                pltpu.make_async_copy(srcs[a].at[q], dsts[a].at[slot], s_w.at[a, q]).start()

    for q in range(W):
        own = both & ((pair == q) if back else (p == q))
        from_me = both & ((p == q) if back else (pair == q))
        for a in range(n):

            @pl.when(jnp.logical_not(own))
            def _():
                remote(
                    srcs[a].at[q], dsts[a].at[slot], s_w.at[a, q], r_w.at[a, slot], there(q)
                ).wait_send()

            @pl.when(own)
            def _():
                pltpu.make_async_copy(srcs[a].at[q], dsts[a].at[slot], s_w.at[a, q]).wait()

            @pl.when(jnp.logical_not(from_me))
            def _():
                remote(
                    srcs[a].at[q], dsts[a].at[q], s_w.at[a, q], r_w.at[a, q], there(q)
                ).wait_recv()


def spread_call(cid, back, arrays):
    n = len(arrays)
    return pl.pallas_call(
        functools.partial(spread_body, n, back),
        out_shape=tuple(out(a.shape, a.dtype) for a in arrays),
        in_specs=[hbm()] * n,
        out_specs=(hbm(),) * n,
        scratch_shapes=[dma(n, W), dma(n, W)],
        compiler_params=talk(cid),
        name="spread%d" % cid,
    )(*arrays)


def plane_sum_body(x, o, sb, recv, ss, rs):
    t, p, c = here()
    for d in range(1, W):
        greet((t, flip(p, d), c))
    sb[...] = x[...].astype(BF)
    arrive(W - 1)
    copies = [
        remote(sb, recv.at[d - 1], ss.at[d - 1], rs.at[d - 1], (t, flip(p, d), c))
        for d in range(1, W)
    ]
    for copy in copies:
        copy.start()
    for copy in copies:
        copy.wait()
    total = x[...]
    for d in range(W - 1):
        total = total + recv[d].astype(F32)
    o[...] = total


def plane_sum(cid, x):
    return pl.pallas_call(
        plane_sum_body,
        out_shape=out(x.shape),
        in_specs=[vmem()],
        out_specs=vmem(),
        scratch_shapes=[
            pltpu.VMEM(x.shape, BF),
            pltpu.VMEM((W - 1,) + x.shape, BF),
            dma(W - 1),
            dma(W - 1),
        ],
        compiler_params=talk(cid),
        name="plane_sum%d" % cid,
    )(x)


def turn_body(back, gather, parts, *refs):
    refs = list(refs)
    part = refs.pop(0)
    x = refs.pop(0)
    g = refs.pop(0) if back else None
    o = refs.pop(0)
    gath = refs.pop(0) if gather else None
    own, recv, sbuf, ss, rs, ls, ss2, rs2, ls2 = refs
    t, p, c = here()
    B = x.shape[0]
    rows = B // parts
    for d in range(1, W):
        greet((t, flip(p, d), c))
    local = pltpu.make_async_copy(part.at[pl.ds(pl.multiple_of(p * B, B), B)], own, ls)
    local.start()
    arrive(W - 1)
    first = {}
    for k in range(parts):
        for d in range(1, W):
            q = flip(p, d)
            first[k, d] = remote(
                part.at[pl.ds(pl.multiple_of(q * B + k * rows, rows), rows)],
                recv.at[d - 1, pl.ds(k * rows, rows)],
                ss.at[d - 1, k],
                rs.at[d - 1, k],
                (t, q, c),
            )
            first[k, d].start()
    local.wait()
    later = []
    for k in range(parts):
        for d in range(1, W):
            first[k, d].wait_recv()
        cut = pl.ds(k * rows, rows)
        total = own[cut, :].astype(F32)
        for d in range(W - 1):
            total = total + recv[d, cut, :].astype(F32)
        value = x[cut, :]
        if back:
            r = lax.rsqrt(jnp.mean(value * value, axis=-1, keepdims=True) + EPS)
            hat = value * r
            new = g[cut, :] + r * (total - hat * jnp.mean(total * hat, axis=-1, keepdims=True))
        else:
            new = value + total
        o[cut, :] = new.astype(o.dtype)
        if gather:
            sbuf[cut, :] = (new if back else unit(new)).astype(BF)
            place = gath.at[pl.ds(pl.multiple_of(p * B + k * rows, rows), rows)]
            for d in range(1, W):
                later.append(
                    remote(sbuf.at[cut], place, ss2.at[d - 1, k], rs2.at[d - 1, k], (t, flip(p, d), c))
                )
            later.append(pltpu.make_async_copy(sbuf.at[cut], place, ls2.at[k]))
            for copy in later[-W:]:
                copy.start()
    for copy in first.values():
        copy.wait_send()
    for copy in later:
        copy.wait()


def turn(cid, part, x, g=None, gather=True, dtype=F32, parts=2):
    B, D = x.shape
    back = g is not None
    shapes = [out((B, D), dtype)]
    specs = [vmem()]
    if gather:
        shapes.append(out((W * B, D), BF))
        specs.append(hbm())
    args = (part, x) + ((g,) if back else ())
    return pl.pallas_call(
        functools.partial(turn_body, back, gather, parts),
        out_shape=tuple(shapes),
        in_specs=[hbm()] + [vmem()] * (len(args) - 1),
        out_specs=tuple(specs),
        scratch_shapes=[
            pltpu.VMEM((B, D), BF),
            pltpu.VMEM((W - 1, B, D), BF),
            pltpu.VMEM((B, D), BF),
            dma(W - 1, parts), dma(W - 1, parts), pltpu.SemaphoreType.DMA,
            dma(W - 1, parts), dma(W - 1, parts), dma(parts),
        ],
        compiler_params=talk(cid),
        name="turn%d" % cid,
    )(*args)


def chain_body(T, back, v, a2, h, recv, ss, rs):
    t, p, c = here()
    sign = -1 if back else 1
    for k in range(1, T):
        source = t - sign * k

        @pl.when((source >= 0) & (source < T))
        def _():
            greet((lax.rem(source + T, T), p, c))

    arrive_some(t if back else T - 1 - t)

    def send(k):
        to = lax.rem(t + sign * k + T, T)
        return remote(v, recv.at[k - 1], ss.at[k - 1], rs.at[k - 1], (to, p, c))

    for k in range(1, T):
        to = t + sign * k

        @pl.when((to >= 0) & (to < T))
        def _():
            send(k).start()

    h[...] = jnp.zeros_like(h)
    for k in range(T - 1, 0, -1):
        source = t - sign * k

        @pl.when((source >= 0) & (source < T))
        def _():
            send(k).wait_recv()
            decay = jnp.exp2(a2[...] * recv[k - 1, 16:17, :]) * recv[k - 1, 17:18, :]
            h[...] = recv[k - 1, 0:16, :] + decay * h[...]

    for k in range(1, T):
        to = t + sign * k

        @pl.when((to >= 0) & (to < T))
        def _():
            send(k).wait_send()


def chain(cid, T, back, v, a2):
    return pl.pallas_call(
        functools.partial(chain_body, T, back),
        out_shape=out(a2.shape),
        in_specs=[vmem(), vmem()],
        out_specs=vmem(),
        scratch_shapes=[pltpu.VMEM((T - 1,) + v.shape, F32), dma(T - 1), dma(T - 1)],
        compiler_params=talk(cid),
        name="chain%d" % cid,
    )(v, a2)


def rope(w, cosine, sine):
    return w * cosine + pltpu.roll(w, HD // 2, 1) * sine


def keys_body(T, hops, qkv, cosine, sine, q, k_all, v_all, ss, rs):
    t, p, c = here()
    CH = q.shape[0]
    width = q.shape[1]

    @pl.when(t > 0)
    def _():
        greet((lax.rem(t - 1 + T, T), p, c))

    mine = pl.ds(hops * CH, CH)
    for h in range(width // HD):
        cols = pl.ds(h * HD, HD)
        k_all[mine, cols] = rope(
            qkv[:, pl.ds(width + h * HD, HD)], cosine[...], sine[...]
        ).astype(BF)
    v_all[mine, :] = qkv[:, pl.ds(2 * width, width)].astype(BF)

    @pl.when(t < T - 1)
    def _():
        arrive(1)

    def send(a, d):
        ref = (k_all, v_all)[a]
        return remote(
            ref.at[pl.ds((hops - d + 1) * CH, CH)],
            ref.at[pl.ds((hops - d) * CH, CH)],
            ss.at[a, d - 1],
            rs.at[a, d - 1],
            (lax.rem(t + 1, T), p, c),
        )

    for d in range(1, hops + 1):
        goes = (t < T - 1) & (t >= d - 1)

        @pl.when(goes)
        def _():
            send(0, d).start()
            send(1, d).start()

        if d == 1:
            for h in range(width // HD):
                cols = pl.ds(h * HD, HD)
                q[:, cols] = rope(qkv[:, cols], cosine[...], sine[...]).astype(BF)

        @pl.when(t < d)
        def _():
            k_all[pl.ds((hops - d) * CH, CH), :] = jnp.zeros((CH, width), BF)
            v_all[pl.ds((hops - d) * CH, CH), :] = jnp.zeros((CH, width), BF)

        @pl.when(t >= d)
        def _():
            send(0, d).wait_recv()
            send(1, d).wait_recv()

    for d in range(1, hops + 1):
        goes = (t < T - 1) & (t >= d - 1)

        @pl.when(goes)
        def _():
            send(0, d).wait_send()
            send(1, d).wait_send()


def keys_call(cid, T, hops, qkv, cosine, sine):
    CH = qkv.shape[0]
    width = qkv.shape[1] // 3
    return pl.pallas_call(
        functools.partial(keys_body, T, hops),
        out_shape=(
            out((CH, width), BF),
            out(((hops + 1) * CH, width), BF),
            out(((hops + 1) * CH, width), BF),
        ),
        in_specs=[vmem()] * 3,
        out_specs=(vmem(),) * 3,
        scratch_shapes=[dma(2, hops), dma(2, hops)],
        compiler_params=talk(cid),
        name="keys",
    )(qkv, cosine, sine)


def keys_back_body(T, hops, dq, dk, dv, cosine, sine, dqkv, sb, recv, ss, rs):
    t, p, c = here()
    CH = dq.shape[0]
    width = dq.shape[1]

    @pl.when(t < T - 1)
    def _():
        greet((lax.rem(t + 1, T), p, c))

    def send(a, d):
        return remote(
            sb.at[a, d - 1],
            recv.at[a, d - 1],
            ss.at[a, d - 1],
            rs.at[a, d - 1],
            (lax.rem(t - 1 + T, T), p, c),
        )

    for d in range(hops, 0, -1):
        rows = pl.ds((hops - d) * CH, CH)
        k_sum = dk[rows, :]
        v_sum = dv[rows, :]
        if d == hops:
            sb[0, d - 1] = k_sum.astype(BF)
            sb[1, d - 1] = v_sum.astype(BF)

            @pl.when(t > 0)
            def _():
                arrive(1)
        else:

            @pl.when((t < T - 1) & (t >= d))
            def _():
                send(0, d + 1).wait_recv()
                send(1, d + 1).wait_recv()

            @pl.when((t == T - 1) | (t < d))
            def _():
                recv[0, d] = jnp.zeros((CH, width), BF)
                recv[1, d] = jnp.zeros((CH, width), BF)

            sb[0, d - 1] = (k_sum + recv[0, d].astype(F32)).astype(BF)
            sb[1, d - 1] = (v_sum + recv[1, d].astype(F32)).astype(BF)

        @pl.when(t >= d)
        def _():
            send(0, d).start()
            send(1, d).start()

        if d == hops:
            for h in range(width // HD):
                cols = pl.ds(h * HD, HD)
                dqkv[:, cols] = rope(dq[:, cols], cosine[...], -sine[...]).astype(BF)

    @pl.when(t < T - 1)
    def _():
        send(0, 1).wait_recv()
        send(1, 1).wait_recv()

    @pl.when(t == T - 1)
    def _():
        recv[0, 0] = jnp.zeros((CH, width), BF)
        recv[1, 0] = jnp.zeros((CH, width), BF)

    mine = pl.ds(hops * CH, CH)
    for h in range(width // HD):
        cols = pl.ds(h * HD, HD)
        k_sum = dk[mine, cols] + recv[0, 0, :, cols].astype(F32)
        v_sum = dv[mine, cols] + recv[1, 0, :, cols].astype(F32)
        dqkv[:, pl.ds(width + h * HD, HD)] = rope(k_sum, cosine[...], -sine[...]).astype(BF)
        dqkv[:, pl.ds(2 * width + h * HD, HD)] = v_sum.astype(BF)
    for d in range(hops, 0, -1):

        @pl.when(t >= d)
        def _():
            send(0, d).wait_send()
            send(1, d).wait_send()


def keys_back_call(cid, T, hops, dq, dk, dv, cosine, sine):
    CH, width = dq.shape
    return pl.pallas_call(
        functools.partial(keys_back_body, T, hops),
        out_shape=out((CH, 3 * width), BF),
        in_specs=[vmem()] * 5,
        out_specs=vmem(),
        scratch_shapes=[
            pltpu.VMEM((2, hops, CH, width), BF),
            pltpu.VMEM((2, hops, CH, width), BF),
            dma(2, hops),
            dma(2, hops),
        ],
        compiler_params=talk(cid, 48),
        name="keys_back",
    )(dq, dk, dv, cosine, sine)


def rim_body(T, x, o, recv, ss, rs):
    t, p, c = here()

    @pl.when(t < T - 1)
    def _():
        greet((lax.rem(t + 1, T), p, c))

    def send():
        return remote(x, recv, ss, rs, (lax.rem(t + T - 1, T), p, c))

    @pl.when(t > 0)
    def _():
        arrive(1)
        send().start()
        send().wait_send()

    o[...] = jnp.zeros_like(o)

    @pl.when(t < T - 1)
    def _():
        send().wait_recv()
        o[...] = recv[...]


def rim_back(cid, T, x):
    return pl.pallas_call(
        functools.partial(rim_body, T),
        out_shape=out(x.shape),
        in_specs=[vmem()],
        out_specs=vmem(),
        scratch_shapes=[pltpu.VMEM(x.shape, F32), pltpu.SemaphoreType.DMA, pltpu.SemaphoreType.DMA],
        compiler_params=talk(cid),
        name="rim_back",
    )(x)


def small_body(T, x, o, recv, ss, rs):
    t, p, c = here()
    peers = [(dt, dc) for dt in range(T) for dc in range(2) if dt or dc]

    def device(dt, dc):
        return lax.rem(t + dt, T), flip(c, dc)

    for dt, dc in peers:
        tt, cc = device(dt, dc)
        greet((tt, p, cc))
    arrive(len(peers))
    copies = []
    for i, (dt, dc) in enumerate(peers):
        tt, cc = device(dt, dc)
        copies.append(remote(x.at[tt * 2 + cc], recv.at[i], ss.at[i], rs.at[i], (tt, p, cc)))
        copies[-1].start()
    total = x[t * 2 + c].astype(F32)
    for i, copy in enumerate(copies):
        copy.wait()
        total = total + recv[i].astype(F32)
    o[...] = total


def small_sum(cid, T, x):
    n = x.shape[0] - 1
    return pl.pallas_call(
        functools.partial(small_body, T),
        out_shape=out(x.shape[1:]),
        in_specs=[vmem()],
        out_specs=vmem(),
        scratch_shapes=[pltpu.VMEM((n,) + x.shape[1:], x.dtype), dma(n), dma(n)],
        compiler_params=talk(cid),
        name="small_sum",
    )(x)


def conv_sum(xz, mask, taps, lo, size):
    width = taps.shape[1]
    total = jnp.broadcast_to(taps[4:5, :], (size, width))
    for j in range(4):
        rows = xz[pl.ds(lo + HALO - 3 + j, size), pl.ds(0, width)]
        total = total + taps[j : j + 1, :] * rows * mask[pl.ds(lo, size), j : j + 1]
    return total


def conv_body(xz, mask, taps, proj, u, u_low, part):
    CH = u.shape[0]
    step = min(CH, 128)
    for lo in range(0, CH, step):
        cut = pl.ds(lo, step)
        c = conv_sum(xz, mask, taps, lo, step)
        value = c / (1.0 + jnp.exp(-c))
        u[cut, :] = value
        low = value.astype(BF)
        u_low[cut, :] = low
        part[cut, :] = jnp.dot(low, proj[...], preferred_element_type=F32)


def conv_call(xz, mask, taps, proj):
    CH = mask.shape[0]
    width = taps.shape[1]
    return pl.pallas_call(
        conv_body,
        out_shape=(out((CH, width)), out((CH, width), BF), out((CH, proj.shape[1]))),
        in_specs=[vmem()] * 4,
        out_specs=(vmem(),) * 3,
        compiler_params=alone(),
        name="conv",
    )(xz, mask, taps, proj)


def conv_back_body(xz, mask, taps, du, dxs, grads):
    CH, width = du.shape
    step = min(CH, 128)
    dxs[...] = jnp.zeros_like(dxs)
    sums = [jnp.zeros((1, width), F32) for _ in range(5)]
    for lo in range(0, CH, step):
        c = conv_sum(xz, mask, taps, lo, step)
        s = 1.0 / (1.0 + jnp.exp(-c))
        dc = du[pl.ds(lo, step), :] * (s * (1.0 + c * (1.0 - s)))
        sums[4] = sums[4] + jnp.sum(dc, axis=0, keepdims=True)
        for j in range(4):
            rows = pl.ds(lo + HALO - 3 + j, step)
            live = dc * mask[pl.ds(lo, step), j : j + 1]
            sums[j] = sums[j] + jnp.sum(live * xz[rows, pl.ds(0, width)], axis=0, keepdims=True)
            dxs[rows, :] = dxs[rows, :] + live * taps[j : j + 1, :]
    grads[...] = jnp.zeros_like(grads)
    for j in range(5):
        grads[j : j + 1, :] = sums[j]


def conv_back_call(xz, mask, taps, du):
    CH, width = du.shape
    return pl.pallas_call(
        conv_back_body,
        out_shape=(out((HALO + CH, width)), out((8, width))),
        in_specs=[vmem()] * 4,
        out_specs=(vmem(),) * 2,
        compiler_params=alone(),
        name="conv_back",
    )(xz, mask, taps, du)


def wide(block, width):
    return jnp.concatenate([block] * (width // 128), axis=1) if width > 128 else block


def fold(block):
    total = block[:, 0:128]
    for lo in range(128, block.shape[1], 128):
        total = total + block[:, lo : lo + 128]
    return total


def scan_one_body(delta, u, a2, brep, first, end):
    CH, width = delta.shape
    decay = a2[...]

    def group(g, h):
        lo = pl.multiple_of(g * 8, 8)
        d8 = delta[pl.ds(lo, 8), :]
        du8 = d8 * u[pl.ds(lo, 8), :]
        for i in range(8):
            d = d8[i : i + 1, :] + first[lo + i]
            b = wide(brep[pl.ds(pl.multiple_of(g * 128 + i * 16, 16), 16), :], width)
            h = jnp.exp2(d * decay) * h + du8[i : i + 1, :] * b
        return h

    end[...] = lax.fori_loop(0, CH // 8, group, jnp.zeros(decay.shape, F32))


def scan_one(delta, u, a2, brep, first):
    return pl.pallas_call(
        scan_one_body,
        out_shape=out(a2.shape),
        in_specs=[vmem()] * 4 + [smem()],
        out_specs=vmem(),
        compiler_params=alone(),
        name="scan_one",
    )(delta, u, a2, brep, first)


def scan_two_body(delta, u, a2, brep, crep, first, h_in, y, marks):
    CH, width = delta.shape
    decay = a2[...]
    row = lax.broadcasted_iota(jnp.int32, (8, width), 0)

    def group(g, h):
        lo = pl.multiple_of(g * 8, 8)

        @pl.when(lax.rem(g, SUB // 8) == 0)
        def _():
            marks[pl.ds(pl.multiple_of(lax.div(g, SUB // 8) * 16, 16), 16), :] = h

        d8 = delta[pl.ds(lo, 8), :]
        du8 = d8 * u[pl.ds(lo, 8), :]
        y8 = jnp.zeros((8, width), F32)
        for i in range(8):
            at = pl.ds(pl.multiple_of(g * 128 + i * 16, 16), 16)
            d = d8[i : i + 1, :] + first[lo + i]
            h = jnp.exp2(d * decay) * h + du8[i : i + 1, :] * wide(brep[at, :], width)
            total = jnp.sum(h * wide(crep[at, :], width), axis=0, keepdims=True)
            y8 = jnp.where(row == i, total, y8)
        y[pl.ds(lo, 8), :] = y8
        return h

    lax.fori_loop(0, CH // 8, group, h_in[...])


def scan_two(delta, u, a2, brep, crep, first, h_in):
    CH, width = delta.shape
    return pl.pallas_call(
        scan_two_body,
        out_shape=(out((CH, width)), out((CH // SUB * 16, width))),
        in_specs=[vmem()] * 5 + [smem(), vmem()],
        out_specs=(vmem(),) * 2,
        compiler_params=alone(),
        name="scan_two",
    )(delta, u, a2, brep, crep, first, h_in)


def scan_three_body(delta, dy, a2, crep, first, start):
    CH, width = delta.shape
    decay = a2[...]

    def group(step, carry):
        g = CH // 8 - 1 - step
        lo = pl.multiple_of(g * 8, 8)
        d8 = delta[pl.ds(lo, 8), :]
        dy8 = dy[pl.ds(lo, 8), :]
        for i in range(7, -1, -1):
            at = pl.ds(pl.multiple_of(g * 128 + i * 16, 16), 16)
            d = d8[i : i + 1, :] + first[lo + i]
            lam = dy8[i : i + 1, :] * wide(crep[at, :], width) + carry
            carry = jnp.exp2(d * decay) * lam
        return carry

    start[...] = lax.fori_loop(0, CH // 8, group, jnp.zeros(decay.shape, F32))


def scan_three(delta, dy, a2, crep, first):
    return pl.pallas_call(
        scan_three_body,
        out_shape=out(a2.shape),
        in_specs=[vmem()] * 4 + [smem()],
        out_specs=vmem(),
        compiler_params=alone(),
        name="scan_three",
    )(delta, dy, a2, crep, first)


def scan_four_body(
    delta, u, dy, skip, a2, brep, crep, first, marks, g_in,
    ddelta, du_out, db, dc, ga, keep_a, keep_w,
):
    CH, width = delta.shape
    decay = a2[...]
    rate = decay * (1.0 / LOG2E)
    row = lax.broadcasted_iota(jnp.int32, (8, width), 0)
    per = SUB // 8

    def block(step, carried):
        blk = CH // SUB - 1 - step

        def forward(k, h):
            g = blk * per + k
            lo = pl.multiple_of(g * 8, 8)
            d8 = delta[pl.ds(lo, 8), :]
            du8 = d8 * u[pl.ds(lo, 8), :]
            for i in range(8):
                at = pl.ds(pl.multiple_of(g * 128 + i * 16, 16), 16)
                put = pl.ds(pl.multiple_of(k * 128 + i * 16, 16), 16)
                d = d8[i : i + 1, :] + first[lo + i]
                a = jnp.exp2(d * decay)
                keep_a[put, :] = a
                w = a * h
                keep_w[put, :] = w
                h = w + du8[i : i + 1, :] * wide(brep[at, :], width)
            return h

        lax.fori_loop(0, per, forward, marks[pl.ds(pl.multiple_of(blk * 16, 16), 16), :])

        def backward(back, state):
            carry, total_a = state
            k = per - 1 - back
            g = blk * per + k
            lo = pl.multiple_of(g * 8, 8)
            d8 = delta[pl.ds(lo, 8), :]
            u8 = u[pl.ds(lo, 8), :]
            du8 = d8 * u8
            dy8 = dy[pl.ds(lo, 8), :]
            s1 = jnp.zeros((8, width), F32)
            s2 = jnp.zeros((8, width), F32)
            for i in range(7, -1, -1):
                at = pl.ds(pl.multiple_of(g * 128 + i * 16, 16), 16)
                put = pl.ds(pl.multiple_of(k * 128 + i * 16, 16), 16)
                b = wide(brep[at, :], width)
                du = du8[i : i + 1, :]
                dyi = dy8[i : i + 1, :]
                w = keep_w[put, :]
                lam = dyi * wide(crep[at, :], width) + carry
                lw = lam * w
                s1 = jnp.where(row == i, jnp.sum(lam * b, axis=0, keepdims=True), s1)
                s2 = jnp.where(row == i, jnp.sum(lw * rate, axis=0, keepdims=True), s2)
                total_a = total_a + lw * d8[i : i + 1, :]
                dc[at, :] = fold((w + du * b) * dyi)
                db[at, :] = fold(lam * du)
                carry = keep_a[put, :] * lam
            ddelta[pl.ds(lo, 8), :] = s2 + u8 * s1
            du_out[pl.ds(lo, 8), :] = d8 * s1 + skip[0:1, :] * dy8
            return carry, total_a

        return lax.fori_loop(0, per, backward, carried)

    carry, total_a = lax.fori_loop(
        0, CH // SUB, block, (g_in[...], jnp.zeros(decay.shape, F32))
    )
    ga[...] = total_a * rate


def scan_four(delta, u, dy, skip, a2, brep, crep, first, marks, g_in):
    CH, width = delta.shape
    return pl.pallas_call(
        scan_four_body,
        out_shape=(
            out((CH, width)),
            out((CH, width)),
            out((CH * 16, 128)),
            out((CH * 16, 128)),
            out(a2.shape),
        ),
        in_specs=[vmem()] * 7 + [smem(), vmem(), vmem()],
        out_specs=(vmem(),) * 5,
        scratch_shapes=[pltpu.VMEM((SUB * 16, width), F32), pltpu.VMEM((SUB * 16, width), F32)],
        compiler_params=alone(),
        name="scan_four",
    )(delta, u, dy, skip, a2, brep, crep, first, marks, g_in)


def nt(a, b):
    return lax.dot_general(a, b, (((1,), (1,)), ((), ())), preferred_element_type=F32)


def tn(a, b):
    return lax.dot_general(a, b, (((0,), (0,)), ((), ())), preferred_element_type=F32)


def nn(a, b):
    return jnp.dot(a, b, preferred_element_type=F32)


def attend_body(q, k, v, bias, o, lse):
    s = nt(q[...], k[...]) * (HD**-0.5) + bias[...].astype(F32)
    top = jnp.max(s, axis=-1, keepdims=True)
    e = jnp.exp(s - top)
    total = jnp.sum(e, axis=-1, keepdims=True)
    o[...] = nn((e / total).astype(BF), v[...]).astype(BF)
    lse[...] = jnp.broadcast_to(top + jnp.log(total), lse.shape)


def attend(q, k, v, bias):
    CH, width = q.shape
    NK = k.shape[0]
    tq = min(CH, 256)
    return pl.pallas_call(
        attend_body,
        grid=(width // HD, CH // tq),
        out_shape=(out((CH, width), BF), out((CH, width))),
        in_specs=[
            pl.BlockSpec((tq, HD), lambda h, i: (i, h)),
            pl.BlockSpec((NK, HD), lambda h, i: (0, h)),
            pl.BlockSpec((NK, HD), lambda h, i: (0, h)),
            pl.BlockSpec((tq, NK), lambda h, i: (i, 0)),
        ],
        out_specs=(
            pl.BlockSpec((tq, HD), lambda h, i: (i, h)),
            pl.BlockSpec((tq, HD), lambda h, i: (i, h)),
        ),
        compiler_params=alone(),
        name="attend",
    )(q, k, v, bias)


def attend_back_body(q, k, v, bias, lse, do, dq, dk, dv):
    scale = HD**-0.5
    first = pl.program_id(1) == 0
    s = nt(q[...], k[...]) * scale + bias[...].astype(F32)
    prob = jnp.exp(s - lse[:, 0:1])
    dp = nt(do[...], v[...])
    rowdot = jnp.sum(prob * dp, axis=-1, keepdims=True)
    ds = (prob * (dp - rowdot)).astype(BF)
    dq[...] = nn(ds, k[...]) * scale
    add_k = tn(ds, q[...]) * scale
    add_v = tn(prob.astype(BF), do[...])

    @pl.when(first)
    def _():
        dk[...] = add_k
        dv[...] = add_v

    @pl.when(jnp.logical_not(first))
    def _():
        dk[...] += add_k
        dv[...] += add_v


def attend_back(q, k, v, bias, lse, do):
    CH, width = q.shape
    NK = k.shape[0]
    tq = min(CH, 256)
    rows = pl.BlockSpec((tq, HD), lambda h, i: (i, h))
    keys = pl.BlockSpec((NK, HD), lambda h, i: (0, h))
    return pl.pallas_call(
        attend_back_body,
        grid=(width // HD, CH // tq),
        out_shape=(out((CH, width)), out((NK, width)), out((NK, width))),
        in_specs=[rows, keys, keys, pl.BlockSpec((tq, NK), lambda h, i: (i, 0)), rows, rows],
        out_specs=(rows, keys, keys),
        compiler_params=alone(),
        name="attend_back",
    )(q, k, v, bias, lse, do)


def columns_out(weight, gain, groups, T, cols):
    rows = weight.shape[0]
    scaled = (weight.astype(F32) * gain.astype(F32)[:, None]).astype(BF)
    return scaled.reshape(rows, groups, T, W, cols).transpose(3, 0, 1, 2, 4).reshape(W, rows, -1)


def columns_back(blocks, groups, T, cols):
    rows = blocks.shape[1]
    wide_form = blocks.reshape(W, rows, groups, T, cols).transpose(1, 2, 3, 0, 4)
    return wide_form.reshape(rows, -1).astype(F32)


def gather_tc(x):
    return lax.all_gather(x.reshape(-1, x.shape[-1]), ("t", "c"), axis=0, tiled=True)


def together(*values):
    return lax.optimization_barrier(values)


def scatter_tc(x):
    return lax.psum_scatter(x, ("t", "c"), scatter_dimension=0, tiled=True)


def swiglu(a):
    width = a.shape[1] // 2
    return jax.nn.silu(a[:, :width]) * a[:, width:]


def swiglu_back(a, dh):
    width = a.shape[1] // 2
    gate, up = a[:, :width], a[:, width:]
    s = jax.nn.sigmoid(gate)
    return jnp.concatenate([dh * up * (s * (1.0 + gate * (1.0 - s))), dh * gate * s], axis=1).astype(BF)


def local(
    inputs, segment_ids, cotangent, norm_mixer, in_proj, conv_weight, conv_bias, state_proj,
    step_proj, step_bias, decay_log, skip_gain, mixer_out, norm_ffn_one, gate_up_one, down_one,
    norm_attn, qkv_proj, attn_out, norm_ffn_two, gate_up_two, down_two,
):
    T = lax.axis_size("t")
    t, p, c = here()
    B, D = inputs.shape[1:]
    CH = W * B
    total = CH * T
    seq_len = min(SEQ_MAX, total)
    CB = conv_bias.shape[0]
    DI = CB * W * T * 2
    FB = down_one.shape[0]
    R = step_proj.shape[0]
    N = decay_log.shape[1]
    NR = state_proj.shape[1]
    width = CB * 2 * T
    heads = H // W * HD
    most = min(WIN, total // 2)
    hops = -(-(most - 1) // CH)

    par = jnp.concatenate(
        [
            state_proj, step_proj.T, decay_log, conv_weight.T,
            conv_bias[:, None], step_bias[:, None], skip_gain[:, None],
        ],
        axis=1,
    )
    used = par.shape[1]
    par = jnp.pad(par, ((0, 0), (0, 256 - used)))
    win_out = columns_out(in_proj, norm_mixer, 2, T, 2 * CB)
    seg8 = jnp.broadcast_to(segment_ids, (8, B))
    x0 = inputs[0].astype(F32)
    (win_mine,) = spread_call(21, False, (win_out,))
    w_in = gather_tc(win_mine)
    nh1_ext, seg_all, par_all, gl4 = start_call(T, inputs[0], seg8, par, cotangent[0])

    gu1_out = columns_out(gate_up_one, norm_ffn_one, 2, T, 2 * FB)
    qkv_out = columns_out(qkv_proj, norm_attn, 3, 1, heads)
    gu2_out = columns_out(gate_up_two, norm_ffn_two, 2, T, 2 * FB)
    gu1_mine, qkv_mine, gu2_mine = spread_call(1, False, (gu1_out, qkv_out, gu2_out))
    devices = 2 * W * T
    pairs = []
    for d in range(devices):
        rest = d % (2 * T)
        pairs.append((d, (rest // 2) * 2 * W + (d // (2 * T)) * 2 + rest % 2))
    ao_mine = lax.ppermute(attn_out, ("t", "p", "c"), pairs)
    w_mix = gather_tc(mixer_out)
    w_gu1 = gather_tc(gu1_mine)
    w_d1 = gather_tc(down_one)
    w_qkv = gather_tc(qkv_mine)
    w_ao = gather_tc(ao_mine)
    w_gu2 = gather_tc(gu2_mine)
    w_d2 = gather_tc(down_two)

    seg = seg_all[:, 0, :].reshape(total)
    pos = t * CH + jnp.arange(CH, dtype=jnp.int32)
    padded = jnp.pad(seg, (max(hops * CH, HALO), 0), constant_values=-1)
    lead = max(hops * CH, HALO)
    near = lax.dynamic_slice(padded, (t * CH + lead - HALO,), (CH + HALO,))
    own_seg = near[HALO:]
    conv_mask = jnp.stack(
        [
            (near[HALO - 3 + j : HALO - 3 + j + CH] == own_seg) & ((pos - 3 + j) // seq_len == pos // seq_len)
            & (pos - 3 + j >= 0)
            for j in range(4)
        ]
        + [jnp.zeros((CH,), jnp.bool_)] * 4,
        axis=1,
    ).astype(F32)
    starts = (pos % seq_len == 0) | (near[HALO - 1 : HALO - 1 + CH] != own_seg)
    first = jnp.where(starts, BIG, 0.0).astype(F32)
    alive = jnp.where(jnp.any(starts), 0.0, 1.0).astype(F32)
    NK = (hops + 1) * CH
    key_seg = lax.dynamic_slice(padded, (t * CH + lead - hops * CH,), (NK,))
    key_pos = t * CH - hops * CH + jnp.arange(NK, dtype=jnp.int32)
    away = pos[:, None] - key_pos[None, :]
    allowed = (
        (key_pos[None, :] >= 0) & (away >= 0) & (away < WIN) & (key_seg[None, :] == own_seg[:, None])
        & (key_pos[None, :] // seq_len == (pos // seq_len)[:, None])
    )
    bias = jnp.where(allowed, 0.0, NEG).astype(BF)
    half = HD // 2
    inverse = jnp.exp(jnp.arange(half, dtype=F32) * (-math.log(10000.0) * 2.0 / HD))
    angles = (pos % seq_len).astype(F32)[:, None] * inverse[None, :]
    cos_half, sin_half = jnp.cos(angles), jnp.sin(angles)
    cosine = jnp.concatenate([cos_half, cos_half], axis=1)
    sine = jnp.concatenate([-sin_half, sin_half], axis=1)

    par_all = par_all.reshape(width, 256)
    w_state = par_all[:, :NR]
    w_step = par_all[:, NR : NR + R].T
    side = par_all[:, NR + R : used].astype(F32).T
    a2 = -jnp.exp(side[:N]) * LOG2E
    taps = jnp.pad(side[N : N + 5], ((0, 3), (0, 0)))
    step_row = side[N + 5 : N + 6]
    skip_row = side[N + 6 : N + 7]

    xz = nn(nh1_ext, w_in)
    nh1 = nh1_ext[HALO:]
    u, u_low, part = conv_call(xz, conv_mask, taps, w_state)
    pr = plane_sum(3, part)
    dt_low = pr[:, :R].astype(BF)
    pre = nn(dt_low, w_step) + step_row
    delta = jax.nn.softplus(pre)

    def replicated(block):
        return jnp.broadcast_to(block[:, :, None], (CH, N, 128)).reshape(CH * N, 128)

    brep = replicated(pr[:, R : R + N])
    crep = replicated(pr[:, R + N :])
    sum_delta = jnp.sum(delta, axis=0, keepdims=True)

    def packed(state):
        return jnp.concatenate(
            [state, sum_delta, jnp.full((1, width), alive, F32), jnp.zeros((6, width), F32)], axis=0
        )

    end = scan_one(delta, u, a2, brep, first)
    h_in = chain(4, T, False, packed(end), a2)
    y_scan, marks = scan_two(delta, u, a2, brep, crep, first, h_in)
    y = y_scan + skip_row * u
    zg = xz[HALO:, width:]
    gate_s = jax.nn.sigmoid(zg)
    gated = (y * zg * gate_s).astype(BF)
    x1, nh2 = turn(5, nn(gated, w_mix).astype(BF), x0)

    a_one = nn(nh2, w_gu1)
    h_one = swiglu(a_one).astype(BF)
    x2, nh3 = turn(6, nn(h_one, w_d1).astype(BF), x1)

    qkv = nn(nh3, w_qkv)
    q, k_all, v_all = keys_call(7, T, hops, qkv, cosine, sine)
    o, lse = attend(q, k_all, v_all, bias)
    x3, nh4 = turn(8, nn(o, w_ao).astype(BF), x2)

    a_two = nn(nh4, w_gu2)
    h_two = swiglu(a_two).astype(BF)
    (final,) = turn(9, nn(h_two, w_d2).astype(BF), x3, gather=False, dtype=BF)

    g4 = cotangent[0].astype(F32)
    dw_d2 = tn(h_two, gl4).astype(BF)
    da_two = swiglu_back(a_two, nt(gl4, w_d2))
    da_two, dw_d2 = together(da_two, dw_d2)
    grad_d2 = scatter_tc(dw_d2)
    part, dw_gu2 = together(nt(da_two, w_gu2).astype(BF), tn(nh4, da_two).astype(BF))
    g3, gl3 = turn(10, part, x3, g4)
    raw_gu2 = scatter_tc(dw_gu2)

    do, dw_ao = together(nt(gl3, w_ao).astype(BF), tn(o, gl3).astype(BF))
    raw_ao = scatter_tc(dw_ao)
    dq, dk, dv = attend_back(q, k_all, v_all, bias, lse, do)
    dq, grad_d2 = together(dq, grad_d2)
    dqkv = keys_back_call(11, T, hops, dq, dk, dv, cosine, sine)
    part, dw_qkv = together(nt(dqkv, w_qkv).astype(BF), tn(nh3, dqkv).astype(BF))
    raw_qkv = scatter_tc(dw_qkv)
    part, raw_gu2 = together(part, raw_gu2)
    g2, gl2 = turn(12, part, x2, g3)
    gl2, raw_ao = together(gl2, raw_ao)

    da_one, dw_d1 = together(swiglu_back(a_one, nt(gl2, w_d1)), tn(h_one, gl2).astype(BF))
    grad_d1 = scatter_tc(dw_d1)
    part, dw_gu1 = together(nt(da_one, w_gu1).astype(BF), tn(nh2, da_one).astype(BF))
    raw_gu1 = scatter_tc(dw_gu1)
    g1, gl1 = turn(13, part, x1, g2)
    gl1, raw_qkv = together(gl1, raw_qkv)

    dgate = nt(gl1, w_mix)
    dy = dgate * zg * gate_s
    dz_low = (dgate * y * gate_s * (1.0 + zg * (1.0 - gate_s))).astype(BF)
    dy, dw_mix, dw_z = together(dy, tn(gated, gl1).astype(BF), tn(nh1, dz_low).astype(BF))
    grad_mix = scatter_tc(dw_mix)
    raw_z = scatter_tc(dw_z)
    begin = scan_three(delta, dy, a2, crep, first)
    g_in = chain(14, T, True, packed(begin), a2)
    g_in, grad_d1 = together(g_in, grad_d1)
    ddelta, du_scan, db, dc_mat, ga = scan_four(
        delta, u, dy, skip_row, a2, brep, crep, first, marks, g_in
    )
    dpre = ddelta * jax.nn.sigmoid(pre)
    dpre_low = dpre.astype(BF)
    part_back = jnp.concatenate(
        [
            nt(dpre_low, w_step),
            jnp.sum(db, axis=1).reshape(CH, N),
            jnp.sum(dc_mat, axis=1).reshape(CH, N),
        ],
        axis=1,
    )
    part_back, raw_gu1 = together(part_back, raw_gu1)
    dpr_low = plane_sum(15, part_back).astype(BF)
    du = du_scan + nt(dpr_low, w_state)
    dxs_ext, conv_grads = conv_back_call(xz, conv_mask, taps, du)
    rim = rim_back(16, T, dxs_ext[8:16])
    dxs_low = jnp.concatenate(
        [dxs_ext[HALO : HALO + CH - 8], dxs_ext[HALO + CH - 8 :] + rim], axis=0
    ).astype(BF)
    dxz = jnp.concatenate([dxs_low, dz_low], axis=1)
    dxz, dw_x, grad_mix = together(dxz, tn(nh1, dxs_low).astype(BF), grad_mix)
    raw_x = scatter_tc(dw_x)
    (grad_x,) = turn(17, nt(dxz, w_in).astype(BF), x0, g1, gather=False)

    small = jnp.concatenate(
        [
            tn(u_low, dpr_low),
            tn(dpre_low, dt_low),
            ga.T,
            conv_grads[:5].T,
            jnp.sum(dpre, axis=0)[:, None],
            jnp.sum(dy * u, axis=0)[:, None],
        ],
        axis=1,
    )
    small = jnp.pad(small, ((0, 0), (0, 256 - used))).astype(BF).reshape(2 * T, CB, 256)
    small, raw_z = together(small, raw_z)
    small = small_sum(18, T, small)

    def blocks(x):
        return x.reshape(W, x.shape[0] // W, x.shape[1])

    gu2_b, qkv_b, gu1_b, z_b = spread_call(
        19, True, (blocks(raw_gu2), blocks(raw_qkv), blocks(raw_gu1), blocks(raw_z))
    )
    (x_b,) = spread_call(20, True, (blocks(raw_x),))
    in_b = jnp.concatenate([x_b, z_b], axis=2)
    grad_ao = lax.ppermute(raw_ao, ("t", "p", "c"), [(b, a) for a, b in pairs]).astype(F32)

    def finished(blocks_in, weight, gain, groups, groups_t, cols):
        raw = columns_back(blocks_in, groups, groups_t, cols)
        return (
            jnp.sum(weight.astype(F32) * raw, axis=1),
            raw * gain.astype(F32)[:, None],
        )

    grad_n1, grad_in = finished(in_b, in_proj, norm_mixer, 2, T, 2 * CB)
    grad_n2, grad_gu1 = finished(gu1_b, gate_up_one, norm_ffn_one, 2, T, 2 * FB)
    grad_n3, grad_qkv = finished(qkv_b, qkv_proj, norm_attn, 3, 1, heads)
    grad_n4, grad_gu2 = finished(gu2_b, gate_up_two, norm_ffn_two, 2, T, 2 * FB)
    at = NR + R + N
    return (
        final[None],
        grad_x[None],
        grad_n1,
        grad_in,
        small[:, at : at + 4].T,
        small[:, at + 4],
        small[:, :NR],
        small[:, NR : NR + R].T,
        small[:, at + 5],
        small[:, NR + R : at],
        small[:, at + 6],
        grad_mix.astype(F32),
        grad_n2,
        grad_gu1,
        grad_d1.astype(F32),
        grad_n3,
        grad_qkv,
        grad_ao,
        grad_n4,
        grad_gu2,
        grad_d2.astype(F32),
    )


def solution(mesh):
    chunks = mesh.shape["seq"] // W
    view = Mesh(mesh.devices.reshape(chunks, W, mesh.shape["fsdp"]), ("t", "p", "c"))
    every = ("t", "p", "c")
    tokens = P("c", ("t", "p"), None)
    vector, rows, cols = P(every), P(every, None), P(None, every)
    placed = (
        tokens, P("c", ("t", "p")), tokens,
        vector, rows, cols, vector, rows, cols, vector, rows, vector, rows,
        vector, rows, rows, vector, rows, rows, vector, rows, rows,
    )
    return jax.shard_map(
        local,
        mesh=view,
        in_specs=placed,
        out_specs=(tokens, tokens) + placed[3:],
        check_vma=False,
    )
```

```python
import functools
import math

import jax
import jax.numpy as jnp
from jax import lax
from jax.experimental import pallas as pl
from jax.experimental.pallas import tpu as pltpu
from jax.sharding import Mesh
from jax.sharding import PartitionSpec as P

W = 4
H = 12
HD = 128
WIN = 2048
SEQ_MAX = 8192
EPS = 1e-05
NEG = -1e30
BIG = 1e30
LOG2E = 1.4426950408889634
BF = jnp.bfloat16
F32 = jnp.float32
MESH = pl.DeviceIdType.MESH
HALO = 16
SUB = 64
MIB = 1 << 20


def vmem():
    return pl.BlockSpec(memory_space=pltpu.VMEM)


def hbm():
    return pl.BlockSpec(memory_space=pl.ANY)


def smem():
    return pl.BlockSpec(memory_space=pltpu.SMEM)


def here():
    return lax.axis_index("t"), lax.axis_index("p"), lax.axis_index("c")


def greet(device):
    pl.semaphore_signal(
        pltpu.get_barrier_semaphore(), inc=1, device_id=device, device_id_type=MESH
    )


def arrive(count):
    pl.semaphore_wait(pltpu.get_barrier_semaphore(), count)


def arrive_some(count):
    @pl.when(count > 0)
    def _():
        arrive(count)


def remote(src, dst, send, recv, device):
    return pltpu.make_async_remote_copy(
        src_ref=src,
        dst_ref=dst,
        send_sem=send,
        recv_sem=recv,
        device_id=device,
        device_id_type=MESH,
    )


def flip(p, d):
    return lax.bitwise_xor(p, d)


def dma(*shape):
    return pltpu.SemaphoreType.DMA(shape)


def talk(cid, limit=40):
    return pltpu.CompilerParams(
        collective_id=cid, has_side_effects=True, vmem_limit_bytes=limit * MIB
    )


def alone(limit=56):
    return pltpu.CompilerParams(vmem_limit_bytes=limit * MIB)


def out(shape, dtype=F32):
    return jax.ShapeDtypeStruct(shape, dtype)


def unit(x):
    return x * lax.rsqrt(jnp.mean(x * x, axis=-1, keepdims=True) + EPS)


def first_body(
    T, n, x, seg, par, win, *refs
):
    srcs, refs = refs[:n], refs[n:]
    nh, seg_out, par_out, w_in = refs[:4]
    dsts, refs = refs[4 : 4 + n], refs[4 + n :]
    (nbuf, zbuf, s_n, r_n, s_h, r_h, s_s, r_s, s_p, r_p, s_w, r_w, s_z, r_z, s_c, r_c, s_l, s_o, r_o) = refs
    t, p, c = here()
    B = x.shape[0]
    count = 0
    for dt in range(T):
        tt = lax.rem(t + dt, T)
        for dp in range(W):
            pp = flip(p, dp)
            if dt or dp:
                greet((tt, pp, c))
                count += 1
            if dt == 0 or dp == 0:
                greet((tt, pp, 1 - c))
                count += 1
    nbuf[...] = unit(x[...].astype(F32)).astype(BF)
    zbuf[...] = jnp.zeros_like(zbuf)
    arrive(count)
    half = lax.div(p, 2)
    slot = lax.rem(p, 2) * 2 + c
    me = t * 2 + c

    def block(src, dst, send, recv, q):
        return remote(src.at[q], dst.at[slot], send.at[q], recv.at[slot], (t, q, half))

    def kept(src, dst, send, q):
        return pltpu.make_async_copy(src.at[q], dst.at[slot], send.at[q])

    def exchange(src, dst, send, recv):
        for q in range(W):
            mine = (p == q) & (half == c)

            @pl.when(jnp.logical_not(mine))
            def _():
                block(src, dst, send, recv, q).start()

            @pl.when(mine)
            def _():
                kept(src, dst, send, q).start()

    def exchanged(src, dst, send, recv, j):
        own = (half == c) & (slot == j)

        @pl.when(jnp.logical_not(own))
        def _():
            remote(src.at[0], dst.at[j], send.at[0], recv.at[j], (t, 0, half)).wait_recv()

    def sent(src, dst, send, recv):
        for q in range(W):
            mine = (p == q) & (half == c)

            @pl.when(jnp.logical_not(mine))
            def _():
                block(src, dst, send, recv, q).wait_send()

    landing = w_in.at[t * 2 + half]
    exchange(win, landing, s_w, r_w)
    rows = pl.ds(pl.multiple_of(HALO + p * B, HALO), B)
    copies = []
    for dt in range(T):
        for dc in range(2):
            if dt or dc:
                copies.append(
                    remote(
                        par, par_out.at[me], s_p.at[dt, dc], r_p.at[dt, dc],
                        (lax.rem(t + dt, T), p, flip(c, dc)),
                    )
                )
    for d in range(1, W):
        copies.append(remote(nbuf, nh.at[rows], s_n.at[d], r_n.at[d], (t, flip(p, d), c)))
    for dt in range(T):
        for dp in range(W):
            if dt or dp:
                copies.append(
                    remote(
                        seg, seg_out.at[t * W + p], s_s.at[dt, dp], r_s.at[dt, dp],
                        (lax.rem(t + dt, T), flip(p, dp), c),
                    )
                )
    copies += [
        pltpu.make_async_copy(nbuf, nh.at[rows], s_l.at[0]),
        pltpu.make_async_copy(par, par_out.at[me], s_l.at[1]),
        pltpu.make_async_copy(seg, seg_out.at[t * W + p], s_l.at[2]),
    ]
    for copy in copies:
        copy.start()
    last = (p == W - 1) & (t < T - 1)
    tail = nbuf.at[pl.ds(B - HALO, HALO)]
    head = nh.at[pl.ds(0, HALO)]

    def rim(q):
        return remote(tail, head, s_h.at[q], r_h, (lax.rem(t + 1, T), q, c))

    @pl.when(last)
    def _():
        for q in range(W):
            rim(q).start()

    @pl.when(t == 0)
    def _():
        clear = pltpu.make_async_copy(zbuf, head, s_l.at[3])
        clear.start()
        clear.wait()

    for i in range(n):
        exchange(srcs[i], dsts[i], s_o.at[i], r_o.at[i])

    def on(way, d, j):
        step = 1 - 2 * way
        source = lax.rem(t - step * d + T, T) * 2 + c
        part = w_in.at[source, j]
        return remote(
            part, part, s_z.at[way, d, j], r_z.at[way, d + 1, j], (lax.rem(t + step + T, T), p, c)
        )

    def came(way, d, j):
        step = 1 - 2 * way
        part = w_in.at[lax.rem(t - step * d + T, T) * 2 + c, j]
        return remote(part, part, s_z.at[way, d, j], r_z.at[way, d, j], (lax.rem(t + step + T, T), p, c))

    def across(way, d, j):
        step = 1 - 2 * way
        part = w_in.at[lax.rem(t - step * d + T, T) * 2 + c, j]
        return remote(part, part, s_c.at[way, d, j], r_c.at[way, d, j], (t, p, 1 - c))

    def crossed(way, d, j):
        step = 1 - 2 * way
        part = w_in.at[lax.rem(t - step * d + T, T) * 2 + 1 - c, j]
        return remote(part, part, s_c.at[way, d, j], r_c.at[way, d, j], (t, p, 1 - c))

    def goes(way, d):
        if way == 0:
            return (t >= d) & (t < T - 1)
        return (t + d < T) & (t > 0)

    def arrives(way, d):
        return (t >= d) if way == 0 else (t + d < T)

    for j in range(W):
        mine = (half == c) & (slot == j)

        @pl.when(mine)
        def _():
            for q in range(W):

                @pl.when(p == q)
                def _():
                    kept(win, landing, s_w, q).wait()

        exchanged(win, w_in.at[me], s_w, r_w, j)
        across(0, 0, j).start()
        for way in range(2):

            @pl.when(goes(way, 0))
            def _():
                on(way, 0, j).start()

    for d in range(1, T):
        for j in range(W):
            for way in range(2):

                @pl.when(arrives(way, d))
                def _():
                    came(way, d, j).wait_recv()
                    across(way, d, j).start()

                @pl.when(goes(way, d))
                def _():
                    on(way, d, j).start()

    for copy in copies:
        copy.wait()

    @pl.when(last)
    def _():
        for q in range(W):
            rim(q).wait_send()

    @pl.when(t > 0)
    def _():
        rim(0).wait_recv()

    sent(win, landing, s_w, r_w)
    for i in range(n):
        sent(srcs[i], dsts[i], s_o.at[i], r_o.at[i])
        for q in range(W):
            mine = (p == q) & (half == c)

            @pl.when(mine)
            def _():
                kept(srcs[i], dsts[i], s_o.at[i], q).wait()

        for j in range(W):
            exchanged(srcs[i], dsts[i], s_o.at[i], r_o.at[i], j)
    for d in range(T):
        for j in range(W):
            for way in range(2):
                if d or way == 0:

                    @pl.when(arrives(way, d))
                    def _():
                        across(way, d, j).wait_send()
                        crossed(way, d, j).wait_recv()

                @pl.when(goes(way, d))
                def _():
                    on(way, d, j).wait_send()


def first_call(T, x, seg, par, win, others):
    B, D = x.shape
    n = len(others)
    return pl.pallas_call(
        functools.partial(first_body, T, n),
        out_shape=(
            out((HALO + W * B, D), BF),
            out((W * T,) + seg.shape, jnp.int32),
            out((2 * T,) + par.shape, BF),
            out((2 * T,) + win.shape, BF),
        )
        + tuple(out(a.shape, BF) for a in others),
        in_specs=[vmem()] + [hbm()] * (3 + n),
        out_specs=(hbm(),) * (4 + n),
        scratch_shapes=[
            pltpu.VMEM((B, D), BF),
            pltpu.VMEM((HALO, D), BF),
            dma(W), dma(W), dma(W), pltpu.SemaphoreType.DMA,
            dma(T, W), dma(T, W), dma(T, 2), dma(T, 2), dma(W), dma(W),
            dma(2, T, W), dma(2, T + 1, W), dma(2, T, W), dma(2, T, W), dma(4),
            dma(n, W), dma(n, W),
        ],
        compiler_params=talk(0),
        name="first",
    )(x, seg, par, win, *others)


def spread_body(n, back, *refs):
    srcs, dsts = refs[:n], refs[n : 2 * n]
    s_w, r_w = refs[2 * n :]
    t, p, c = here()
    half = lax.div(p, 2)
    pair = lax.rem(p, 2) * 2 + c
    both = half == c

    def there(q):
        if back:
            return (t, c * 2 + q // 2, jnp.int32(q % 2))
        return (t, jnp.int32(q), half)

    def comes(j):
        if back:
            return (t, jnp.int32(j), half)
        return (t, c * 2 + j // 2, jnp.int32(j % 2))

    slot = p if back else pair
    for q in range(W):
        to, source = there(q), comes(q)
        own = both & ((pair == q) if back else (p == q))
        from_me = both & ((p == q) if back else (pair == q))

        @pl.when(jnp.logical_not(from_me))
        def _():
            greet(source)

    arrive(W - both.astype(jnp.int32))
    for q in range(W):
        own = both & ((pair == q) if back else (p == q))
        for a in range(n):

            @pl.when(jnp.logical_not(own))
            def _():
                remote(
                    srcs[a].at[q], dsts[a].at[slot], s_w.at[a, q], r_w.at[a, slot], there(q)
                ).start()

            @pl.when(own)
            def _():
                pltpu.make_async_copy(srcs[a].at[q], dsts[a].at[slot], s_w.at[a, q]).start()

    for q in range(W):
        own = both & ((pair == q) if back else (p == q))
        from_me = both & ((p == q) if back else (pair == q))
        for a in range(n):

            @pl.when(jnp.logical_not(own))
            def _():
                remote(
                    srcs[a].at[q], dsts[a].at[slot], s_w.at[a, q], r_w.at[a, slot], there(q)
                ).wait_send()

            @pl.when(own)
            def _():
                pltpu.make_async_copy(srcs[a].at[q], dsts[a].at[slot], s_w.at[a, q]).wait()

            @pl.when(jnp.logical_not(from_me))
            def _():
                remote(
                    srcs[a].at[q], dsts[a].at[q], s_w.at[a, q], r_w.at[a, q], there(q)
                ).wait_recv()


def spread_call(cid, back, arrays):
    n = len(arrays)
    return pl.pallas_call(
        functools.partial(spread_body, n, back),
        out_shape=tuple(out(a.shape, a.dtype) for a in arrays),
        in_specs=[hbm()] * n,
        out_specs=(hbm(),) * n,
        scratch_shapes=[dma(n, W), dma(n, W)],
        compiler_params=talk(cid),
        name="spread%d" % cid,
    )(*arrays)


def plane_sum_body(x, o, sb, recv, ss, rs):
    t, p, c = here()
    for d in range(1, W):
        greet((t, flip(p, d), c))
    sb[...] = x[...].astype(BF)
    arrive(W - 1)
    copies = [
        remote(sb, recv.at[d - 1], ss.at[d - 1], rs.at[d - 1], (t, flip(p, d), c))
        for d in range(1, W)
    ]
    for copy in copies:
        copy.start()
    for copy in copies:
        copy.wait()
    total = x[...]
    for d in range(W - 1):
        total = total + recv[d].astype(F32)
    o[...] = total


def plane_sum(cid, x):
    return pl.pallas_call(
        plane_sum_body,
        out_shape=out(x.shape),
        in_specs=[vmem()],
        out_specs=vmem(),
        scratch_shapes=[
            pltpu.VMEM(x.shape, BF),
            pltpu.VMEM((W - 1,) + x.shape, BF),
            dma(W - 1),
            dma(W - 1),
        ],
        compiler_params=talk(cid),
        name="plane_sum%d" % cid,
    )(x)


def gather_job(T, src, dst, s_z, r_z, s_c, r_c, s_l):
    t, p, c = here()

    def part(dt, core):
        return dst.at[lax.rem(t - dt + T, T) * 2 + core]

    def out_to(dt):
        return remote(src, part(0, c), s_z.at[dt], r_z.at[dt], (lax.rem(t + dt, T), p, c))

    def across(dt):
        return remote(src if dt == 0 else part(dt, c), part(dt, c), s_c.at[dt], r_c.at[dt], (t, p, 1 - c))

    keep = pltpu.make_async_copy(src, part(0, c), s_l)

    def begin():
        for dt in range(1, T):
            out_to(dt).start()
        across(0).start()
        keep.start()

    def end():
        for dt in range(1, T):
            out_to(dt).wait_recv()
            across(dt).start()
        keep.wait()
        for dt in range(T):
            across(dt).wait_send()
            remote(part(dt, 1 - c), part(dt, 1 - c), s_c.at[dt], r_c.at[dt], (t, p, 1 - c)).wait_recv()
        for dt in range(1, T):
            out_to(dt).wait_send()

    return begin, end


def scatter_job(T, src, dst, mine, other, recv, s_z, r_z, s_c, r_c, s_l):
    t, p, c = here()

    def at(dt):
        return lax.rem(t + dt, T)

    def across(dt):
        return remote(
            src.at[at(dt) * 2 + 1 - c], other.at[dt], s_c.at[dt], r_c.at[dt], (t, p, 1 - c)
        )

    def load(dt):
        return pltpu.make_async_copy(src.at[at(dt) * 2 + c], mine.at[dt], s_l.at[dt])

    def out_to(dt):
        return remote(mine.at[dt], recv.at[dt - 1], s_z.at[dt], r_z.at[dt], (at(dt), p, c))

    order = list(range(1, T)) + [0]

    def begin():
        for dt in order:
            across(dt).start()
            load(dt).start()
        for dt in order[:-1]:
            across(dt).wait_recv()
            load(dt).wait()
            mine[dt] = (mine[dt].astype(F32) + other[dt].astype(F32)).astype(BF)
            out_to(dt).start()

    def end():
        across(0).wait_recv()
        load(0).wait()
        total = mine[0].astype(F32) + other[0].astype(F32)
        for dt in range(1, T):
            out_to(dt).wait_recv()
            total = total + recv[dt - 1].astype(F32)
        dst[...] = total
        for dt in range(T):
            across(dt).wait_send()
        for dt in range(1, T):
            out_to(dt).wait_send()

    return begin, end


def turn_body(T, back, gather, parts, job, *refs):
    refs = list(refs)
    part = refs.pop(0)
    x = refs.pop(0)
    g = refs.pop(0) if back else None
    job_src = refs.pop(0) if job else None
    o = refs.pop(0)
    gath = refs.pop(0) if gather else None
    job_dst = refs.pop(0) if job else None
    own, recv, sbuf, ss, rs, ls, ss2, rs2, ls2 = refs[:9]
    t, p, c = here()
    B = x.shape[0]
    rows = B // parts
    for d in range(1, W):
        greet((t, flip(p, d), c))
    count = W - 1
    if job:
        for dt in range(1, T):
            greet((lax.rem(t + dt, T), p, c))
        greet((t, p, 1 - c))
        count += T
        build = gather_job if job == "gather" else scatter_job
        begin, end = build(T, job_src, job_dst, *refs[9:])
    local = pltpu.make_async_copy(part.at[pl.ds(pl.multiple_of(p * B, B), B)], own, ls)
    local.start()
    arrive(count)
    first = {}
    for k in range(parts):
        for d in range(1, W):
            q = flip(p, d)
            first[k, d] = remote(
                part.at[pl.ds(pl.multiple_of(q * B + k * rows, rows), rows)],
                recv.at[d - 1, pl.ds(k * rows, rows)],
                ss.at[d - 1, k],
                rs.at[d - 1, k],
                (t, q, c),
            )
            first[k, d].start()
    if job:
        begin()
    local.wait()
    later = []
    for k in range(parts):
        for d in range(1, W):
            first[k, d].wait_recv()
        cut = pl.ds(k * rows, rows)
        total = own[cut, :].astype(F32)
        for d in range(W - 1):
            total = total + recv[d, cut, :].astype(F32)
        value = x[cut, :]
        if back:
            r = lax.rsqrt(jnp.mean(value * value, axis=-1, keepdims=True) + EPS)
            hat = value * r
            new = g[cut, :] + r * (total - hat * jnp.mean(total * hat, axis=-1, keepdims=True))
        else:
            new = value + total
        o[cut, :] = new.astype(o.dtype)
        if gather:
            sbuf[cut, :] = (new if back else unit(new)).astype(BF)
            place = gath.at[pl.ds(pl.multiple_of(p * B + k * rows, rows), rows)]
            for d in range(1, W):
                later.append(
                    remote(sbuf.at[cut], place, ss2.at[d - 1, k], rs2.at[d - 1, k], (t, flip(p, d), c))
                )
            later.append(pltpu.make_async_copy(sbuf.at[cut], place, ls2.at[k]))
            for copy in later[-W:]:
                copy.start()
    if job:
        end()
    for copy in first.values():
        copy.wait_send()
    for copy in later:
        copy.wait()


def turn(cid, part, x, g=None, gather=True, dtype=F32, parts=2, T=1, fetch=None, give=None):
    B, D = x.shape
    back = g is not None
    shapes = [out((B, D), dtype)]
    specs = [vmem()]
    args = (part, x) + ((g,) if back else ())
    in_specs = [hbm()] + [vmem()] * (len(args) - 1)
    scratch = [
        pltpu.VMEM((B, D), BF),
        pltpu.VMEM((W - 1, B, D), BF),
        pltpu.VMEM((B, D), BF),
        dma(W - 1, parts), dma(W - 1, parts), pltpu.SemaphoreType.DMA,
        dma(W - 1, parts), dma(W - 1, parts), dma(parts),
    ]
    if gather:
        shapes.append(out((W * B, D), BF))
        specs.append(hbm())
    job = None
    if fetch is not None:
        job = "gather"
        args += (fetch,)
        in_specs.append(hbm())
        shapes.append(out((2 * T,) + fetch.shape, BF))
        specs.append(hbm())
        scratch += [dma(T), dma(T), dma(T), dma(T), pltpu.SemaphoreType.DMA]
    if give is not None:
        job = "scatter"
        give = give.reshape(2 * T, -1, give.shape[-1])
        args += (give,)
        in_specs.append(hbm())
        shapes.append(out(give.shape[1:]))
        specs.append(vmem())
        scratch += [
            pltpu.VMEM((T,) + give.shape[1:], BF),
            pltpu.VMEM((T,) + give.shape[1:], BF),
            pltpu.VMEM((T - 1,) + give.shape[1:], BF),
            dma(T), dma(T), dma(T), dma(T), dma(T),
        ]
    return pl.pallas_call(
        functools.partial(turn_body, T, back, gather, parts, job),
        out_shape=tuple(shapes),
        in_specs=in_specs,
        out_specs=tuple(specs),
        scratch_shapes=scratch,
        compiler_params=talk(cid),
        name="turn%d" % cid,
    )(*args)


def chain_body(T, back, v, a2, h, recv, ss, rs):
    t, p, c = here()
    sign = -1 if back else 1
    for k in range(1, T):
        source = t - sign * k

        @pl.when((source >= 0) & (source < T))
        def _():
            greet((lax.rem(source + T, T), p, c))

    arrive_some(t if back else T - 1 - t)

    def send(k):
        to = lax.rem(t + sign * k + T, T)
        return remote(v, recv.at[k - 1], ss.at[k - 1], rs.at[k - 1], (to, p, c))

    for k in range(1, T):
        to = t + sign * k

        @pl.when((to >= 0) & (to < T))
        def _():
            send(k).start()

    h[...] = jnp.zeros_like(h)
    for k in range(T - 1, 0, -1):
        source = t - sign * k

        @pl.when((source >= 0) & (source < T))
        def _():
            send(k).wait_recv()
            decay = jnp.exp2(a2[...] * recv[k - 1, 16:17, :]) * recv[k - 1, 17:18, :]
            h[...] = recv[k - 1, 0:16, :] + decay * h[...]

    for k in range(1, T):
        to = t + sign * k

        @pl.when((to >= 0) & (to < T))
        def _():
            send(k).wait_send()


def chain(cid, T, back, v, a2):
    return pl.pallas_call(
        functools.partial(chain_body, T, back),
        out_shape=out(a2.shape),
        in_specs=[vmem(), vmem()],
        out_specs=vmem(),
        scratch_shapes=[pltpu.VMEM((T - 1,) + v.shape, F32), dma(T - 1), dma(T - 1)],
        compiler_params=talk(cid),
        name="chain%d" % cid,
    )(v, a2)


def rope(w, cosine, sine):
    return w * cosine + pltpu.roll(w, HD // 2, 1) * sine


def keys_body(T, hops, qkv, cosine, sine, ct, q, k_all, v_all, ct_out, ss, rs, s_g, r_g, s_l):
    t, p, c = here()
    CH = q.shape[0]
    width = q.shape[1]
    B = ct.shape[0]

    @pl.when(t > 0)
    def _():
        greet((lax.rem(t - 1 + T, T), p, c))

    for d in range(1, W):
        greet((t, flip(p, d), c))

    mine = pl.ds(hops * CH, CH)
    for h in range(width // HD):
        cols = pl.ds(h * HD, HD)
        k_all[mine, cols] = rope(
            qkv[:, pl.ds(width + h * HD, HD)], cosine[...], sine[...]
        ).astype(BF)
    v_all[mine, :] = qkv[:, pl.ds(2 * width, width)].astype(BF)

    @pl.when(t < T - 1)
    def _():
        arrive(W)

    @pl.when(t == T - 1)
    def _():
        arrive(W - 1)

    def send(a, d):
        ref = (k_all, v_all)[a]
        return remote(
            ref.at[pl.ds((hops - d + 1) * CH, CH)],
            ref.at[pl.ds((hops - d) * CH, CH)],
            ss.at[a, d - 1],
            rs.at[a, d - 1],
            (lax.rem(t + 1, T), p, c),
        )

    for d in range(1, hops + 1):
        goes = (t < T - 1) & (t >= d - 1)

        @pl.when(goes)
        def _():
            send(0, d).start()
            send(1, d).start()

        if d == 1:
            rows = ct_out.at[pl.ds(pl.multiple_of(p * B, B), B)]
            copies = [
                remote(ct, rows, s_g.at[e], r_g.at[e], (t, flip(p, e), c)) for e in range(1, W)
            ] + [pltpu.make_async_copy(ct, rows, s_l)]
            for copy in copies:
                copy.start()
            for h in range(width // HD):
                cols = pl.ds(h * HD, HD)
                q[:, cols] = rope(qkv[:, cols], cosine[...], sine[...]).astype(BF)

        @pl.when(t < d)
        def _():
            k_all[pl.ds((hops - d) * CH, CH), :] = jnp.zeros((CH, width), BF)
            v_all[pl.ds((hops - d) * CH, CH), :] = jnp.zeros((CH, width), BF)

        @pl.when(t >= d)
        def _():
            send(0, d).wait_recv()
            send(1, d).wait_recv()

    for d in range(1, hops + 1):
        goes = (t < T - 1) & (t >= d - 1)

        @pl.when(goes)
        def _():
            send(0, d).wait_send()
            send(1, d).wait_send()

    for copy in copies:
        copy.wait()


def keys_call(cid, T, hops, qkv, cosine, sine, ct):
    CH = qkv.shape[0]
    width = qkv.shape[1] // 3
    return pl.pallas_call(
        functools.partial(keys_body, T, hops),
        out_shape=(
            out((CH, width), BF),
            out(((hops + 1) * CH, width), BF),
            out(((hops + 1) * CH, width), BF),
            out((W * ct.shape[0], ct.shape[1]), BF),
        ),
        in_specs=[vmem()] * 3 + [hbm()],
        out_specs=(vmem(),) * 3 + (hbm(),),
        scratch_shapes=[
            dma(2, hops), dma(2, hops), dma(W), dma(W), pltpu.SemaphoreType.DMA,
        ],
        compiler_params=talk(cid),
        name="keys",
    )(qkv, cosine, sine, ct)


def keys_back_body(T, hops, dq, dk, dv, cosine, sine, dqkv, sb, recv, ss, rs):
    t, p, c = here()
    CH = dq.shape[0]
    width = dq.shape[1]

    @pl.when(t < T - 1)
    def _():
        greet((lax.rem(t + 1, T), p, c))

    def send(a, d):
        return remote(
            sb.at[a, d - 1],
            recv.at[a, d - 1],
            ss.at[a, d - 1],
            rs.at[a, d - 1],
            (lax.rem(t - 1 + T, T), p, c),
        )

    for d in range(hops, 0, -1):
        rows = pl.ds((hops - d) * CH, CH)
        k_sum = dk[rows, :]
        v_sum = dv[rows, :]
        if d == hops:
            sb[0, d - 1] = k_sum.astype(BF)
            sb[1, d - 1] = v_sum.astype(BF)

            @pl.when(t > 0)
            def _():
                arrive(1)
        else:

            @pl.when((t < T - 1) & (t >= d))
            def _():
                send(0, d + 1).wait_recv()
                send(1, d + 1).wait_recv()

            @pl.when((t == T - 1) | (t < d))
            def _():
                recv[0, d] = jnp.zeros((CH, width), BF)
                recv[1, d] = jnp.zeros((CH, width), BF)

            sb[0, d - 1] = (k_sum + recv[0, d].astype(F32)).astype(BF)
            sb[1, d - 1] = (v_sum + recv[1, d].astype(F32)).astype(BF)

        @pl.when(t >= d)
        def _():
            send(0, d).start()
            send(1, d).start()

        if d == hops:
            for h in range(width // HD):
                cols = pl.ds(h * HD, HD)
                dqkv[:, cols] = rope(dq[:, cols], cosine[...], -sine[...]).astype(BF)

    @pl.when(t < T - 1)
    def _():
        send(0, 1).wait_recv()
        send(1, 1).wait_recv()

    @pl.when(t == T - 1)
    def _():
        recv[0, 0] = jnp.zeros((CH, width), BF)
        recv[1, 0] = jnp.zeros((CH, width), BF)

    mine = pl.ds(hops * CH, CH)
    for h in range(width // HD):
        cols = pl.ds(h * HD, HD)
        k_sum = dk[mine, cols] + recv[0, 0, :, cols].astype(F32)
        v_sum = dv[mine, cols] + recv[1, 0, :, cols].astype(F32)
        dqkv[:, pl.ds(width + h * HD, HD)] = rope(k_sum, cosine[...], -sine[...]).astype(BF)
        dqkv[:, pl.ds(2 * width + h * HD, HD)] = v_sum.astype(BF)
    for d in range(hops, 0, -1):

        @pl.when(t >= d)
        def _():
            send(0, d).wait_send()
            send(1, d).wait_send()


def keys_back_call(cid, T, hops, dq, dk, dv, cosine, sine):
    CH, width = dq.shape
    return pl.pallas_call(
        functools.partial(keys_back_body, T, hops),
        out_shape=out((CH, 3 * width), BF),
        in_specs=[vmem()] * 5,
        out_specs=vmem(),
        scratch_shapes=[
            pltpu.VMEM((2, hops, CH, width), BF),
            pltpu.VMEM((2, hops, CH, width), BF),
            dma(2, hops),
            dma(2, hops),
        ],
        compiler_params=talk(cid, 48),
        name="keys_back",
    )(dq, dk, dv, cosine, sine)


def rim_body(T, x, o, recv, ss, rs):
    t, p, c = here()

    @pl.when(t < T - 1)
    def _():
        greet((lax.rem(t + 1, T), p, c))

    def send():
        return remote(x, recv, ss, rs, (lax.rem(t + T - 1, T), p, c))

    @pl.when(t > 0)
    def _():
        arrive(1)
        send().start()
        send().wait_send()

    o[...] = jnp.zeros_like(o)

    @pl.when(t < T - 1)
    def _():
        send().wait_recv()
        o[...] = recv[...]


def rim_back(cid, T, x):
    return pl.pallas_call(
        functools.partial(rim_body, T),
        out_shape=out(x.shape),
        in_specs=[vmem()],
        out_specs=vmem(),
        scratch_shapes=[pltpu.VMEM(x.shape, F32), pltpu.SemaphoreType.DMA, pltpu.SemaphoreType.DMA],
        compiler_params=talk(cid),
        name="rim_back",
    )(x)


def small_body(T, x, o, recv, ss, rs):
    t, p, c = here()
    peers = [(dt, dc) for dt in range(T) for dc in range(2) if dt or dc]

    def device(dt, dc):
        return lax.rem(t + dt, T), flip(c, dc)

    for dt, dc in peers:
        tt, cc = device(dt, dc)
        greet((tt, p, cc))
    arrive(len(peers))
    copies = []
    for i, (dt, dc) in enumerate(peers):
        tt, cc = device(dt, dc)
        copies.append(remote(x.at[tt * 2 + cc], recv.at[i], ss.at[i], rs.at[i], (tt, p, cc)))
        copies[-1].start()
    total = x[t * 2 + c].astype(F32)
    for i, copy in enumerate(copies):
        copy.wait()
        total = total + recv[i].astype(F32)
    o[...] = total


def small_sum(cid, T, x):
    n = x.shape[0] - 1
    return pl.pallas_call(
        functools.partial(small_body, T),
        out_shape=out(x.shape[1:]),
        in_specs=[vmem()],
        out_specs=vmem(),
        scratch_shapes=[pltpu.VMEM((n,) + x.shape[1:], x.dtype), dma(n), dma(n)],
        compiler_params=talk(cid),
        name="small_sum",
    )(x)


def conv_sum(xz, mask, taps, lo, size):
    width = taps.shape[1]
    total = jnp.broadcast_to(taps[4:5, :], (size, width))
    for j in range(4):
        rows = xz[pl.ds(lo + HALO - 3 + j, size), pl.ds(0, width)]
        total = total + taps[j : j + 1, :] * rows * mask[pl.ds(lo, size), j : j + 1]
    return total


def conv_body(xz, mask, taps, proj, u, u_low, part):
    CH = u.shape[0]
    step = min(CH, 128)
    for lo in range(0, CH, step):
        cut = pl.ds(lo, step)
        c = conv_sum(xz, mask, taps, lo, step)
        value = c / (1.0 + jnp.exp(-c))
        u[cut, :] = value
        low = value.astype(BF)
        u_low[cut, :] = low
        part[cut, :] = jnp.dot(low, proj[...], preferred_element_type=F32)


def conv_call(xz, mask, taps, proj):
    CH = mask.shape[0]
    width = taps.shape[1]
    return pl.pallas_call(
        conv_body,
        out_shape=(out((CH, width)), out((CH, width), BF), out((CH, proj.shape[1]))),
        in_specs=[vmem()] * 4,
        out_specs=(vmem(),) * 3,
        compiler_params=alone(),
        name="conv",
    )(xz, mask, taps, proj)


def conv_back_body(xz, mask, taps, du, dxs, grads):
    CH, width = du.shape
    step = min(CH, 128)
    dxs[...] = jnp.zeros_like(dxs)
    sums = [jnp.zeros((1, width), F32) for _ in range(5)]
    for lo in range(0, CH, step):
        c = conv_sum(xz, mask, taps, lo, step)
        s = 1.0 / (1.0 + jnp.exp(-c))
        dc = du[pl.ds(lo, step), :] * (s * (1.0 + c * (1.0 - s)))
        sums[4] = sums[4] + jnp.sum(dc, axis=0, keepdims=True)
        for j in range(4):
            rows = pl.ds(lo + HALO - 3 + j, step)
            live = dc * mask[pl.ds(lo, step), j : j + 1]
            sums[j] = sums[j] + jnp.sum(live * xz[rows, pl.ds(0, width)], axis=0, keepdims=True)
            dxs[rows, :] = dxs[rows, :] + live * taps[j : j + 1, :]
    grads[...] = jnp.zeros_like(grads)
    for j in range(5):
        grads[j : j + 1, :] = sums[j]


def conv_back_call(xz, mask, taps, du):
    CH, width = du.shape
    return pl.pallas_call(
        conv_back_body,
        out_shape=(out((HALO + CH, width)), out((8, width))),
        in_specs=[vmem()] * 4,
        out_specs=(vmem(),) * 2,
        compiler_params=alone(),
        name="conv_back",
    )(xz, mask, taps, du)


def wide(block, width):
    return jnp.concatenate([block] * (width // 128), axis=1) if width > 128 else block


def fold(block):
    total = block[:, 0:128]
    for lo in range(128, block.shape[1], 128):
        total = total + block[:, lo : lo + 128]
    return total


def scan_one_body(delta, u, a2, brep, first, end):
    CH, width = delta.shape
    decay = a2[...]

    def group(g, h):
        lo = pl.multiple_of(g * 8, 8)
        d8 = delta[pl.ds(lo, 8), :]
        du8 = d8 * u[pl.ds(lo, 8), :]
        for i in range(8):
            d = d8[i : i + 1, :] + first[lo + i]
            b = wide(brep[pl.ds(pl.multiple_of(g * 128 + i * 16, 16), 16), :], width)
            h = jnp.exp2(d * decay) * h + du8[i : i + 1, :] * b
        return h

    end[...] = lax.fori_loop(0, CH // 8, group, jnp.zeros(decay.shape, F32))


def scan_one(delta, u, a2, brep, first):
    return pl.pallas_call(
        scan_one_body,
        out_shape=out(a2.shape),
        in_specs=[vmem()] * 4 + [smem()],
        out_specs=vmem(),
        compiler_params=alone(),
        name="scan_one",
    )(delta, u, a2, brep, first)


def scan_two_body(delta, u, a2, brep, crep, first, h_in, y, marks):
    CH, width = delta.shape
    decay = a2[...]
    row = lax.broadcasted_iota(jnp.int32, (8, width), 0)

    def group(g, h):
        lo = pl.multiple_of(g * 8, 8)

        @pl.when(lax.rem(g, SUB // 8) == 0)
        def _():
            marks[pl.ds(pl.multiple_of(lax.div(g, SUB // 8) * 16, 16), 16), :] = h

        d8 = delta[pl.ds(lo, 8), :]
        du8 = d8 * u[pl.ds(lo, 8), :]
        y8 = jnp.zeros((8, width), F32)
        for i in range(8):
            at = pl.ds(pl.multiple_of(g * 128 + i * 16, 16), 16)
            d = d8[i : i + 1, :] + first[lo + i]
            h = jnp.exp2(d * decay) * h + du8[i : i + 1, :] * wide(brep[at, :], width)
            total = jnp.sum(h * wide(crep[at, :], width), axis=0, keepdims=True)
            y8 = jnp.where(row == i, total, y8)
        y[pl.ds(lo, 8), :] = y8
        return h

    lax.fori_loop(0, CH // 8, group, h_in[...])


def scan_two(delta, u, a2, brep, crep, first, h_in):
    CH, width = delta.shape
    return pl.pallas_call(
        scan_two_body,
        out_shape=(out((CH, width)), out((CH // SUB * 16, width))),
        in_specs=[vmem()] * 5 + [smem(), vmem()],
        out_specs=(vmem(),) * 2,
        compiler_params=alone(),
        name="scan_two",
    )(delta, u, a2, brep, crep, first, h_in)


def scan_three_body(delta, dy, a2, crep, first, start):
    CH, width = delta.shape
    decay = a2[...]

    def group(step, carry):
        g = CH // 8 - 1 - step
        lo = pl.multiple_of(g * 8, 8)
        d8 = delta[pl.ds(lo, 8), :]
        dy8 = dy[pl.ds(lo, 8), :]
        for i in range(7, -1, -1):
            at = pl.ds(pl.multiple_of(g * 128 + i * 16, 16), 16)
            d = d8[i : i + 1, :] + first[lo + i]
            lam = dy8[i : i + 1, :] * wide(crep[at, :], width) + carry
            carry = jnp.exp2(d * decay) * lam
        return carry

    start[...] = lax.fori_loop(0, CH // 8, group, jnp.zeros(decay.shape, F32))


def scan_three(delta, dy, a2, crep, first):
    return pl.pallas_call(
        scan_three_body,
        out_shape=out(a2.shape),
        in_specs=[vmem()] * 4 + [smem()],
        out_specs=vmem(),
        compiler_params=alone(),
        name="scan_three",
    )(delta, dy, a2, crep, first)


def scan_four_body(
    delta, u, dy, skip, a2, brep, crep, first, marks, g_in,
    ddelta, du_out, db, dc, ga, keep_a, keep_w,
):
    CH, width = delta.shape
    decay = a2[...]
    rate = decay * (1.0 / LOG2E)
    row = lax.broadcasted_iota(jnp.int32, (8, width), 0)
    per = SUB // 8

    def block(step, carried):
        blk = CH // SUB - 1 - step

        def forward(k, h):
            g = blk * per + k
            lo = pl.multiple_of(g * 8, 8)
            d8 = delta[pl.ds(lo, 8), :]
            du8 = d8 * u[pl.ds(lo, 8), :]
            for i in range(8):
                at = pl.ds(pl.multiple_of(g * 128 + i * 16, 16), 16)
                put = pl.ds(pl.multiple_of(k * 128 + i * 16, 16), 16)
                d = d8[i : i + 1, :] + first[lo + i]
                a = jnp.exp2(d * decay)
                keep_a[put, :] = a
                w = a * h
                keep_w[put, :] = w
                h = w + du8[i : i + 1, :] * wide(brep[at, :], width)
            return h

        lax.fori_loop(0, per, forward, marks[pl.ds(pl.multiple_of(blk * 16, 16), 16), :])

        def backward(back, state):
            carry, total_a = state
            k = per - 1 - back
            g = blk * per + k
            lo = pl.multiple_of(g * 8, 8)
            d8 = delta[pl.ds(lo, 8), :]
            u8 = u[pl.ds(lo, 8), :]
            du8 = d8 * u8
            dy8 = dy[pl.ds(lo, 8), :]
            s1 = jnp.zeros((8, width), F32)
            s2 = jnp.zeros((8, width), F32)
            for i in range(7, -1, -1):
                at = pl.ds(pl.multiple_of(g * 128 + i * 16, 16), 16)
                put = pl.ds(pl.multiple_of(k * 128 + i * 16, 16), 16)
                b = wide(brep[at, :], width)
                du = du8[i : i + 1, :]
                dyi = dy8[i : i + 1, :]
                w = keep_w[put, :]
                lam = dyi * wide(crep[at, :], width) + carry
                lw = lam * w
                s1 = jnp.where(row == i, jnp.sum(lam * b, axis=0, keepdims=True), s1)
                s2 = jnp.where(row == i, jnp.sum(lw * rate, axis=0, keepdims=True), s2)
                total_a = total_a + lw * d8[i : i + 1, :]
                dc[at, :] = fold((w + du * b) * dyi)
                db[at, :] = fold(lam * du)
                carry = keep_a[put, :] * lam
            ddelta[pl.ds(lo, 8), :] = s2 + u8 * s1
            du_out[pl.ds(lo, 8), :] = d8 * s1 + skip[0:1, :] * dy8
            return carry, total_a

        return lax.fori_loop(0, per, backward, carried)

    carry, total_a = lax.fori_loop(
        0, CH // SUB, block, (g_in[...], jnp.zeros(decay.shape, F32))
    )
    ga[...] = total_a * rate


def scan_four(delta, u, dy, skip, a2, brep, crep, first, marks, g_in):
    CH, width = delta.shape
    return pl.pallas_call(
        scan_four_body,
        out_shape=(
            out((CH, width)),
            out((CH, width)),
            out((CH * 16, 128)),
            out((CH * 16, 128)),
            out(a2.shape),
        ),
        in_specs=[vmem()] * 7 + [smem(), vmem(), vmem()],
        out_specs=(vmem(),) * 5,
        scratch_shapes=[pltpu.VMEM((SUB * 16, width), F32), pltpu.VMEM((SUB * 16, width), F32)],
        compiler_params=alone(),
        name="scan_four",
    )(delta, u, dy, skip, a2, brep, crep, first, marks, g_in)


def nt(a, b):
    return lax.dot_general(a, b, (((1,), (1,)), ((), ())), preferred_element_type=F32)


def tn(a, b):
    return lax.dot_general(a, b, (((0,), (0,)), ((), ())), preferred_element_type=F32)


def nn(a, b):
    return jnp.dot(a, b, preferred_element_type=F32)


def attend_body(q, k, v, bias, o, lse):
    s = nt(q[...], k[...]) * (HD**-0.5) + bias[...].astype(F32)
    top = jnp.max(s, axis=-1, keepdims=True)
    e = jnp.exp(s - top)
    total = jnp.sum(e, axis=-1, keepdims=True)
    o[...] = nn((e / total).astype(BF), v[...]).astype(BF)
    lse[...] = jnp.broadcast_to(top + jnp.log(total), lse.shape)


def attend(q, k, v, bias):
    CH, width = q.shape
    NK = k.shape[0]
    tq = min(CH, 256)
    return pl.pallas_call(
        attend_body,
        grid=(width // HD, CH // tq),
        out_shape=(out((CH, width), BF), out((CH, width))),
        in_specs=[
            pl.BlockSpec((tq, HD), lambda h, i: (i, h)),
            pl.BlockSpec((NK, HD), lambda h, i: (0, h)),
            pl.BlockSpec((NK, HD), lambda h, i: (0, h)),
            pl.BlockSpec((tq, NK), lambda h, i: (i, 0)),
        ],
        out_specs=(
            pl.BlockSpec((tq, HD), lambda h, i: (i, h)),
            pl.BlockSpec((tq, HD), lambda h, i: (i, h)),
        ),
        compiler_params=alone(),
        name="attend",
    )(q, k, v, bias)


def attend_back_body(q, k, v, bias, lse, do, dq, dk, dv):
    scale = HD**-0.5
    first = pl.program_id(1) == 0
    s = nt(q[...], k[...]) * scale + bias[...].astype(F32)
    prob = jnp.exp(s - lse[:, 0:1])
    dp = nt(do[...], v[...])
    rowdot = jnp.sum(prob * dp, axis=-1, keepdims=True)
    ds = (prob * (dp - rowdot)).astype(BF)
    dq[...] = nn(ds, k[...]) * scale
    add_k = tn(ds, q[...]) * scale
    add_v = tn(prob.astype(BF), do[...])

    @pl.when(first)
    def _():
        dk[...] = add_k
        dv[...] = add_v

    @pl.when(jnp.logical_not(first))
    def _():
        dk[...] += add_k
        dv[...] += add_v


def attend_back(q, k, v, bias, lse, do):
    CH, width = q.shape
    NK = k.shape[0]
    tq = min(CH, 256)
    rows = pl.BlockSpec((tq, HD), lambda h, i: (i, h))
    keys = pl.BlockSpec((NK, HD), lambda h, i: (0, h))
    return pl.pallas_call(
        attend_back_body,
        grid=(width // HD, CH // tq),
        out_shape=(out((CH, width)), out((NK, width)), out((NK, width))),
        in_specs=[rows, keys, keys, pl.BlockSpec((tq, NK), lambda h, i: (i, 0)), rows, rows],
        out_specs=(rows, keys, keys),
        compiler_params=alone(),
        name="attend_back",
    )(q, k, v, bias, lse, do)


def columns_out(weight, gain, groups, T, cols):
    rows = weight.shape[0]
    scaled = (weight.astype(F32) * gain.astype(F32)[:, None]).astype(BF)
    return scaled.reshape(rows, groups, T, W, cols).transpose(3, 0, 1, 2, 4).reshape(W, rows, -1)


def columns_back(blocks, groups, T, cols):
    rows = blocks.shape[1]
    wide_form = blocks.reshape(W, rows, groups, T, cols).transpose(1, 2, 3, 0, 4)
    return wide_form.reshape(rows, -1).astype(F32)


def gather_tc(x):
    return lax.all_gather(x.reshape(-1, x.shape[-1]), ("t", "c"), axis=0, tiled=True)


def together(*values):
    return lax.optimization_barrier(values)


def scatter_tc(x):
    return lax.psum_scatter(x, ("t", "c"), scatter_dimension=0, tiled=True)


def swiglu(a):
    width = a.shape[1] // 2
    return jax.nn.silu(a[:, :width]) * a[:, width:]


def swiglu_back(a, dh):
    width = a.shape[1] // 2
    gate, up = a[:, :width], a[:, width:]
    s = jax.nn.sigmoid(gate)
    return jnp.concatenate([dh * up * (s * (1.0 + gate * (1.0 - s))), dh * gate * s], axis=1).astype(BF)


def local(
    inputs, segment_ids, cotangent, norm_mixer, in_proj, conv_weight, conv_bias, state_proj,
    step_proj, step_bias, decay_log, skip_gain, mixer_out, norm_ffn_one, gate_up_one, down_one,
    norm_attn, qkv_proj, attn_out, norm_ffn_two, gate_up_two, down_two,
):
    T = lax.axis_size("t")
    t, p, c = here()
    B, D = inputs.shape[1:]
    CH = W * B
    total = CH * T
    seq_len = min(SEQ_MAX, total)
    CB = conv_bias.shape[0]
    DI = CB * W * T * 2
    FB = down_one.shape[0]
    R = step_proj.shape[0]
    N = decay_log.shape[1]
    NR = state_proj.shape[1]
    width = CB * 2 * T
    heads = H // W * HD
    most = min(WIN, total // 2)
    hops = -(-(most - 1) // CH)

    par = jnp.concatenate(
        [
            state_proj, step_proj.T, decay_log, conv_weight.T,
            conv_bias[:, None], step_bias[:, None], skip_gain[:, None],
        ],
        axis=1,
    )
    used = par.shape[1]
    par = jnp.pad(par, ((0, 0), (0, 256 - used)))
    win_out = columns_out(in_proj, norm_mixer, 2, T, 2 * CB)
    seg8 = jnp.broadcast_to(segment_ids, (8, B))
    x0 = inputs[0].astype(F32)

    gu1_out = columns_out(gate_up_one, norm_ffn_one, 2, T, 2 * FB)
    qkv_out = columns_out(qkv_proj, norm_attn, 3, 1, heads)
    gu2_out = columns_out(gate_up_two, norm_ffn_two, 2, T, 2 * FB)
    nh1_ext, seg_all, par_all, w_in, gu1_mine, qkv_mine, gu2_mine = first_call(
        T, inputs[0], seg8, par, win_out, (gu1_out, qkv_out, gu2_out)
    )
    w_in = w_in.reshape(D, -1)
    devices = 2 * W * T
    pairs = []
    for d in range(devices):
        rest = d % (2 * T)
        pairs.append((d, (rest // 2) * 2 * W + (d // (2 * T)) * 2 + rest % 2))
    ao_mine = lax.ppermute(attn_out, ("t", "p", "c"), pairs)
    w_mix = gather_tc(mixer_out)
    w_gu1 = gather_tc(gu1_mine)
    w_qkv = gather_tc(qkv_mine)
    w_gu2 = gather_tc(gu2_mine)

    seg = seg_all[:, 0, :].reshape(total)
    pos = t * CH + jnp.arange(CH, dtype=jnp.int32)
    padded = jnp.pad(seg, (max(hops * CH, HALO), 0), constant_values=-1)
    lead = max(hops * CH, HALO)
    near = lax.dynamic_slice(padded, (t * CH + lead - HALO,), (CH + HALO,))
    own_seg = near[HALO:]
    conv_mask = jnp.stack(
        [
            (near[HALO - 3 + j : HALO - 3 + j + CH] == own_seg) & ((pos - 3 + j) // seq_len == pos // seq_len)
            & (pos - 3 + j >= 0)
            for j in range(4)
        ]
        + [jnp.zeros((CH,), jnp.bool_)] * 4,
        axis=1,
    ).astype(F32)
    starts = (pos % seq_len == 0) | (near[HALO - 1 : HALO - 1 + CH] != own_seg)
    first = jnp.where(starts, BIG, 0.0).astype(F32)
    alive = jnp.where(jnp.any(starts), 0.0, 1.0).astype(F32)
    NK = (hops + 1) * CH
    key_seg = lax.dynamic_slice(padded, (t * CH + lead - hops * CH,), (NK,))
    key_pos = t * CH - hops * CH + jnp.arange(NK, dtype=jnp.int32)
    away = pos[:, None] - key_pos[None, :]
    allowed = (
        (key_pos[None, :] >= 0) & (away >= 0) & (away < WIN) & (key_seg[None, :] == own_seg[:, None])
        & (key_pos[None, :] // seq_len == (pos // seq_len)[:, None])
    )
    bias = jnp.where(allowed, 0.0, NEG).astype(BF)
    half = HD // 2
    inverse = jnp.exp(jnp.arange(half, dtype=F32) * (-math.log(10000.0) * 2.0 / HD))
    angles = (pos % seq_len).astype(F32)[:, None] * inverse[None, :]
    cos_half, sin_half = jnp.cos(angles), jnp.sin(angles)
    cosine = jnp.concatenate([cos_half, cos_half], axis=1)
    sine = jnp.concatenate([-sin_half, sin_half], axis=1)

    par_all = par_all.reshape(width, 256)
    w_state = par_all[:, :NR]
    w_step = par_all[:, NR : NR + R].T
    side = par_all[:, NR + R : used].astype(F32).T
    a2 = -jnp.exp(side[:N]) * LOG2E
    taps = jnp.pad(side[N : N + 5], ((0, 3), (0, 0)))
    step_row = side[N + 5 : N + 6]
    skip_row = side[N + 6 : N + 7]

    xz = nn(nh1_ext, w_in)
    nh1 = nh1_ext[HALO:]
    u, u_low, part = conv_call(xz, conv_mask, taps, w_state)
    pr = plane_sum(3, part)
    dt_low = pr[:, :R].astype(BF)
    pre = nn(dt_low, w_step) + step_row
    delta = jax.nn.softplus(pre)

    def replicated(block):
        return jnp.broadcast_to(block[:, :, None], (CH, N, 128)).reshape(CH * N, 128)

    brep = replicated(pr[:, R : R + N])
    crep = replicated(pr[:, R + N :])
    sum_delta = jnp.sum(delta, axis=0, keepdims=True)

    def packed(state):
        return jnp.concatenate(
            [state, sum_delta, jnp.full((1, width), alive, F32), jnp.zeros((6, width), F32)], axis=0
        )

    end = scan_one(delta, u, a2, brep, first)
    h_in = chain(4, T, False, packed(end), a2)
    y_scan, marks = scan_two(delta, u, a2, brep, crep, first, h_in)
    y = y_scan + skip_row * u
    zg = xz[HALO:, width:]
    gate_s = jax.nn.sigmoid(zg)
    gated = (y * zg * gate_s).astype(BF)
    x1, nh2, w_d1 = turn(5, nn(gated, w_mix).astype(BF), x0, T=T, fetch=down_one)
    w_d1 = w_d1.reshape(-1, D)

    a_one = nn(nh2, w_gu1)
    h_one = swiglu(a_one).astype(BF)
    x2, nh3, w_ao = turn(6, nn(h_one, w_d1).astype(BF), x1, T=T, fetch=ao_mine)
    w_ao = w_ao.reshape(-1, D)

    qkv = nn(nh3, w_qkv)
    q, k_all, v_all, gl4 = keys_call(7, T, hops, qkv, cosine, sine, cotangent[0])
    o, lse = attend(q, k_all, v_all, bias)
    x3, nh4, w_d2 = turn(8, nn(o, w_ao).astype(BF), x2, T=T, fetch=down_two)
    w_d2 = w_d2.reshape(-1, D)

    a_two = nn(nh4, w_gu2)
    h_two = swiglu(a_two).astype(BF)
    (final,) = turn(9, nn(h_two, w_d2).astype(BF), x3, gather=False, dtype=BF)

    g4 = cotangent[0].astype(F32)
    dw_d2 = tn(h_two, gl4).astype(BF)
    da_two = swiglu_back(a_two, nt(gl4, w_d2))
    part, dw_gu2 = together(nt(da_two, w_gu2).astype(BF), tn(nh4, da_two).astype(BF))
    g3, gl3, grad_d2 = turn(10, part, x3, g4, T=T, give=dw_d2)
    raw_gu2 = scatter_tc(dw_gu2)

    do, dw_ao = together(nt(gl3, w_ao).astype(BF), tn(o, gl3).astype(BF))
    dq, dk, dv = attend_back(q, k_all, v_all, bias, lse, do)
    dq, final = together(dq, final)
    dqkv = keys_back_call(11, T, hops, dq, dk, dv, cosine, sine)
    part, dw_qkv = together(nt(dqkv, w_qkv).astype(BF), tn(nh3, dqkv).astype(BF))
    raw_qkv = scatter_tc(dw_qkv)
    part, raw_gu2 = together(part, raw_gu2)
    g2, gl2, raw_ao = turn(12, part, x2, g3, T=T, give=dw_ao)

    da_one, dw_d1 = together(swiglu_back(a_one, nt(gl2, w_d1)), tn(h_one, gl2).astype(BF))
    part, dw_gu1 = together(nt(da_one, w_gu1).astype(BF), tn(nh2, da_one).astype(BF))
    raw_gu1 = scatter_tc(dw_gu1)
    g1, gl1, grad_d1 = turn(13, part, x1, g2, T=T, give=dw_d1)
    gl1, raw_qkv = together(gl1, raw_qkv)

    dgate = nt(gl1, w_mix)
    dy = dgate * zg * gate_s
    dz_low = (dgate * y * gate_s * (1.0 + zg * (1.0 - gate_s))).astype(BF)
    dy, dw_mix, dw_z = together(dy, tn(gated, gl1).astype(BF), tn(nh1, dz_low).astype(BF))
    grad_mix = scatter_tc(dw_mix)
    raw_z = scatter_tc(dw_z)
    begin = scan_three(delta, dy, a2, crep, first)
    g_in = chain(14, T, True, packed(begin), a2)
    ddelta, du_scan, db, dc_mat, ga = scan_four(
        delta, u, dy, skip_row, a2, brep, crep, first, marks, g_in
    )
    dpre = ddelta * jax.nn.sigmoid(pre)
    dpre_low = dpre.astype(BF)
    part_back = jnp.concatenate(
        [
            nt(dpre_low, w_step),
            jnp.sum(db, axis=1).reshape(CH, N),
            jnp.sum(dc_mat, axis=1).reshape(CH, N),
        ],
        axis=1,
    )
    part_back, raw_gu1 = together(part_back, raw_gu1)
    dpr_low = plane_sum(15, part_back).astype(BF)
    du = du_scan + nt(dpr_low, w_state)
    dxs_ext, conv_grads = conv_back_call(xz, conv_mask, taps, du)
    rim = rim_back(16, T, dxs_ext[8:16])
    dxs_low = jnp.concatenate(
        [dxs_ext[HALO : HALO + CH - 8], dxs_ext[HALO + CH - 8 :] + rim], axis=0
    ).astype(BF)
    dxz = jnp.concatenate([dxs_low, dz_low], axis=1)
    dxz, dw_x, grad_mix = together(dxz, tn(nh1, dxs_low).astype(BF), grad_mix)
    raw_x = scatter_tc(dw_x)
    (grad_x,) = turn(17, nt(dxz, w_in).astype(BF), x0, g1, gather=False)

    small = jnp.concatenate(
        [
            tn(u_low, dpr_low),
            tn(dpre_low, dt_low),
            ga.T,
            conv_grads[:5].T,
            jnp.sum(dpre, axis=0)[:, None],
            jnp.sum(dy * u, axis=0)[:, None],
        ],
        axis=1,
    )
    small = jnp.pad(small, ((0, 0), (0, 256 - used))).astype(BF).reshape(2 * T, CB, 256)
    small, raw_z = together(small, raw_z)
    small = small_sum(18, T, small)

    def blocks(x):
        return x.reshape(W, x.shape[0] // W, x.shape[1])

    gu2_b, qkv_b, gu1_b, z_b = spread_call(
        19, True, (blocks(raw_gu2), blocks(raw_qkv), blocks(raw_gu1), blocks(raw_z))
    )
    (x_b,) = spread_call(20, True, (blocks(raw_x),))
    in_b = jnp.concatenate([x_b, z_b], axis=2)
    grad_ao = lax.ppermute(raw_ao.astype(BF), ("t", "p", "c"), [(b, a) for a, b in pairs]).astype(F32)

    def finished(blocks_in, weight, gain, groups, groups_t, cols):
        raw = columns_back(blocks_in, groups, groups_t, cols)
        return (
            jnp.sum(weight.astype(F32) * raw, axis=1),
            raw * gain.astype(F32)[:, None],
        )

    grad_n1, grad_in = finished(in_b, in_proj, norm_mixer, 2, T, 2 * CB)
    grad_n2, grad_gu1 = finished(gu1_b, gate_up_one, norm_ffn_one, 2, T, 2 * FB)
    grad_n3, grad_qkv = finished(qkv_b, qkv_proj, norm_attn, 3, 1, heads)
    grad_n4, grad_gu2 = finished(gu2_b, gate_up_two, norm_ffn_two, 2, T, 2 * FB)
    at = NR + R + N
    return (
        final[None],
        grad_x[None],
        grad_n1,
        grad_in,
        small[:, at : at + 4].T,
        small[:, at + 4],
        small[:, :NR],
        small[:, NR : NR + R].T,
        small[:, at + 5],
        small[:, NR + R : at],
        small[:, at + 6],
        grad_mix.astype(F32),
        grad_n2,
        grad_gu1,
        grad_d1,
        grad_n3,
        grad_qkv,
        grad_ao,
        grad_n4,
        grad_gu2,
        grad_d2,
    )


def solution(mesh):
    chunks = mesh.shape["seq"] // W
    view = Mesh(mesh.devices.reshape(chunks, W, mesh.shape["fsdp"]), ("t", "p", "c"))
    every = ("t", "p", "c")
    tokens = P("c", ("t", "p"), None)
    vector, rows, cols = P(every), P(every, None), P(None, every)
    placed = (
        tokens, P("c", ("t", "p")), tokens,
        vector, rows, cols, vector, rows, cols, vector, rows, vector, rows,
        vector, rows, rows, vector, rows, rows, vector, rows, rows,
    )
    return jax.shard_map(
        local,
        mesh=view,
        in_specs=placed,
        out_specs=(tokens, tokens) + placed[3:],
        check_vma=False,
    )
```

```python
import functools
import math

import jax
import jax.numpy as jnp
from jax import lax
from jax.experimental import pallas as pl
from jax.experimental.pallas import tpu as pltpu
from jax.sharding import Mesh
from jax.sharding import PartitionSpec as P

W = 4
H = 12
HD = 128
WIN = 2048
SEQ_MAX = 8192
EPS = 1e-05
NEG = -1e30
BIG = 1e30
LOG2E = 1.4426950408889634
BF = jnp.bfloat16
F32 = jnp.float32
MESH = pl.DeviceIdType.MESH
HALO = 16
SUB = 64
MIB = 1 << 20


def vmem():
    return pl.BlockSpec(memory_space=pltpu.VMEM)


def hbm():
    return pl.BlockSpec(memory_space=pl.ANY)


def smem():
    return pl.BlockSpec(memory_space=pltpu.SMEM)


def here():
    return lax.axis_index("t"), lax.axis_index("p"), lax.axis_index("c")


def greet(device):
    pl.semaphore_signal(
        pltpu.get_barrier_semaphore(), inc=1, device_id=device, device_id_type=MESH
    )


def arrive(count):
    pl.semaphore_wait(pltpu.get_barrier_semaphore(), count)


def arrive_some(count):
    @pl.when(count > 0)
    def _():
        arrive(count)


def remote(src, dst, send, recv, device):
    return pltpu.make_async_remote_copy(
        src_ref=src,
        dst_ref=dst,
        send_sem=send,
        recv_sem=recv,
        device_id=device,
        device_id_type=MESH,
    )


def flip(p, d):
    return lax.bitwise_xor(p, d)


def dma(*shape):
    return pltpu.SemaphoreType.DMA(shape)


def talk(cid, limit=40):
    return pltpu.CompilerParams(
        collective_id=cid, has_side_effects=True, vmem_limit_bytes=limit * MIB
    )


def alone(limit=56):
    return pltpu.CompilerParams(vmem_limit_bytes=limit * MIB)


def out(shape, dtype=F32):
    return jax.ShapeDtypeStruct(shape, dtype)


def unit(x):
    return x * lax.rsqrt(jnp.mean(x * x, axis=-1, keepdims=True) + EPS)


def column_blocks(w, gain, chunk, blocks):
    groups = w.shape[1] // (W * chunk)
    for q in range(W):
        pieces = [w[:, (k * W + q) * chunk : (k * W + q + 1) * chunk] for k in range(groups)]
        value = jnp.concatenate(pieces, axis=1) if groups > 1 else pieces[0]
        blocks[q] = (value.astype(F32) * gain).astype(BF)


def first_body(T, chunks, x, seg, state, rows_in, log_in, gains, *refs):
    n = len(chunks) - 1
    weights, refs = refs[: n + 1], refs[n + 1 :]
    nh, seg_out, par_out, w_in = refs[:4]
    dsts, refs = refs[4 : 4 + n], refs[4 + n :]
    win, srcs, par, refs = refs[0], refs[1 : n + 1], refs[n + 1], refs[n + 2 :]
    (nbuf, zbuf, s_n, r_n, s_h, r_h, s_s, r_s, s_p, r_p, s_w, r_w, s_z, r_z, s_c, r_c, s_l, s_o, r_o) = refs
    t, p, c = here()
    B = x.shape[0]
    count = 0
    for dt in range(T):
        tt = lax.rem(t + dt, T)
        for dp in range(W):
            pp = flip(p, dp)
            if dt or dp:
                greet((tt, pp, c))
                count += 1
            if dt == 0 or dp == 0:
                greet((tt, pp, 1 - c))
                count += 1
    column_blocks(weights[0], gains[:, 0:1], chunks[0], win)
    arrive(count)
    half = lax.div(p, 2)
    slot = lax.rem(p, 2) * 2 + c
    me = t * 2 + c

    def block(src, dst, send, recv, q):
        return remote(src.at[q], dst.at[slot], send.at[q], recv.at[slot], (t, q, half))

    def kept(src, dst, send, q):
        return pltpu.make_async_copy(src.at[q], dst.at[slot], send.at[q])

    def exchange(src, dst, send, recv):
        for q in range(W):
            mine = (p == q) & (half == c)

            @pl.when(jnp.logical_not(mine))
            def _():
                block(src, dst, send, recv, q).start()

            @pl.when(mine)
            def _():
                kept(src, dst, send, q).start()

    def exchanged(src, dst, send, recv, j):
        own = (half == c) & (slot == j)

        @pl.when(jnp.logical_not(own))
        def _():
            remote(src.at[0], dst.at[j], send.at[0], recv.at[j], (t, 0, half)).wait_recv()

    def sent(src, dst, send, recv):
        for q in range(W):
            mine = (p == q) & (half == c)

            @pl.when(jnp.logical_not(mine))
            def _():
                block(src, dst, send, recv, q).wait_send()

    landing = w_in.at[t * 2 + half]
    exchange(win, landing, s_w, r_w)
    nbuf[...] = unit(x[...].astype(F32)).astype(BF)
    zbuf[...] = jnp.zeros_like(zbuf)
    size = rows_in.shape[1]
    eye = (
        lax.broadcasted_iota(jnp.int32, (size, size), 0)
        == lax.broadcasted_iota(jnp.int32, (size, size), 1)
    ).astype(BF)
    lines = nt(eye, rows_in[...]).astype(BF)
    wide_at = state.shape[1]
    par[:, 0:wide_at] = state[...]
    par[:, wide_at:] = jnp.concatenate(
        [lines, log_in[...], jnp.zeros((size, 256 - wide_at - lines.shape[1] - log_in.shape[1]), BF)],
        axis=1,
    )
    rows = pl.ds(pl.multiple_of(HALO + p * B, HALO), B)
    copies = []
    for dt in range(T):
        for dc in range(2):
            if dt or dc:
                copies.append(
                    remote(
                        par, par_out.at[me], s_p.at[dt, dc], r_p.at[dt, dc],
                        (lax.rem(t + dt, T), p, flip(c, dc)),
                    )
                )
    for d in range(1, W):
        copies.append(remote(nbuf, nh.at[rows], s_n.at[d], r_n.at[d], (t, flip(p, d), c)))
    for dt in range(T):
        for dp in range(W):
            if dt or dp:
                copies.append(
                    remote(
                        seg, seg_out.at[t * W + p], s_s.at[dt, dp], r_s.at[dt, dp],
                        (lax.rem(t + dt, T), flip(p, dp), c),
                    )
                )
    copies += [
        pltpu.make_async_copy(nbuf, nh.at[rows], s_l.at[0]),
        pltpu.make_async_copy(par, par_out.at[me], s_l.at[1]),
        pltpu.make_async_copy(seg, seg_out.at[t * W + p], s_l.at[2]),
    ]
    for copy in copies:
        copy.start()
    last = (p == W - 1) & (t < T - 1)
    tail = nbuf.at[pl.ds(B - HALO, HALO)]
    head = nh.at[pl.ds(0, HALO)]

    def rim(q):
        return remote(tail, head, s_h.at[q], r_h, (lax.rem(t + 1, T), q, c))

    @pl.when(last)
    def _():
        for q in range(W):
            rim(q).start()

    @pl.when(t == 0)
    def _():
        clear = pltpu.make_async_copy(zbuf, head, s_l.at[3])
        clear.start()
        clear.wait()

    for i in range(n):
        column_blocks(weights[i + 1], gains[:, i + 1 : i + 2], chunks[i + 1], srcs[i])
        exchange(srcs[i], dsts[i], s_o.at[i], r_o.at[i])

    def on(way, d, j):
        step = 1 - 2 * way
        source = lax.rem(t - step * d + T, T) * 2 + c
        part = w_in.at[source, j]
        return remote(
            part, part, s_z.at[way, d, j], r_z.at[way, d + 1, j], (lax.rem(t + step + T, T), p, c)
        )

    def came(way, d, j):
        step = 1 - 2 * way
        part = w_in.at[lax.rem(t - step * d + T, T) * 2 + c, j]
        return remote(part, part, s_z.at[way, d, j], r_z.at[way, d, j], (lax.rem(t + step + T, T), p, c))

    def across(way, d, j):
        step = 1 - 2 * way
        part = w_in.at[lax.rem(t - step * d + T, T) * 2 + c, j]
        return remote(part, part, s_c.at[way, d, j], r_c.at[way, d, j], (t, p, 1 - c))

    def crossed(way, d, j):
        step = 1 - 2 * way
        part = w_in.at[lax.rem(t - step * d + T, T) * 2 + 1 - c, j]
        return remote(part, part, s_c.at[way, d, j], r_c.at[way, d, j], (t, p, 1 - c))

    def goes(way, d):
        if way == 0:
            return (t >= d) & (t < T - 1)
        return (t + d < T) & (t > 0)

    def arrives(way, d):
        return (t >= d) if way == 0 else (t + d < T)

    for j in range(W):
        mine = (half == c) & (slot == j)

        @pl.when(mine)
        def _():
            for q in range(W):

                @pl.when(p == q)
                def _():
                    kept(win, landing, s_w, q).wait()

        exchanged(win, w_in.at[me], s_w, r_w, j)
        across(0, 0, j).start()
        for way in range(2):

            @pl.when(goes(way, 0))
            def _():
                on(way, 0, j).start()

    for d in range(1, T):
        for j in range(W):
            for way in range(2):

                @pl.when(arrives(way, d))
                def _():
                    came(way, d, j).wait_recv()
                    across(way, d, j).start()

                @pl.when(goes(way, d))
                def _():
                    on(way, d, j).start()

    for copy in copies:
        copy.wait()

    @pl.when(last)
    def _():
        for q in range(W):
            rim(q).wait_send()

    @pl.when(t > 0)
    def _():
        rim(0).wait_recv()

    sent(win, landing, s_w, r_w)
    for i in range(n):
        sent(srcs[i], dsts[i], s_o.at[i], r_o.at[i])
        for q in range(W):
            mine = (p == q) & (half == c)

            @pl.when(mine)
            def _():
                kept(srcs[i], dsts[i], s_o.at[i], q).wait()

        for j in range(W):
            exchanged(srcs[i], dsts[i], s_o.at[i], r_o.at[i], j)
    for d in range(T):
        for j in range(W):
            for way in range(2):
                if d or way == 0:

                    @pl.when(arrives(way, d))
                    def _():
                        across(way, d, j).wait_send()
                        crossed(way, d, j).wait_recv()

                @pl.when(goes(way, d))
                def _():
                    on(way, d, j).wait_send()


def first_call(T, x, seg, state, rows_in, log_in, gains, weights, chunks):
    B, D = x.shape
    n = len(weights) - 1
    blocks = [(W, w.shape[0], w.shape[1] // W) for w in weights]
    return pl.pallas_call(
        functools.partial(first_body, T, chunks),
        out_shape=(
            out((HALO + W * B, D), BF),
            out((W * T,) + seg.shape, jnp.int32),
            out((2 * T, state.shape[0], 256), BF),
            out((2 * T,) + blocks[0], BF),
        )
        + tuple(out(b, BF) for b in blocks[1:]),
        in_specs=[vmem(), hbm()] + [vmem()] * (5 + n),
        out_specs=(hbm(),) * (4 + n),
        scratch_shapes=[pltpu.VMEM(b, BF) for b in blocks]
        + [
            pltpu.VMEM((state.shape[0], 256), BF),
            pltpu.VMEM((B, D), BF),
            pltpu.VMEM((HALO, D), BF),
            dma(W), dma(W), dma(W), pltpu.SemaphoreType.DMA,
            dma(T, W), dma(T, W), dma(T, 2), dma(T, 2), dma(W), dma(W),
            dma(2, T, W), dma(2, T + 1, W), dma(2, T, W), dma(2, T, W), dma(4),
            dma(n, W), dma(n, W),
        ],
        compiler_params=talk(0),
        name="first",
    )(x, seg, state, rows_in, log_in, gains, *weights)


class Job:
    def __init__(self, build, inputs, in_specs, shapes, specs, scratch):
        self.build, self.inputs, self.in_specs = build, tuple(inputs), list(in_specs)
        self.shapes, self.specs, self.scratch = tuple(shapes), tuple(specs), list(scratch)


def take(refs, count):
    head = refs[:count]
    del refs[:count]
    return head


def started(jobs, ins, outs, scratch):
    made = []
    for job in jobs:
        made.append(
            job.build(
                take(ins, len(job.inputs)), take(outs, len(job.shapes)), take(scratch, len(job.scratch))
            )
        )
    return made


def spread_build(n, back):
    def build(srcs, dsts, sems):
        s_w, r_w = sems
        t, p, c = here()
        half = lax.div(p, 2)
        pair = lax.rem(p, 2) * 2 + c
        both = half == c

        def there(q):
            if back:
                return (t, c * 2 + q // 2, jnp.int32(q % 2))
            return (t, jnp.int32(q), half)

        def comes(j):
            if back:
                return (t, jnp.int32(j), half)
            return (t, c * 2 + j // 2, jnp.int32(j % 2))

        slot = p if back else pair

        def own(q):
            return both & ((pair == q) if back else (p == q))

        def from_me(q):
            return both & ((p == q) if back else (pair == q))

        def away(a, q):
            return remote(
                srcs[a].at[q], dsts[a].at[slot], s_w.at[a, q], r_w.at[a, slot], there(q)
            )

        def kept(a, q):
            return pltpu.make_async_copy(srcs[a].at[q], dsts[a].at[slot], s_w.at[a, q])

        for q in range(W):
            source = comes(q)

            @pl.when(jnp.logical_not(from_me(q)))
            def _():
                greet(source)

        def begin():
            for a in range(n):
                for q in range(W):

                    @pl.when(jnp.logical_not(own(q)))
                    def _():
                        away(a, q).start()

                    @pl.when(own(q))
                    def _():
                        kept(a, q).start()

        def end():
            for a in range(n):
                for q in range(W):

                    @pl.when(jnp.logical_not(own(q)))
                    def _():
                        away(a, q).wait_send()

                    @pl.when(own(q))
                    def _():
                        kept(a, q).wait()

                    @pl.when(jnp.logical_not(from_me(q)))
                    def _():
                        remote(
                            srcs[a].at[q], dsts[a].at[q], s_w.at[a, q], r_w.at[a, q], there(q)
                        ).wait_recv()

        return W - both.astype(jnp.int32), begin, end

    return build


def spread_job(back, arrays):
    n = len(arrays)
    return Job(
        spread_build(n, back), arrays, [hbm()] * n,
        [out(a.shape, a.dtype) for a in arrays], [hbm()] * n, [dma(n, W), dma(n, W)],
    )


def jobs_body(counts, jobs, *refs):
    refs = list(refs)
    ins, outs = take(refs, counts[0]), take(refs, counts[1])
    made = started(jobs, ins, outs, refs)
    arrive(sum(m[0] for m in made))
    for m in made:
        m[1]()
    for m in made:
        m[2]()


def run_jobs(cid, *jobs):
    inputs = sum((j.inputs for j in jobs), ())
    shapes = sum((j.shapes for j in jobs), ())
    return pl.pallas_call(
        functools.partial(jobs_body, (len(inputs), len(shapes)), jobs),
        out_shape=shapes,
        in_specs=sum((j.in_specs for j in jobs), []),
        out_specs=sum((j.specs for j in jobs), ()),
        scratch_shapes=sum((j.scratch for j in jobs), []),
        compiler_params=talk(cid),
        name="jobs%d" % cid,
    )(*inputs)


def plane_sum_body(x, o, sb, recv, ss, rs):
    t, p, c = here()
    for d in range(1, W):
        greet((t, flip(p, d), c))
    sb[...] = x[...].astype(BF)
    arrive(W - 1)
    copies = [
        remote(sb, recv.at[d - 1], ss.at[d - 1], rs.at[d - 1], (t, flip(p, d), c))
        for d in range(1, W)
    ]
    for copy in copies:
        copy.start()
    for copy in copies:
        copy.wait()
    total = x[...]
    for d in range(W - 1):
        total = total + recv[d].astype(F32)
    o[...] = total


def plane_sum(cid, x):
    return pl.pallas_call(
        plane_sum_body,
        out_shape=out(x.shape),
        in_specs=[vmem()],
        out_specs=vmem(),
        scratch_shapes=[
            pltpu.VMEM(x.shape, BF),
            pltpu.VMEM((W - 1,) + x.shape, BF),
            dma(W - 1),
            dma(W - 1),
        ],
        compiler_params=talk(cid),
        name="plane_sum%d" % cid,
    )(x)


def gather_job(T, piece):
    def build(ins, outs, sems):
        (src,), (dst,) = ins, outs
        s_z, r_z, s_c, r_c, s_l = sems
        t, p, c = here()

        def part(dt, core):
            return dst.at[lax.rem(t - dt + T, T) * 2 + core]

        def out_to(dt):
            return remote(src, part(0, c), s_z.at[dt], r_z.at[dt], (lax.rem(t + dt, T), p, c))

        def across(dt):
            return remote(
                src if dt == 0 else part(dt, c), part(dt, c), s_c.at[dt], r_c.at[dt], (t, p, 1 - c)
            )

        keep = pltpu.make_async_copy(src, part(0, c), s_l)
        for dt in range(1, T):
            greet((lax.rem(t + dt, T), p, c))
        greet((t, p, 1 - c))

        def begin():
            for dt in range(1, T):
                out_to(dt).start()
            across(0).start()
            keep.start()

        def end():
            for dt in range(1, T):
                out_to(dt).wait_recv()
                across(dt).start()
            keep.wait()
            for dt in range(T):
                across(dt).wait_send()
                other = part(dt, 1 - c)
                remote(other, other, s_c.at[dt], r_c.at[dt], (t, p, 1 - c)).wait_recv()
            for dt in range(1, T):
                out_to(dt).wait_send()

        return T, begin, end

    return Job(
        build, [piece], [hbm()], [out((2 * T,) + piece.shape, BF)], [hbm()],
        [dma(T), dma(T), dma(T), dma(T), pltpu.SemaphoreType.DMA],
    )


def scatter_job(T, grad):
    grad = grad.reshape(2 * T, -1, grad.shape[-1])

    def build(ins, outs, scratch):
        (src,), (dst,) = ins, outs
        mine, other, recv, s_z, r_z, s_c, r_c, s_l = scratch
        t, p, c = here()

        def at(dt):
            return lax.rem(t + dt, T)

        def across(dt):
            return remote(
                src.at[at(dt) * 2 + 1 - c], other.at[dt], s_c.at[dt], r_c.at[dt], (t, p, 1 - c)
            )

        def load(dt):
            return pltpu.make_async_copy(src.at[at(dt) * 2 + c], mine.at[dt], s_l.at[dt])

        def out_to(dt):
            return remote(mine.at[dt], recv.at[dt - 1], s_z.at[dt], r_z.at[dt], (at(dt), p, c))

        order = list(range(1, T)) + [0]
        for dt in range(1, T):
            greet((at(dt), p, c))
        greet((t, p, 1 - c))

        def begin():
            for dt in order:
                across(dt).start()
                load(dt).start()
            for dt in order[:-1]:
                across(dt).wait_recv()
                load(dt).wait()
                mine[dt] = (mine[dt].astype(F32) + other[dt].astype(F32)).astype(BF)
                out_to(dt).start()

        def end():
            across(0).wait_recv()
            load(0).wait()
            total = mine[0].astype(F32) + other[0].astype(F32)
            for dt in range(1, T):
                out_to(dt).wait_recv()
                total = total + recv[dt - 1].astype(F32)
            dst[...] = total
            for dt in range(T):
                across(dt).wait_send()
            for dt in range(1, T):
                out_to(dt).wait_send()

        return T, begin, end

    shape = grad.shape[1:]
    return Job(
        build, [grad], [hbm()], [out(shape)], [vmem()],
        [
            pltpu.VMEM((T,) + shape, BF),
            pltpu.VMEM((T,) + shape, BF),
            pltpu.VMEM((T - 1,) + shape, BF),
            dma(T), dma(T), dma(T), dma(T), dma(T),
        ],
    )


def small_job(T, x):
    peers = [(dt, dc) for dt in range(T) for dc in range(2) if dt or dc]
    n = len(peers)

    def build(ins, outs, scratch):
        (src,), (dst,) = ins, outs
        recv, ss, rs = scratch
        t, p, c = here()

        def copy(i):
            dt, dc = peers[i]
            tt, cc = lax.rem(t + dt, T), flip(c, dc)
            return remote(src.at[tt * 2 + cc], recv.at[i], ss.at[i], rs.at[i], (tt, p, cc))

        for dt, dc in peers:
            greet((lax.rem(t + dt, T), p, flip(c, dc)))

        def begin():
            for i in range(n):
                copy(i).start()

        def end():
            total = src[t * 2 + c].astype(F32)
            for i in range(n):
                copy(i).wait()
                total = total + recv[i].astype(F32)
            dst[...] = total

        return n, begin, end

    return Job(
        build, [x], [vmem()], [out(x.shape[1:])], [vmem()],
        [pltpu.VMEM((n,) + x.shape[1:], x.dtype), dma(n), dma(n)],
    )


def sum_job(part, x, dtype):
    B, D = x.shape

    def build(ins, outs, scratch):
        src, base = ins
        (o,) = outs
        own, recv, ss, rs, ls = scratch
        t, p, c = here()

        def copy(d):
            q = flip(p, d)
            return remote(
                src.at[pl.ds(pl.multiple_of(q * B, B), B)], recv.at[d - 1],
                ss.at[d - 1], rs.at[d - 1], (t, q, c),
            )

        local = pltpu.make_async_copy(src.at[pl.ds(pl.multiple_of(p * B, B), B)], own, ls)
        for d in range(1, W):
            greet((t, flip(p, d), c))

        def begin():
            for d in range(1, W):
                copy(d).start()
            local.start()

        def end():
            local.wait()
            total = base[...] + own[...].astype(F32)
            for d in range(1, W):
                copy(d).wait()
                total = total + recv[d - 1].astype(F32)
            o[...] = total.astype(o.dtype)

        return W - 1, begin, end

    return Job(
        build, [part, x], [hbm(), vmem()], [out((B, D), dtype)], [vmem()],
        [
            pltpu.VMEM((B, D), BF), pltpu.VMEM((W - 1, B, D), BF),
            dma(W - 1), dma(W - 1), pltpu.SemaphoreType.DMA,
        ],
    )


def turn_body(back, gather, parts, jobs, counts, *refs):
    refs = list(refs)
    ins, outs = take(refs, counts[0]), take(refs, counts[1])
    part, x = take(ins, 2)
    g = take(ins, 1)[0] if back else None
    o = take(outs, 1)[0]
    gath = take(outs, 1)[0] if gather else None
    own, recv, sbuf, ss, rs, ls, ss2, rs2, ls2 = take(refs, 9)
    t, p, c = here()
    B = x.shape[0]
    rows = B // parts
    for d in range(1, W):
        greet((t, flip(p, d), c))
    made = started(jobs, ins, outs, refs)
    local = pltpu.make_async_copy(part.at[pl.ds(pl.multiple_of(p * B, B), B)], own, ls)
    local.start()
    arrive(sum((m[0] for m in made), W - 1))
    first = {}
    for k in range(parts):
        for d in range(1, W):
            q = flip(p, d)
            first[k, d] = remote(
                part.at[pl.ds(pl.multiple_of(q * B + k * rows, rows), rows)],
                recv.at[d - 1, pl.ds(k * rows, rows)],
                ss.at[d - 1, k],
                rs.at[d - 1, k],
                (t, q, c),
            )
            first[k, d].start()
    for m in made:
        m[1]()
    local.wait()
    later = []
    for k in range(parts):
        for d in range(1, W):
            first[k, d].wait_recv()
        cut = pl.ds(k * rows, rows)
        total = own[cut, :].astype(F32)
        for d in range(W - 1):
            total = total + recv[d, cut, :].astype(F32)
        value = x[cut, :]
        if back:
            r = lax.rsqrt(jnp.mean(value * value, axis=-1, keepdims=True) + EPS)
            hat = value * r
            new = g[cut, :] + r * (total - hat * jnp.mean(total * hat, axis=-1, keepdims=True))
        else:
            new = value + total
        o[cut, :] = new.astype(o.dtype)
        if gather:
            sbuf[cut, :] = (new if back else unit(new)).astype(BF)
            place = gath.at[pl.ds(pl.multiple_of(p * B + k * rows, rows), rows)]
            for d in range(1, W):
                later.append(
                    remote(sbuf.at[cut], place, ss2.at[d - 1, k], rs2.at[d - 1, k], (t, flip(p, d), c))
                )
            later.append(pltpu.make_async_copy(sbuf.at[cut], place, ls2.at[k]))
            for copy in later[-W:]:
                copy.start()
    for m in made:
        m[2]()
    for copy in first.values():
        copy.wait_send()
    for copy in later:
        copy.wait()


def turn(cid, part, x, g=None, gather=True, dtype=F32, parts=2, jobs=()):
    B, D = x.shape
    back = g is not None
    args = (part, x) + ((g,) if back else ())
    in_specs = [hbm()] + [vmem()] * (len(args) - 1)
    shapes, specs = (out((B, D), dtype),), (vmem(),)
    if gather:
        shapes += (out((W * B, D), BF),)
        specs += (hbm(),)
    scratch = [
        pltpu.VMEM((B, D), BF),
        pltpu.VMEM((W - 1, B, D), BF),
        pltpu.VMEM((B, D), BF),
        dma(W - 1, parts), dma(W - 1, parts), pltpu.SemaphoreType.DMA,
        dma(W - 1, parts), dma(W - 1, parts), dma(parts),
    ]
    for job in jobs:
        args += job.inputs
        in_specs += job.in_specs
        shapes += job.shapes
        specs += job.specs
        scratch += job.scratch
    return pl.pallas_call(
        functools.partial(turn_body, back, gather, parts, jobs, (len(args), len(shapes))),
        out_shape=shapes,
        in_specs=in_specs,
        out_specs=specs,
        scratch_shapes=scratch,
        compiler_params=talk(cid),
        name="turn%d" % cid,
    )(*args)


def chain_body(T, back, jobs, counts, *refs):
    refs = list(refs)
    ins, outs = take(refs, counts[0]), take(refs, counts[1])
    v, a2 = take(ins, 2)
    (h,) = take(outs, 1)
    recv, ss, rs = take(refs, 3)
    t, p, c = here()
    sign = -1 if back else 1
    for k in range(1, T):
        source = t - sign * k

        @pl.when((source >= 0) & (source < T))
        def _():
            greet((lax.rem(source + T, T), p, c))

    made = started(jobs, ins, outs, refs)
    arrive_some(sum((m[0] for m in made), t if back else T - 1 - t))

    def send(k):
        to = lax.rem(t + sign * k + T, T)
        return remote(v, recv.at[k - 1], ss.at[k - 1], rs.at[k - 1], (to, p, c))

    for k in range(1, T):
        to = t + sign * k

        @pl.when((to >= 0) & (to < T))
        def _():
            send(k).start()

    for m in made:
        m[1]()
    h[...] = jnp.zeros_like(h)
    for k in range(T - 1, 0, -1):
        source = t - sign * k

        @pl.when((source >= 0) & (source < T))
        def _():
            send(k).wait_recv()
            decay = jnp.exp2(a2[...] * recv[k - 1, 16:17, :]) * recv[k - 1, 17:18, :]
            h[...] = recv[k - 1, 0:16, :] + decay * h[...]

    for k in range(1, T):
        to = t + sign * k

        @pl.when((to >= 0) & (to < T))
        def _():
            send(k).wait_send()

    for m in made:
        m[2]()


def chain(cid, T, back, v, a2, jobs=()):
    args, in_specs = (v, a2), [vmem(), vmem()]
    shapes, specs = (out(a2.shape),), (vmem(),)
    scratch = [pltpu.VMEM((T - 1,) + v.shape, F32), dma(T - 1), dma(T - 1)]
    for job in jobs:
        args += job.inputs
        in_specs += job.in_specs
        shapes += job.shapes
        specs += job.specs
        scratch += job.scratch
    return pl.pallas_call(
        functools.partial(chain_body, T, back, jobs, (len(args), len(shapes))),
        out_shape=shapes,
        in_specs=in_specs,
        out_specs=specs,
        scratch_shapes=scratch,
        compiler_params=talk(cid),
        name="chain%d" % cid,
    )(*args)


def rope(w, cosine, sine):
    return w * cosine + pltpu.roll(w, HD // 2, 1) * sine


def keys_body(T, hops, qkv, cosine, sine, ct, q, k_all, v_all, ct_out, ss, rs, s_g, r_g, s_l):
    t, p, c = here()
    CH = q.shape[0]
    width = q.shape[1]
    B = ct.shape[0]

    @pl.when(t > 0)
    def _():
        greet((lax.rem(t - 1 + T, T), p, c))

    for d in range(1, W):
        greet((t, flip(p, d), c))

    mine = pl.ds(hops * CH, CH)
    for h in range(width // HD):
        cols = pl.ds(h * HD, HD)
        k_all[mine, cols] = rope(
            qkv[:, pl.ds(width + h * HD, HD)], cosine[...], sine[...]
        ).astype(BF)
    v_all[mine, :] = qkv[:, pl.ds(2 * width, width)].astype(BF)

    @pl.when(t < T - 1)
    def _():
        arrive(W)

    @pl.when(t == T - 1)
    def _():
        arrive(W - 1)

    def send(a, d):
        ref = (k_all, v_all)[a]
        return remote(
            ref.at[pl.ds((hops - d + 1) * CH, CH)],
            ref.at[pl.ds((hops - d) * CH, CH)],
            ss.at[a, d - 1],
            rs.at[a, d - 1],
            (lax.rem(t + 1, T), p, c),
        )

    for d in range(1, hops + 1):
        goes = (t < T - 1) & (t >= d - 1)

        @pl.when(goes)
        def _():
            send(0, d).start()
            send(1, d).start()

        if d == 1:
            rows = ct_out.at[pl.ds(pl.multiple_of(p * B, B), B)]
            copies = [
                remote(ct, rows, s_g.at[e], r_g.at[e], (t, flip(p, e), c)) for e in range(1, W)
            ] + [pltpu.make_async_copy(ct, rows, s_l)]
            for copy in copies:
                copy.start()
            for h in range(width // HD):
                cols = pl.ds(h * HD, HD)
                q[:, cols] = rope(qkv[:, cols], cosine[...], sine[...]).astype(BF)

        @pl.when(t < d)
        def _():
            k_all[pl.ds((hops - d) * CH, CH), :] = jnp.zeros((CH, width), BF)
            v_all[pl.ds((hops - d) * CH, CH), :] = jnp.zeros((CH, width), BF)

        @pl.when(t >= d)
        def _():
            send(0, d).wait_recv()
            send(1, d).wait_recv()

    for d in range(1, hops + 1):
        goes = (t < T - 1) & (t >= d - 1)

        @pl.when(goes)
        def _():
            send(0, d).wait_send()
            send(1, d).wait_send()

    for copy in copies:
        copy.wait()


def keys_call(cid, T, hops, qkv, cosine, sine, ct):
    CH = qkv.shape[0]
    width = qkv.shape[1] // 3
    return pl.pallas_call(
        functools.partial(keys_body, T, hops),
        out_shape=(
            out((CH, width), BF),
            out(((hops + 1) * CH, width), BF),
            out(((hops + 1) * CH, width), BF),
            out((W * ct.shape[0], ct.shape[1]), BF),
        ),
        in_specs=[vmem()] * 3 + [hbm()],
        out_specs=(vmem(),) * 3 + (hbm(),),
        scratch_shapes=[
            dma(2, hops), dma(2, hops), dma(W), dma(W), pltpu.SemaphoreType.DMA,
        ],
        compiler_params=talk(cid),
        name="keys",
    )(qkv, cosine, sine, ct)


def keys_back_body(T, hops, jobs, counts, *refs):
    refs = list(refs)
    ins, outs = take(refs, counts[0]), take(refs, counts[1])
    dq, dk, dv, cosine, sine = take(ins, 5)
    (dqkv,) = take(outs, 1)
    sb, recv, ss, rs = take(refs, 4)
    t, p, c = here()
    CH = dq.shape[0]
    width = dq.shape[1]

    @pl.when(t < T - 1)
    def _():
        greet((lax.rem(t + 1, T), p, c))

    made = started(jobs, ins, outs, refs)
    extra = sum(m[0] for m in made)

    def send(a, d):
        return remote(
            sb.at[a, d - 1],
            recv.at[a, d - 1],
            ss.at[a, d - 1],
            rs.at[a, d - 1],
            (lax.rem(t - 1 + T, T), p, c),
        )

    for d in range(hops, 0, -1):
        rows = pl.ds((hops - d) * CH, CH)
        k_sum = dk[rows, :]
        v_sum = dv[rows, :]
        if d == hops:
            sb[0, d - 1] = k_sum.astype(BF)
            sb[1, d - 1] = v_sum.astype(BF)

            @pl.when(t > 0)
            def _():
                arrive(1 + extra)

            if extra:

                @pl.when(t == 0)
                def _():
                    arrive(extra)

        else:

            @pl.when((t < T - 1) & (t >= d))
            def _():
                send(0, d + 1).wait_recv()
                send(1, d + 1).wait_recv()

            @pl.when((t == T - 1) | (t < d))
            def _():
                recv[0, d] = jnp.zeros((CH, width), BF)
                recv[1, d] = jnp.zeros((CH, width), BF)

            sb[0, d - 1] = (k_sum + recv[0, d].astype(F32)).astype(BF)
            sb[1, d - 1] = (v_sum + recv[1, d].astype(F32)).astype(BF)

        @pl.when(t >= d)
        def _():
            send(0, d).start()
            send(1, d).start()

        if d == hops:
            for m in made:
                m[1]()
            for h in range(width // HD):
                cols = pl.ds(h * HD, HD)
                dqkv[:, cols] = rope(dq[:, cols], cosine[...], -sine[...]).astype(BF)

    @pl.when(t < T - 1)
    def _():
        send(0, 1).wait_recv()
        send(1, 1).wait_recv()

    @pl.when(t == T - 1)
    def _():
        recv[0, 0] = jnp.zeros((CH, width), BF)
        recv[1, 0] = jnp.zeros((CH, width), BF)

    mine = pl.ds(hops * CH, CH)
    for h in range(width // HD):
        cols = pl.ds(h * HD, HD)
        k_sum = dk[mine, cols] + recv[0, 0, :, cols].astype(F32)
        v_sum = dv[mine, cols] + recv[1, 0, :, cols].astype(F32)
        dqkv[:, pl.ds(width + h * HD, HD)] = rope(k_sum, cosine[...], -sine[...]).astype(BF)
        dqkv[:, pl.ds(2 * width + h * HD, HD)] = v_sum.astype(BF)
    for m in made:
        m[2]()
    for d in range(hops, 0, -1):

        @pl.when(t >= d)
        def _():
            send(0, d).wait_send()
            send(1, d).wait_send()


def keys_back_call(cid, T, hops, dq, dk, dv, cosine, sine, jobs=()):
    CH, width = dq.shape
    args, in_specs = (dq, dk, dv, cosine, sine), [vmem()] * 5
    shapes, specs = (out((CH, 3 * width), BF),), (vmem(),)
    scratch = [
        pltpu.VMEM((2, hops, CH, width), BF), pltpu.VMEM((2, hops, CH, width), BF),
        dma(2, hops), dma(2, hops),
    ]
    for job in jobs:
        args += job.inputs
        in_specs += job.in_specs
        shapes += job.shapes
        specs += job.specs
        scratch += job.scratch
    return pl.pallas_call(
        functools.partial(keys_back_body, T, hops, jobs, (len(args), len(shapes))),
        out_shape=shapes,
        in_specs=in_specs,
        out_specs=specs,
        scratch_shapes=scratch,
        compiler_params=talk(cid, 48),
        name="keys_back",
    )(*args)


def rim_body(T, x, o, recv, ss, rs):
    t, p, c = here()

    @pl.when(t < T - 1)
    def _():
        greet((lax.rem(t + 1, T), p, c))

    def send():
        return remote(x, recv, ss, rs, (lax.rem(t + T - 1, T), p, c))

    @pl.when(t > 0)
    def _():
        arrive(1)
        send().start()
        send().wait_send()

    o[...] = jnp.zeros_like(o)

    @pl.when(t < T - 1)
    def _():
        send().wait_recv()
        o[...] = recv[...]


def rim_back(cid, T, x):
    return pl.pallas_call(
        functools.partial(rim_body, T),
        out_shape=out(x.shape),
        in_specs=[vmem()],
        out_specs=vmem(),
        scratch_shapes=[pltpu.VMEM(x.shape, F32), pltpu.SemaphoreType.DMA, pltpu.SemaphoreType.DMA],
        compiler_params=talk(cid),
        name="rim_back",
    )(x)


def conv_sum(xz, mask, taps, lo, size):
    width = taps.shape[1]
    total = jnp.broadcast_to(taps[4:5, :], (size, width))
    for j in range(4):
        rows = xz[pl.ds(lo + HALO - 3 + j, size), pl.ds(0, width)]
        total = total + taps[j : j + 1, :] * rows * mask[pl.ds(lo, size), j : j + 1]
    return total


def conv_body(xz, mask, taps, proj, u, u_low, part):
    CH = u.shape[0]
    step = min(CH, 128)
    for lo in range(0, CH, step):
        cut = pl.ds(lo, step)
        c = conv_sum(xz, mask, taps, lo, step)
        value = c / (1.0 + jnp.exp(-c))
        u[cut, :] = value
        low = value.astype(BF)
        u_low[cut, :] = low
        part[cut, :] = jnp.dot(low, proj[...], preferred_element_type=F32)


def conv_call(xz, mask, taps, proj):
    CH = mask.shape[0]
    width = taps.shape[1]
    return pl.pallas_call(
        conv_body,
        out_shape=(out((CH, width)), out((CH, width), BF), out((CH, proj.shape[1]))),
        in_specs=[vmem()] * 4,
        out_specs=(vmem(),) * 3,
        compiler_params=alone(),
        name="conv",
    )(xz, mask, taps, proj)


def conv_back_body(xz, mask, taps, du, dxs, grads):
    CH, width = du.shape
    step = min(CH, 128)
    dxs[...] = jnp.zeros_like(dxs)
    sums = [jnp.zeros((1, width), F32) for _ in range(5)]
    for lo in range(0, CH, step):
        c = conv_sum(xz, mask, taps, lo, step)
        s = 1.0 / (1.0 + jnp.exp(-c))
        dc = du[pl.ds(lo, step), :] * (s * (1.0 + c * (1.0 - s)))
        sums[4] = sums[4] + jnp.sum(dc, axis=0, keepdims=True)
        for j in range(4):
            rows = pl.ds(lo + HALO - 3 + j, step)
            live = dc * mask[pl.ds(lo, step), j : j + 1]
            sums[j] = sums[j] + jnp.sum(live * xz[rows, pl.ds(0, width)], axis=0, keepdims=True)
            dxs[rows, :] = dxs[rows, :] + live * taps[j : j + 1, :]
    grads[...] = jnp.zeros_like(grads)
    for j in range(5):
        grads[j : j + 1, :] = sums[j]


def conv_back_call(xz, mask, taps, du):
    CH, width = du.shape
    return pl.pallas_call(
        conv_back_body,
        out_shape=(out((HALO + CH, width)), out((8, width))),
        in_specs=[vmem()] * 4,
        out_specs=(vmem(),) * 2,
        compiler_params=alone(),
        name="conv_back",
    )(xz, mask, taps, du)


def wide(block, width):
    return jnp.concatenate([block] * (width // 128), axis=1) if width > 128 else block


def fold(block):
    total = block[:, 0:128]
    for lo in range(128, block.shape[1], 128):
        total = total + block[:, lo : lo + 128]
    return total


def scan_one_body(delta, u, a2, brep, first, end):
    CH, width = delta.shape
    decay = a2[...]

    def group(g, h):
        lo = pl.multiple_of(g * 8, 8)
        d8 = delta[pl.ds(lo, 8), :]
        du8 = d8 * u[pl.ds(lo, 8), :]
        for i in range(8):
            d = d8[i : i + 1, :] + first[lo + i]
            b = wide(brep[pl.ds(pl.multiple_of(g * 128 + i * 16, 16), 16), :], width)
            h = jnp.exp2(d * decay) * h + du8[i : i + 1, :] * b
        return h

    end[...] = lax.fori_loop(0, CH // 8, group, jnp.zeros(decay.shape, F32))


def scan_one(delta, u, a2, brep, first):
    return pl.pallas_call(
        scan_one_body,
        out_shape=out(a2.shape),
        in_specs=[vmem()] * 4 + [smem()],
        out_specs=vmem(),
        compiler_params=alone(),
        name="scan_one",
    )(delta, u, a2, brep, first)


def scan_two_body(delta, u, a2, brep, crep, first, h_in, y, marks):
    CH, width = delta.shape
    decay = a2[...]
    row = lax.broadcasted_iota(jnp.int32, (8, width), 0)

    def group(g, h):
        lo = pl.multiple_of(g * 8, 8)

        @pl.when(lax.rem(g, SUB // 8) == 0)
        def _():
            marks[pl.ds(pl.multiple_of(lax.div(g, SUB // 8) * 16, 16), 16), :] = h

        d8 = delta[pl.ds(lo, 8), :]
        du8 = d8 * u[pl.ds(lo, 8), :]
        y8 = jnp.zeros((8, width), F32)
        for i in range(8):
            at = pl.ds(pl.multiple_of(g * 128 + i * 16, 16), 16)
            d = d8[i : i + 1, :] + first[lo + i]
            h = jnp.exp2(d * decay) * h + du8[i : i + 1, :] * wide(brep[at, :], width)
            total = jnp.sum(h * wide(crep[at, :], width), axis=0, keepdims=True)
            y8 = jnp.where(row == i, total, y8)
        y[pl.ds(lo, 8), :] = y8
        return h

    lax.fori_loop(0, CH // 8, group, h_in[...])


def scan_two(delta, u, a2, brep, crep, first, h_in):
    CH, width = delta.shape
    return pl.pallas_call(
        scan_two_body,
        out_shape=(out((CH, width)), out((CH // SUB * 16, width))),
        in_specs=[vmem()] * 5 + [smem(), vmem()],
        out_specs=(vmem(),) * 2,
        compiler_params=alone(),
        name="scan_two",
    )(delta, u, a2, brep, crep, first, h_in)


def scan_three_body(delta, dy, a2, crep, first, start):
    CH, width = delta.shape
    decay = a2[...]

    def group(step, carry):
        g = CH // 8 - 1 - step
        lo = pl.multiple_of(g * 8, 8)
        d8 = delta[pl.ds(lo, 8), :]
        dy8 = dy[pl.ds(lo, 8), :]
        for i in range(7, -1, -1):
            at = pl.ds(pl.multiple_of(g * 128 + i * 16, 16), 16)
            d = d8[i : i + 1, :] + first[lo + i]
            lam = dy8[i : i + 1, :] * wide(crep[at, :], width) + carry
            carry = jnp.exp2(d * decay) * lam
        return carry

    start[...] = lax.fori_loop(0, CH // 8, group, jnp.zeros(decay.shape, F32))


def scan_three(delta, dy, a2, crep, first):
    return pl.pallas_call(
        scan_three_body,
        out_shape=out(a2.shape),
        in_specs=[vmem()] * 4 + [smem()],
        out_specs=vmem(),
        compiler_params=alone(),
        name="scan_three",
    )(delta, dy, a2, crep, first)


def scan_four_body(
    delta, u, dy, skip, a2, brep, crep, first, marks, g_in,
    ddelta, du_out, db, dc, ga, keep_a, keep_w,
):
    CH, width = delta.shape
    decay = a2[...]
    rate = decay * (1.0 / LOG2E)
    row = lax.broadcasted_iota(jnp.int32, (8, width), 0)
    per = SUB // 8

    def block(step, carried):
        blk = CH // SUB - 1 - step

        def forward(k, h):
            g = blk * per + k
            lo = pl.multiple_of(g * 8, 8)
            d8 = delta[pl.ds(lo, 8), :]
            du8 = d8 * u[pl.ds(lo, 8), :]
            for i in range(8):
                at = pl.ds(pl.multiple_of(g * 128 + i * 16, 16), 16)
                put = pl.ds(pl.multiple_of(k * 128 + i * 16, 16), 16)
                d = d8[i : i + 1, :] + first[lo + i]
                a = jnp.exp2(d * decay)
                keep_a[put, :] = a
                w = a * h
                keep_w[put, :] = w
                h = w + du8[i : i + 1, :] * wide(brep[at, :], width)
            return h

        lax.fori_loop(0, per, forward, marks[pl.ds(pl.multiple_of(blk * 16, 16), 16), :])

        def backward(back, state):
            carry, total_a = state
            k = per - 1 - back
            g = blk * per + k
            lo = pl.multiple_of(g * 8, 8)
            d8 = delta[pl.ds(lo, 8), :]
            u8 = u[pl.ds(lo, 8), :]
            du8 = d8 * u8
            dy8 = dy[pl.ds(lo, 8), :]
            s1 = jnp.zeros((8, width), F32)
            s2 = jnp.zeros((8, width), F32)
            for i in range(7, -1, -1):
                at = pl.ds(pl.multiple_of(g * 128 + i * 16, 16), 16)
                put = pl.ds(pl.multiple_of(k * 128 + i * 16, 16), 16)
                b = wide(brep[at, :], width)
                du = du8[i : i + 1, :]
                dyi = dy8[i : i + 1, :]
                w = keep_w[put, :]
                lam = dyi * wide(crep[at, :], width) + carry
                lw = lam * w
                s1 = jnp.where(row == i, jnp.sum(lam * b, axis=0, keepdims=True), s1)
                s2 = jnp.where(row == i, jnp.sum(lw * rate, axis=0, keepdims=True), s2)
                total_a = total_a + lw * d8[i : i + 1, :]
                dc[at, :] = fold((w + du * b) * dyi)
                db[at, :] = fold(lam * du)
                carry = keep_a[put, :] * lam
            ddelta[pl.ds(lo, 8), :] = s2 + u8 * s1
            du_out[pl.ds(lo, 8), :] = d8 * s1 + skip[0:1, :] * dy8
            return carry, total_a

        return lax.fori_loop(0, per, backward, carried)

    carry, total_a = lax.fori_loop(
        0, CH // SUB, block, (g_in[...], jnp.zeros(decay.shape, F32))
    )
    ga[...] = total_a * rate


def scan_four(delta, u, dy, skip, a2, brep, crep, first, marks, g_in):
    CH, width = delta.shape
    return pl.pallas_call(
        scan_four_body,
        out_shape=(
            out((CH, width)),
            out((CH, width)),
            out((CH * 16, 128)),
            out((CH * 16, 128)),
            out(a2.shape),
        ),
        in_specs=[vmem()] * 7 + [smem(), vmem(), vmem()],
        out_specs=(vmem(),) * 5,
        scratch_shapes=[pltpu.VMEM((SUB * 16, width), F32), pltpu.VMEM((SUB * 16, width), F32)],
        compiler_params=alone(),
        name="scan_four",
    )(delta, u, dy, skip, a2, brep, crep, first, marks, g_in)


def nt(a, b):
    return lax.dot_general(a, b, (((1,), (1,)), ((), ())), preferred_element_type=F32)


def tn(a, b):
    return lax.dot_general(a, b, (((0,), (0,)), ((), ())), preferred_element_type=F32)


def nn(a, b):
    return jnp.dot(a, b, preferred_element_type=F32)


def attend_body(q, k, v, bias, o, lse):
    s = nt(q[...], k[...]) * (HD**-0.5) + bias[...].astype(F32)
    top = jnp.max(s, axis=-1, keepdims=True)
    e = jnp.exp(s - top)
    total = jnp.sum(e, axis=-1, keepdims=True)
    o[...] = nn((e / total).astype(BF), v[...]).astype(BF)
    lse[...] = jnp.broadcast_to(top + jnp.log(total), lse.shape)


def attend(q, k, v, bias):
    CH, width = q.shape
    NK = k.shape[0]
    tq = min(CH, 256)
    return pl.pallas_call(
        attend_body,
        grid=(width // HD, CH // tq),
        out_shape=(out((CH, width), BF), out((CH, width))),
        in_specs=[
            pl.BlockSpec((tq, HD), lambda h, i: (i, h)),
            pl.BlockSpec((NK, HD), lambda h, i: (0, h)),
            pl.BlockSpec((NK, HD), lambda h, i: (0, h)),
            pl.BlockSpec((tq, NK), lambda h, i: (i, 0)),
        ],
        out_specs=(
            pl.BlockSpec((tq, HD), lambda h, i: (i, h)),
            pl.BlockSpec((tq, HD), lambda h, i: (i, h)),
        ),
        compiler_params=alone(),
        name="attend",
    )(q, k, v, bias)


def attend_back_body(q, k, v, bias, lse, do, dq, dk, dv):
    scale = HD**-0.5
    first = pl.program_id(1) == 0
    s = nt(q[...], k[...]) * scale + bias[...].astype(F32)
    prob = jnp.exp(s - lse[:, 0:1])
    dp = nt(do[...], v[...])
    rowdot = jnp.sum(prob * dp, axis=-1, keepdims=True)
    ds = (prob * (dp - rowdot)).astype(BF)
    dq[...] = nn(ds, k[...]) * scale
    add_k = tn(ds, q[...]) * scale
    add_v = tn(prob.astype(BF), do[...])

    @pl.when(first)
    def _():
        dk[...] = add_k
        dv[...] = add_v

    @pl.when(jnp.logical_not(first))
    def _():
        dk[...] += add_k
        dv[...] += add_v


def attend_back(q, k, v, bias, lse, do):
    CH, width = q.shape
    NK = k.shape[0]
    tq = min(CH, 256)
    rows = pl.BlockSpec((tq, HD), lambda h, i: (i, h))
    keys = pl.BlockSpec((NK, HD), lambda h, i: (0, h))
    return pl.pallas_call(
        attend_back_body,
        grid=(width // HD, CH // tq),
        out_shape=(out((CH, width)), out((NK, width)), out((NK, width))),
        in_specs=[rows, keys, keys, pl.BlockSpec((tq, NK), lambda h, i: (i, 0)), rows, rows],
        out_specs=(rows, keys, keys),
        compiler_params=alone(),
        name="attend_back",
    )(q, k, v, bias, lse, do)


def finish_body(n, chunk, *refs):
    blocks, (w, gain, o, total) = refs[:n], refs[n:]
    acc = jnp.zeros((w.shape[0], 1), F32)
    at = 0
    for b in blocks:
        for k in range(b.shape[2] // chunk):
            pieces = [b[q, :, k * chunk : (k + 1) * chunk] for q in range(W)]
            value = jnp.concatenate(pieces, axis=1).astype(F32)
            cut = pl.ds(at, W * chunk)
            acc = acc + jnp.sum(w[:, cut].astype(F32) * value, axis=1, keepdims=True)
            o[:, cut] = value * gain[...]
            at += W * chunk
    total[...] = jnp.broadcast_to(acc, total.shape)


def finish(blocks, w, gain, chunk):
    rows = w.shape[0]
    grad, total = pl.pallas_call(
        functools.partial(finish_body, len(blocks), chunk),
        out_shape=(out(w.shape), out((rows, 128))),
        in_specs=[vmem()] * (len(blocks) + 2),
        out_specs=(vmem(), vmem()),
        compiler_params=alone(),
        name="finish",
    )(*blocks, w, gain.astype(F32).reshape(rows, 1))
    return total[:, 0], grad


def gather_tc(x):
    return lax.all_gather(x.reshape(-1, x.shape[-1]), ("t", "c"), axis=0, tiled=True)


def blocks(x):
    return x.reshape(W, x.shape[0] // W, x.shape[1])


def together(*values):
    return lax.optimization_barrier(values)


def scatter_tc(x):
    return lax.psum_scatter(x, ("t", "c"), scatter_dimension=0, tiled=True)


def swiglu(a):
    width = a.shape[1] // 2
    return jax.nn.silu(a[:, :width]) * a[:, width:]


def swiglu_back(a, dh):
    width = a.shape[1] // 2
    gate, up = a[:, :width], a[:, width:]
    s = jax.nn.sigmoid(gate)
    return jnp.concatenate([dh * up * (s * (1.0 + gate * (1.0 - s))), dh * gate * s], axis=1).astype(BF)


def local(
    inputs, segment_ids, cotangent, norm_mixer, in_proj, conv_weight, conv_bias, state_proj,
    step_proj, step_bias, decay_log, skip_gain, mixer_out, norm_ffn_one, gate_up_one, down_one,
    norm_attn, qkv_proj, attn_out, norm_ffn_two, gate_up_two, down_two,
):
    T = lax.axis_size("t")
    t, p, c = here()
    B, D = inputs.shape[1:]
    CH = W * B
    total = CH * T
    seq_len = min(SEQ_MAX, total)
    CB = conv_bias.shape[0]
    DI = CB * W * T * 2
    FB = down_one.shape[0]
    R = step_proj.shape[0]
    N = decay_log.shape[1]
    NR = state_proj.shape[1]
    width = CB * 2 * T
    heads = H // W * HD
    most = min(WIN, total // 2)
    hops = -(-(most - 1) // CH)

    used = NR + R + N + 7
    rows_in = jnp.concatenate(
        [step_proj, conv_weight, conv_bias[None], step_bias[None], skip_gain[None]]
        + [jnp.zeros((1, CB), BF)],
        axis=0,
    )
    gains = jnp.stack([norm_mixer, norm_ffn_one, norm_attn, norm_ffn_two], axis=1).astype(F32)
    chunks = (2 * CB, 2 * FB, heads, 2 * FB)
    seg8 = jnp.broadcast_to(segment_ids, (8, B))
    x0 = inputs[0].astype(F32)
    nh1_ext, seg_all, par_all, w_in, gu1_mine, qkv_mine, gu2_mine = first_call(
        T, inputs[0], seg8, state_proj, rows_in, decay_log, gains,
        (in_proj, gate_up_one, qkv_proj, gate_up_two), chunks,
    )
    w_in = w_in.reshape(D, -1)
    nh1_ext, attn_late = together(nh1_ext, attn_out)
    devices = 2 * W * T
    pairs = []
    for d in range(devices):
        rest = d % (2 * T)
        pairs.append((d, (rest // 2) * 2 * W + (d // (2 * T)) * 2 + rest % 2))
    ao_mine = lax.ppermute(attn_late, ("t", "p", "c"), pairs)
    w_mix = gather_tc(mixer_out)
    w_gu1 = gather_tc(gu1_mine)
    w_d1 = gather_tc(down_one)
    w_qkv = gather_tc(qkv_mine)
    w_gu2 = gather_tc(gu2_mine)
    w_d2 = gather_tc(down_two)

    seg = seg_all[:, 0, :].reshape(total)
    pos = t * CH + jnp.arange(CH, dtype=jnp.int32)
    padded = jnp.pad(seg, (max(hops * CH, HALO), 0), constant_values=-1)
    lead = max(hops * CH, HALO)
    near = lax.dynamic_slice(padded, (t * CH + lead - HALO,), (CH + HALO,))
    own_seg = near[HALO:]
    conv_mask = jnp.stack(
        [
            (near[HALO - 3 + j : HALO - 3 + j + CH] == own_seg) & ((pos - 3 + j) // seq_len == pos // seq_len)
            & (pos - 3 + j >= 0)
            for j in range(4)
        ]
        + [jnp.zeros((CH,), jnp.bool_)] * 4,
        axis=1,
    ).astype(F32)
    starts = (pos % seq_len == 0) | (near[HALO - 1 : HALO - 1 + CH] != own_seg)
    first = jnp.where(starts, BIG, 0.0).astype(F32)
    alive = jnp.where(jnp.any(starts), 0.0, 1.0).astype(F32)
    NK = (hops + 1) * CH
    key_seg = lax.dynamic_slice(padded, (t * CH + lead - hops * CH,), (NK,))
    key_pos = t * CH - hops * CH + jnp.arange(NK, dtype=jnp.int32)
    away = pos[:, None] - key_pos[None, :]
    allowed = (
        (key_pos[None, :] >= 0) & (away >= 0) & (away < WIN) & (key_seg[None, :] == own_seg[:, None])
        & (key_pos[None, :] // seq_len == (pos // seq_len)[:, None])
    )
    bias = jnp.where(allowed, 0.0, NEG).astype(BF)
    half = HD // 2
    inverse = jnp.exp(jnp.arange(half, dtype=F32) * (-math.log(10000.0) * 2.0 / HD))
    angles = (pos % seq_len).astype(F32)[:, None] * inverse[None, :]
    cos_half, sin_half = jnp.cos(angles), jnp.sin(angles)
    cosine = jnp.concatenate([cos_half, cos_half], axis=1)
    sine = jnp.concatenate([-sin_half, sin_half], axis=1)

    par_all = par_all.reshape(width, 256)
    w_state = par_all[:, :NR]
    w_step = par_all[:, NR : NR + R].T
    side = par_all[:, NR + R : NR + R + 8 + N].astype(F32).T
    a2 = -jnp.exp(side[8:]) * LOG2E
    taps = side[:8]
    step_row = side[5:6]
    skip_row = side[6:7]

    xz = nn(nh1_ext, w_in)
    nh1 = nh1_ext[HALO:]
    u, u_low, part = conv_call(xz, conv_mask, taps, w_state)
    pr = plane_sum(3, part)
    dt_low = pr[:, :R].astype(BF)
    pre = nn(dt_low, w_step) + step_row
    delta = jax.nn.softplus(pre)

    def replicated(block):
        return jnp.broadcast_to(block[:, :, None], (CH, N, 128)).reshape(CH * N, 128)

    brep = replicated(pr[:, R : R + N])
    crep = replicated(pr[:, R + N :])
    sum_delta = jnp.sum(delta, axis=0, keepdims=True)

    def packed(state):
        return jnp.concatenate(
            [state, sum_delta, jnp.full((1, width), alive, F32), jnp.zeros((6, width), F32)], axis=0
        )

    end = scan_one(delta, u, a2, brep, first)
    (h_in,) = chain(4, T, False, packed(end), a2)
    y_scan, marks = scan_two(delta, u, a2, brep, crep, first, h_in)
    y = y_scan + skip_row * u
    zg = xz[HALO:, width:]
    gate_s = jax.nn.sigmoid(zg)
    gated = (y * zg * gate_s).astype(BF)
    x1, nh2 = turn(5, nn(gated, w_mix).astype(BF), x0)

    a_one = nn(nh2, w_gu1)
    h_one = swiglu(a_one).astype(BF)
    x2, nh3, w_ao = turn(6, nn(h_one, w_d1).astype(BF), x1, jobs=(gather_job(T, ao_mine),))
    w_ao = w_ao.reshape(-1, D)

    qkv = nn(nh3, w_qkv)
    q, k_all, v_all, gl4 = keys_call(7, T, hops, qkv, cosine, sine, cotangent[0])
    o, lse = attend(q, k_all, v_all, bias)
    x3, nh4 = turn(8, nn(o, w_ao).astype(BF), x2)

    a_two = nn(nh4, w_gu2)
    h_two = swiglu(a_two).astype(BF)
    last_part = nn(h_two, w_d2).astype(BF)

    g4 = cotangent[0].astype(F32)
    dw_d2 = tn(h_two, gl4).astype(BF)
    da_two = swiglu_back(a_two, nt(gl4, w_d2))
    part, dw_gu2 = together(nt(da_two, w_gu2).astype(BF), tn(nh4, da_two).astype(BF))
    raw_gu2 = scatter_tc(dw_gu2)
    g3, gl3 = turn(10, part, x3, g4)

    do, dw_ao = together(nt(gl3, w_ao).astype(BF), tn(o, gl3).astype(BF))
    dq, dk, dv = attend_back(q, k_all, v_all, bias, lse, do)
    dq, last_part, raw_gu2 = together(dq, last_part, raw_gu2)
    dqkv, final = keys_back_call(
        11, T, hops, dq, dk, dv, cosine, sine, jobs=(sum_job(last_part, x3, BF),)
    )
    dqkv, dw_d2 = together(dqkv, dw_d2)
    grad_d2 = scatter_tc(dw_d2)
    part, dw_qkv = together(nt(dqkv, w_qkv).astype(BF), tn(nh3, dqkv).astype(BF))
    raw_qkv = scatter_tc(dw_qkv)
    g2, gl2, raw_ao = turn(12, part, x2, g3, jobs=(scatter_job(T, dw_ao),))

    da_one, dw_d1 = together(swiglu_back(a_one, nt(gl2, w_d1)), tn(h_one, gl2).astype(BF))
    part, dw_gu1, grad_d2 = together(nt(da_one, w_gu1).astype(BF), tn(nh2, da_one).astype(BF), grad_d2)
    raw_gu1 = scatter_tc(dw_gu1)
    grad_d1 = scatter_tc(dw_d1)
    g1, gl1 = turn(13, part, x1, g2)
    gl1, raw_qkv = together(gl1, raw_qkv)

    dgate = nt(gl1, w_mix)
    dy = dgate * zg * gate_s
    dz_low = (dgate * y * gate_s * (1.0 + zg * (1.0 - gate_s))).astype(BF)
    dy, dw_mix, dw_z = together(dy, tn(gated, gl1).astype(BF), tn(nh1, dz_low).astype(BF))
    grad_mix = scatter_tc(dw_mix)
    raw_z = scatter_tc(dw_z)
    begin = scan_three(delta, dy, a2, crep, first)
    g_in, gu2_b, qkv_b = chain(
        14, T, True, packed(begin), a2, jobs=(spread_job(True, (blocks(raw_gu2), blocks(raw_qkv))),)
    )
    g_in, grad_d1 = together(g_in, grad_d1)
    ddelta, du_scan, db, dc_mat, ga = scan_four(
        delta, u, dy, skip_row, a2, brep, crep, first, marks, g_in
    )
    dpre = ddelta * jax.nn.sigmoid(pre)
    dpre_low = dpre.astype(BF)
    part_back = jnp.concatenate(
        [
            nt(dpre_low, w_step),
            jnp.sum(db, axis=1).reshape(CH, N),
            jnp.sum(dc_mat, axis=1).reshape(CH, N),
        ],
        axis=1,
    )
    part_back, raw_gu1 = together(part_back, raw_gu1)
    dpr_low = plane_sum(15, part_back).astype(BF)
    du = du_scan + nt(dpr_low, w_state)
    dxs_ext, conv_grads = conv_back_call(xz, conv_mask, taps, du)
    rim = rim_back(16, T, dxs_ext[8:16])
    dxs_low = jnp.concatenate(
        [dxs_ext[HALO : HALO + CH - 8], dxs_ext[HALO + CH - 8 :] + rim], axis=0
    ).astype(BF)
    dxz = jnp.concatenate([dxs_low, dz_low], axis=1)
    dxz, dw_x, grad_mix = together(dxz, tn(nh1, dxs_low).astype(BF), grad_mix)
    raw_x = scatter_tc(dw_x)
    small = jnp.concatenate(
        [
            tn(u_low, dpr_low),
            tn(dpre_low, dt_low),
            ga.T,
            conv_grads[:5].T,
            jnp.sum(dpre, axis=0)[:, None],
            jnp.sum(dy * u, axis=0)[:, None],
        ],
        axis=1,
    )
    small = jnp.pad(small, ((0, 0), (0, 256 - used))).astype(BF).reshape(2 * T, CB, 256)
    small, raw_z = together(small, raw_z)
    grad_x, small, gu1_b = turn(
        17, nt(dxz, w_in).astype(BF), x0, g1, gather=False,
        jobs=(small_job(T, small), spread_job(True, (blocks(raw_gu1),))),
    )
    x_b, z_b = run_jobs(20, spread_job(True, (blocks(raw_x), blocks(raw_z))))
    grad_ao = lax.ppermute(raw_ao.astype(BF), ("t", "p", "c"), [(b, a) for a, b in pairs]).astype(F32)

    grad_n1, grad_in = finish((x_b, z_b), in_proj, norm_mixer, chunks[0])
    grad_n2, grad_gu1 = finish((gu1_b,), gate_up_one, norm_ffn_one, chunks[1])
    grad_n3, grad_qkv = finish((qkv_b,), qkv_proj, norm_attn, chunks[2])
    grad_n4, grad_gu2 = finish((gu2_b,), gate_up_two, norm_ffn_two, chunks[3])
    at = NR + R + N
    return (
        final[None],
        grad_x[None],
        grad_n1,
        grad_in,
        small[:, at : at + 4].T,
        small[:, at + 4],
        small[:, :NR],
        small[:, NR : NR + R].T,
        small[:, at + 5],
        small[:, NR + R : at],
        small[:, at + 6],
        grad_mix.astype(F32),
        grad_n2,
        grad_gu1,
        grad_d1.astype(F32),
        grad_n3,
        grad_qkv,
        grad_ao,
        grad_n4,
        grad_gu2,
        grad_d2.astype(F32),
    )


def solution(mesh):
    chunks = mesh.shape["seq"] // W
    view = Mesh(mesh.devices.reshape(chunks, W, mesh.shape["fsdp"]), ("t", "p", "c"))
    every = ("t", "p", "c")
    tokens = P("c", ("t", "p"), None)
    vector, rows, cols = P(every), P(every, None), P(None, every)
    placed = (
        tokens, P("c", ("t", "p")), tokens,
        vector, rows, cols, vector, rows, cols, vector, rows, vector, rows,
        vector, rows, rows, vector, rows, rows, vector, rows, rows,
    )
    return jax.shard_map(
        local,
        mesh=view,
        in_specs=placed,
        out_specs=(tokens, tokens) + placed[3:],
        check_vma=False,
    )
```

```python
import functools
import math

import jax
import jax.numpy as jnp
from jax import lax
from jax.experimental import pallas as pl
from jax.experimental.pallas import tpu as pltpu
from jax.sharding import Mesh
from jax.sharding import PartitionSpec as P

W = 4
H = 12
HD = 128
WIN = 2048
SEQ_MAX = 8192
EPS = 1e-05
NEG = -1e30
BIG = 1e30
LOG2E = 1.4426950408889634
BF = jnp.bfloat16
F32 = jnp.float32
MESH = pl.DeviceIdType.MESH
HALO = 16
SUB = 64
MIB = 1 << 20


def vmem():
    return pl.BlockSpec(memory_space=pltpu.VMEM)


def hbm():
    return pl.BlockSpec(memory_space=pl.ANY)


def smem():
    return pl.BlockSpec(memory_space=pltpu.SMEM)


def here():
    return lax.axis_index("t"), lax.axis_index("p"), lax.axis_index("c")


def greet(device):
    pl.semaphore_signal(
        pltpu.get_barrier_semaphore(), inc=1, device_id=device, device_id_type=MESH
    )


def arrive(count):
    pl.semaphore_wait(pltpu.get_barrier_semaphore(), count)


def arrive_some(count):
    @pl.when(count > 0)
    def _():
        arrive(count)


def remote(src, dst, send, recv, device):
    return pltpu.make_async_remote_copy(
        src_ref=src,
        dst_ref=dst,
        send_sem=send,
        recv_sem=recv,
        device_id=device,
        device_id_type=MESH,
    )


def flip(p, d):
    return lax.bitwise_xor(p, d)


def dma(*shape):
    return pltpu.SemaphoreType.DMA(shape)


def talk(cid, limit=40):
    return pltpu.CompilerParams(
        collective_id=cid, has_side_effects=True, vmem_limit_bytes=limit * MIB
    )


def alone(limit=56):
    return pltpu.CompilerParams(vmem_limit_bytes=limit * MIB)


def out(shape, dtype=F32):
    return jax.ShapeDtypeStruct(shape, dtype)


def unit(x):
    return x * lax.rsqrt(jnp.mean(x * x, axis=-1, keepdims=True) + EPS)


def column_blocks(w, gain, chunk, blocks):
    groups = w.shape[1] // (W * chunk)
    for q in range(W):
        pieces = [w[:, (k * W + q) * chunk : (k * W + q + 1) * chunk] for k in range(groups)]
        value = jnp.concatenate(pieces, axis=1) if groups > 1 else pieces[0]
        blocks[q] = (value.astype(F32) * gain).astype(BF)


def first_body(T, chunks, x, seg, state, rows_in, log_in, gains, *refs):
    n = len(chunks) - 1
    weights, refs = refs[: n + 1], refs[n + 1 :]
    nh, seg_out, par_out, w_in = refs[:4]
    dsts, refs = refs[4 : 4 + n], refs[4 + n :]
    win, srcs, par, refs = refs[0], refs[1 : n + 1], refs[n + 1], refs[n + 2 :]
    (nbuf, zbuf, s_n, r_n, s_h, r_h, s_s, r_s, s_p, r_p, s_w, r_w, s_z, r_z, s_c, r_c, s_l, s_o, r_o) = refs
    t, p, c = here()
    B = x.shape[0]
    count = 0
    for dt in range(T):
        tt = lax.rem(t + dt, T)
        for dp in range(W):
            pp = flip(p, dp)
            if dt or dp:
                greet((tt, pp, c))
                count += 1
            if dt == 0 or dp == 0:
                greet((tt, pp, 1 - c))
                count += 1
    column_blocks(weights[0], gains[:, 0:1], chunks[0], win)
    arrive(count)
    half = lax.div(p, 2)
    slot = lax.rem(p, 2) * 2 + c
    me = t * 2 + c

    def block(src, dst, send, recv, q):
        return remote(src.at[q], dst.at[slot], send.at[q], recv.at[slot], (t, q, half))

    def kept(src, dst, send, q):
        return pltpu.make_async_copy(src.at[q], dst.at[slot], send.at[q])

    def exchange(src, dst, send, recv):
        for q in range(W):
            mine = (p == q) & (half == c)

            @pl.when(jnp.logical_not(mine))
            def _():
                block(src, dst, send, recv, q).start()

            @pl.when(mine)
            def _():
                kept(src, dst, send, q).start()

    def exchanged(src, dst, send, recv, j):
        own = (half == c) & (slot == j)

        @pl.when(jnp.logical_not(own))
        def _():
            remote(src.at[0], dst.at[j], send.at[0], recv.at[j], (t, 0, half)).wait_recv()

    def sent(src, dst, send, recv):
        for q in range(W):
            mine = (p == q) & (half == c)

            @pl.when(jnp.logical_not(mine))
            def _():
                block(src, dst, send, recv, q).wait_send()

    landing = w_in.at[t * 2 + half]
    exchange(win, landing, s_w, r_w)
    nbuf[...] = unit(x[...].astype(F32)).astype(BF)
    zbuf[...] = jnp.zeros_like(zbuf)
    size = rows_in.shape[1]
    eye = (
        lax.broadcasted_iota(jnp.int32, (size, size), 0)
        == lax.broadcasted_iota(jnp.int32, (size, size), 1)
    ).astype(BF)
    lines = nt(eye, rows_in[...]).astype(BF)
    wide_at = state.shape[1]
    par[:, 0:wide_at] = state[...]
    par[:, wide_at:] = jnp.concatenate(
        [lines, log_in[...], jnp.zeros((size, 256 - wide_at - lines.shape[1] - log_in.shape[1]), BF)],
        axis=1,
    )
    rows = pl.ds(pl.multiple_of(HALO + p * B, HALO), B)
    copies = []
    for dt in range(T):
        for dc in range(2):
            if dt or dc:
                copies.append(
                    remote(
                        par, par_out.at[me], s_p.at[dt, dc], r_p.at[dt, dc],
                        (lax.rem(t + dt, T), p, flip(c, dc)),
                    )
                )
    for d in range(1, W):
        copies.append(remote(nbuf, nh.at[rows], s_n.at[d], r_n.at[d], (t, flip(p, d), c)))
    for dt in range(T):
        for dp in range(W):
            if dt or dp:
                copies.append(
                    remote(
                        seg, seg_out.at[t * W + p], s_s.at[dt, dp], r_s.at[dt, dp],
                        (lax.rem(t + dt, T), flip(p, dp), c),
                    )
                )
    copies += [
        pltpu.make_async_copy(nbuf, nh.at[rows], s_l.at[0]),
        pltpu.make_async_copy(par, par_out.at[me], s_l.at[1]),
        pltpu.make_async_copy(seg, seg_out.at[t * W + p], s_l.at[2]),
    ]
    for copy in copies:
        copy.start()
    last = (p == W - 1) & (t < T - 1)
    tail = nbuf.at[pl.ds(B - HALO, HALO)]
    head = nh.at[pl.ds(0, HALO)]

    def rim(q):
        return remote(tail, head, s_h.at[q], r_h, (lax.rem(t + 1, T), q, c))

    @pl.when(last)
    def _():
        for q in range(W):
            rim(q).start()

    @pl.when(t == 0)
    def _():
        clear = pltpu.make_async_copy(zbuf, head, s_l.at[3])
        clear.start()
        clear.wait()

    for i in range(n):
        column_blocks(weights[i + 1], gains[:, i + 1 : i + 2], chunks[i + 1], srcs[i])
        exchange(srcs[i], dsts[i], s_o.at[i], r_o.at[i])

    def on(way, d, j):
        step = 1 - 2 * way
        source = lax.rem(t - step * d + T, T) * 2 + c
        part = w_in.at[source, j]
        return remote(
            part, part, s_z.at[way, d, j], r_z.at[way, d + 1, j], (lax.rem(t + step + T, T), p, c)
        )

    def came(way, d, j):
        step = 1 - 2 * way
        part = w_in.at[lax.rem(t - step * d + T, T) * 2 + c, j]
        return remote(part, part, s_z.at[way, d, j], r_z.at[way, d, j], (lax.rem(t + step + T, T), p, c))

    def across(way, d, j):
        step = 1 - 2 * way
        part = w_in.at[lax.rem(t - step * d + T, T) * 2 + c, j]
        return remote(part, part, s_c.at[way, d, j], r_c.at[way, d, j], (t, p, 1 - c))

    def crossed(way, d, j):
        step = 1 - 2 * way
        part = w_in.at[lax.rem(t - step * d + T, T) * 2 + 1 - c, j]
        return remote(part, part, s_c.at[way, d, j], r_c.at[way, d, j], (t, p, 1 - c))

    def goes(way, d):
        if way == 0:
            return (t >= d) & (t < T - 1)
        return (t + d < T) & (t > 0)

    def arrives(way, d):
        return (t >= d) if way == 0 else (t + d < T)

    for j in range(W):
        mine = (half == c) & (slot == j)

        @pl.when(mine)
        def _():
            for q in range(W):

                @pl.when(p == q)
                def _():
                    kept(win, landing, s_w, q).wait()

        exchanged(win, w_in.at[me], s_w, r_w, j)
        across(0, 0, j).start()
        for way in range(2):

            @pl.when(goes(way, 0))
            def _():
                on(way, 0, j).start()

    for d in range(1, T):
        for j in range(W):
            for way in range(2):

                @pl.when(arrives(way, d))
                def _():
                    came(way, d, j).wait_recv()
                    across(way, d, j).start()

                @pl.when(goes(way, d))
                def _():
                    on(way, d, j).start()

    for copy in copies:
        copy.wait()

    @pl.when(last)
    def _():
        for q in range(W):
            rim(q).wait_send()

    @pl.when(t > 0)
    def _():
        rim(0).wait_recv()

    sent(win, landing, s_w, r_w)
    for i in range(n):
        sent(srcs[i], dsts[i], s_o.at[i], r_o.at[i])
        for q in range(W):
            mine = (p == q) & (half == c)

            @pl.when(mine)
            def _():
                kept(srcs[i], dsts[i], s_o.at[i], q).wait()

        for j in range(W):
            exchanged(srcs[i], dsts[i], s_o.at[i], r_o.at[i], j)
    for d in range(T):
        for j in range(W):
            for way in range(2):
                if d or way == 0:

                    @pl.when(arrives(way, d))
                    def _():
                        across(way, d, j).wait_send()
                        crossed(way, d, j).wait_recv()

                @pl.when(goes(way, d))
                def _():
                    on(way, d, j).wait_send()


def first_call(T, x, seg, state, rows_in, log_in, gains, weights, chunks):
    B, D = x.shape
    n = len(weights) - 1
    blocks = [(W, w.shape[0], w.shape[1] // W) for w in weights]
    return pl.pallas_call(
        functools.partial(first_body, T, chunks),
        out_shape=(
            out((HALO + W * B, D), BF),
            out((W * T,) + seg.shape, jnp.int32),
            out((2 * T, state.shape[0], 256), BF),
            out((2 * T,) + blocks[0], BF),
        )
        + tuple(out(b, BF) for b in blocks[1:]),
        in_specs=[vmem(), hbm()] + [vmem()] * (5 + n),
        out_specs=(hbm(),) * (4 + n),
        scratch_shapes=[pltpu.VMEM(b, BF) for b in blocks]
        + [
            pltpu.VMEM((state.shape[0], 256), BF),
            pltpu.VMEM((B, D), BF),
            pltpu.VMEM((HALO, D), BF),
            dma(W), dma(W), dma(W), pltpu.SemaphoreType.DMA,
            dma(T, W), dma(T, W), dma(T, 2), dma(T, 2), dma(W), dma(W),
            dma(2, T, W), dma(2, T + 1, W), dma(2, T, W), dma(2, T, W), dma(4),
            dma(n, W), dma(n, W),
        ],
        compiler_params=talk(0),
        name="first",
    )(x, seg, state, rows_in, log_in, gains, *weights)


class Job:
    def __init__(self, build, inputs, in_specs, shapes, specs, scratch):
        self.build, self.inputs, self.in_specs = build, tuple(inputs), list(in_specs)
        self.shapes, self.specs, self.scratch = tuple(shapes), tuple(specs), list(scratch)


def take(refs, count):
    head = refs[:count]
    del refs[:count]
    return head


def started(jobs, ins, outs, scratch):
    made = []
    for job in jobs:
        made.append(
            job.build(
                take(ins, len(job.inputs)), take(outs, len(job.shapes)), take(scratch, len(job.scratch))
            )
        )
    return made


def spread_build(n, back):
    def build(srcs, dsts, sems):
        s_w, r_w = sems
        t, p, c = here()
        half = lax.div(p, 2)
        pair = lax.rem(p, 2) * 2 + c
        both = half == c

        def there(q):
            if back:
                return (t, c * 2 + q // 2, jnp.int32(q % 2))
            return (t, jnp.int32(q), half)

        def comes(j):
            if back:
                return (t, jnp.int32(j), half)
            return (t, c * 2 + j // 2, jnp.int32(j % 2))

        slot = p if back else pair

        def own(q):
            return both & ((pair == q) if back else (p == q))

        def from_me(q):
            return both & ((p == q) if back else (pair == q))

        def away(a, q):
            return remote(
                srcs[a].at[q], dsts[a].at[slot], s_w.at[a, q], r_w.at[a, slot], there(q)
            )

        def kept(a, q):
            return pltpu.make_async_copy(srcs[a].at[q], dsts[a].at[slot], s_w.at[a, q])

        for q in range(W):
            source = comes(q)

            @pl.when(jnp.logical_not(from_me(q)))
            def _():
                greet(source)

        def begin():
            for a in range(n):
                for q in range(W):

                    @pl.when(jnp.logical_not(own(q)))
                    def _():
                        away(a, q).start()

                    @pl.when(own(q))
                    def _():
                        kept(a, q).start()

        def end():
            for a in range(n):
                for q in range(W):

                    @pl.when(jnp.logical_not(own(q)))
                    def _():
                        away(a, q).wait_send()

                    @pl.when(own(q))
                    def _():
                        kept(a, q).wait()

                    @pl.when(jnp.logical_not(from_me(q)))
                    def _():
                        remote(
                            srcs[a].at[q], dsts[a].at[q], s_w.at[a, q], r_w.at[a, q], there(q)
                        ).wait_recv()

        return W - both.astype(jnp.int32), begin, end

    return build


def spread_job(back, arrays):
    n = len(arrays)
    return Job(
        spread_build(n, back), arrays, [hbm()] * n,
        [out(a.shape, a.dtype) for a in arrays], [hbm()] * n, [dma(n, W), dma(n, W)],
    )


def finish_body(n, chunk, scaled, *refs):
    blocks, (w, gain, total, o) = refs[:n], refs[n:]
    acc = jnp.zeros((w.shape[0], 1), F32)
    at = 0
    for b in blocks:
        for k in range(b.shape[2] // chunk):
            pieces = [b[q, :, k * chunk : (k + 1) * chunk] for q in range(W)]
            value = jnp.concatenate(pieces, axis=1).astype(F32)
            cut = pl.ds(at, W * chunk)
            acc = acc + jnp.sum(w[:, cut].astype(F32) * value, axis=1, keepdims=True)
            o[:, cut] = value * gain[...] if scaled else value.astype(BF)
            at += W * chunk
    total[...] = jnp.broadcast_to(acc, total.shape)


def finish_job(blocks, w, gain, chunk, scaled=False):
    rows = w.shape[0]
    n = len(blocks)

    def build(ins, outs, scratch):
        return 0, lambda: finish_body(n, chunk, scaled, *ins, *outs), lambda: None

    return Job(
        build, tuple(blocks) + (w, gain.astype(F32).reshape(rows, 1)), [vmem()] * (n + 2),
        [out((rows, 128)), out(w.shape, F32 if scaled else BF)], [vmem(), vmem()], [],
    )


def finish(blocks, w, gain, chunk):
    job = finish_job(blocks, w, gain, chunk, True)
    total, grad = pl.pallas_call(
        functools.partial(finish_body, len(blocks), chunk, True),
        out_shape=job.shapes,
        in_specs=job.in_specs,
        out_specs=job.specs,
        compiler_params=alone(),
        name="finish",
    )(*job.inputs)
    return total[:, 0], grad


def jobs_body(counts, jobs, *refs):
    refs = list(refs)
    ins, outs = take(refs, counts[0]), take(refs, counts[1])
    made = started(jobs, ins, outs, refs)
    arrive(sum(m[0] for m in made))
    for m in made:
        m[1]()
    for m in made:
        m[2]()


def run_jobs(cid, *jobs):
    inputs = sum((j.inputs for j in jobs), ())
    shapes = sum((j.shapes for j in jobs), ())
    return pl.pallas_call(
        functools.partial(jobs_body, (len(inputs), len(shapes)), jobs),
        out_shape=shapes,
        in_specs=sum((j.in_specs for j in jobs), []),
        out_specs=sum((j.specs for j in jobs), ()),
        scratch_shapes=sum((j.scratch for j in jobs), []),
        compiler_params=talk(cid),
        name="jobs%d" % cid,
    )(*inputs)


def plane_sum_body(x, o, sb, recv, ss, rs):
    t, p, c = here()
    for d in range(1, W):
        greet((t, flip(p, d), c))
    sb[...] = x[...].astype(BF)
    arrive(W - 1)
    copies = [
        remote(sb, recv.at[d - 1], ss.at[d - 1], rs.at[d - 1], (t, flip(p, d), c))
        for d in range(1, W)
    ]
    for copy in copies:
        copy.start()
    for copy in copies:
        copy.wait()
    total = x[...]
    for d in range(W - 1):
        total = total + recv[d].astype(F32)
    o[...] = total


def plane_sum(cid, x):
    return pl.pallas_call(
        plane_sum_body,
        out_shape=out(x.shape),
        in_specs=[vmem()],
        out_specs=vmem(),
        scratch_shapes=[
            pltpu.VMEM(x.shape, BF),
            pltpu.VMEM((W - 1,) + x.shape, BF),
            dma(W - 1),
            dma(W - 1),
        ],
        compiler_params=talk(cid),
        name="plane_sum%d" % cid,
    )(x)


def gather_job(T, piece):
    def build(ins, outs, sems):
        (src,), (dst,) = ins, outs
        s_z, r_z, s_c, r_c, s_l = sems
        t, p, c = here()

        def part(dt, core):
            return dst.at[lax.rem(t - dt + T, T) * 2 + core]

        def out_to(dt):
            return remote(src, part(0, c), s_z.at[dt], r_z.at[dt], (lax.rem(t + dt, T), p, c))

        def across(dt):
            return remote(
                src if dt == 0 else part(dt, c), part(dt, c), s_c.at[dt], r_c.at[dt], (t, p, 1 - c)
            )

        keep = pltpu.make_async_copy(src, part(0, c), s_l)
        for dt in range(1, T):
            greet((lax.rem(t + dt, T), p, c))
        greet((t, p, 1 - c))

        def begin():
            for dt in range(1, T):
                out_to(dt).start()
            across(0).start()
            keep.start()

        def end():
            for dt in range(1, T):
                out_to(dt).wait_recv()
                across(dt).start()
            keep.wait()
            for dt in range(T):
                across(dt).wait_send()
                other = part(dt, 1 - c)
                remote(other, other, s_c.at[dt], r_c.at[dt], (t, p, 1 - c)).wait_recv()
            for dt in range(1, T):
                out_to(dt).wait_send()

        return T, begin, end

    return Job(
        build, [piece], [hbm()], [out((2 * T,) + piece.shape, BF)], [hbm()],
        [dma(T), dma(T), dma(T), dma(T), pltpu.SemaphoreType.DMA],
    )


def scatter_job(T, grad):
    grad = grad.reshape(2 * T, -1, grad.shape[-1])

    def build(ins, outs, scratch):
        (src,), (dst,) = ins, outs
        mine, other, recv, s_z, r_z, s_c, r_c, s_l = scratch
        t, p, c = here()

        def at(dt):
            return lax.rem(t + dt, T)

        def across(dt):
            return remote(
                src.at[at(dt) * 2 + 1 - c], other.at[dt], s_c.at[dt], r_c.at[dt], (t, p, 1 - c)
            )

        def load(dt):
            return pltpu.make_async_copy(src.at[at(dt) * 2 + c], mine.at[dt], s_l.at[dt])

        def out_to(dt):
            return remote(mine.at[dt], recv.at[dt - 1], s_z.at[dt], r_z.at[dt], (at(dt), p, c))

        order = list(range(1, T)) + [0]
        for dt in range(1, T):
            greet((at(dt), p, c))
        greet((t, p, 1 - c))

        def begin():
            for dt in order:
                across(dt).start()
                load(dt).start()
            for dt in order[:-1]:
                across(dt).wait_recv()
                load(dt).wait()
                mine[dt] = (mine[dt].astype(F32) + other[dt].astype(F32)).astype(BF)
                out_to(dt).start()

        def end():
            across(0).wait_recv()
            load(0).wait()
            total = mine[0].astype(F32) + other[0].astype(F32)
            for dt in range(1, T):
                out_to(dt).wait_recv()
                total = total + recv[dt - 1].astype(F32)
            dst[...] = total
            for dt in range(T):
                across(dt).wait_send()
            for dt in range(1, T):
                out_to(dt).wait_send()

        return T, begin, end

    shape = grad.shape[1:]
    return Job(
        build, [grad], [hbm()], [out(shape)], [vmem()],
        [
            pltpu.VMEM((T,) + shape, BF),
            pltpu.VMEM((T,) + shape, BF),
            pltpu.VMEM((T - 1,) + shape, BF),
            dma(T), dma(T), dma(T), dma(T), dma(T),
        ],
    )


def sum_job(part, x, dtype):
    B, D = x.shape

    def build(ins, outs, scratch):
        src, base = ins
        (o,) = outs
        own, recv, ss, rs, ls = scratch
        t, p, c = here()

        def copy(d):
            q = flip(p, d)
            return remote(
                src.at[pl.ds(pl.multiple_of(q * B, B), B)], recv.at[d - 1],
                ss.at[d - 1], rs.at[d - 1], (t, q, c),
            )

        local = pltpu.make_async_copy(src.at[pl.ds(pl.multiple_of(p * B, B), B)], own, ls)
        for d in range(1, W):
            greet((t, flip(p, d), c))

        def begin():
            for d in range(1, W):
                copy(d).start()
            local.start()

        def end():
            local.wait()
            total = base[...] + own[...].astype(F32)
            for d in range(1, W):
                copy(d).wait()
                total = total + recv[d - 1].astype(F32)
            o[...] = total.astype(o.dtype)

        return W - 1, begin, end

    return Job(
        build, [part, x], [hbm(), vmem()], [out((B, D), dtype)], [vmem()],
        [
            pltpu.VMEM((B, D), BF), pltpu.VMEM((W - 1, B, D), BF),
            dma(W - 1), dma(W - 1), pltpu.SemaphoreType.DMA,
        ],
    )


def turn_body(back, gather, parts, jobs, counts, *refs):
    refs = list(refs)
    ins, outs = take(refs, counts[0]), take(refs, counts[1])
    part, x = take(ins, 2)
    g = take(ins, 1)[0] if back and gather else None
    o = take(outs, 1)[0]
    gath = take(outs, 1)[0] if gather else None
    own, recv, sbuf, ss, rs, ls, ss2, rs2, ls2 = take(refs, 9)
    t, p, c = here()
    B = x.shape[0]
    rows = B // parts
    for d in range(1, W):
        greet((t, flip(p, d), c))
    made = started(jobs, ins, outs, refs)
    local = pltpu.make_async_copy(part.at[pl.ds(pl.multiple_of(p * B, B), B)], own, ls)
    local.start()
    arrive(sum((m[0] for m in made), W - 1))
    first = {}
    for k in range(parts):
        for d in range(1, W):
            q = flip(p, d)
            first[k, d] = remote(
                part.at[pl.ds(pl.multiple_of(q * B + k * rows, rows), rows)],
                recv.at[d - 1, pl.ds(k * rows, rows)],
                ss.at[d - 1, k],
                rs.at[d - 1, k],
                (t, q, c),
            )
            first[k, d].start()
    for m in made:
        m[1]()
    local.wait()
    later = []
    for k in range(parts):
        for d in range(1, W):
            first[k, d].wait_recv()
        cut = pl.ds(k * rows, rows)
        total = own[cut, :].astype(F32)
        for d in range(W - 1):
            total = total + recv[d, cut, :].astype(F32)
        value = x[cut, :]
        if back:
            r = lax.rsqrt(jnp.mean(value * value, axis=-1, keepdims=True) + EPS)
            hat = value * r
            new = r * (total - hat * jnp.mean(total * hat, axis=-1, keepdims=True))
            new = g[cut, :] + new if g is not None else new
        else:
            new = value + total
        o[cut, :] = new.astype(o.dtype)
        if gather:
            sbuf[cut, :] = (new if back else unit(new)).astype(BF)
            place = gath.at[pl.ds(pl.multiple_of(p * B + k * rows, rows), rows)]
            for d in range(1, W):
                later.append(
                    remote(sbuf.at[cut], place, ss2.at[d - 1, k], rs2.at[d - 1, k], (t, flip(p, d), c))
                )
            later.append(pltpu.make_async_copy(sbuf.at[cut], place, ls2.at[k]))
            for copy in later[-W:]:
                copy.start()
    for m in made:
        m[2]()
    for copy in first.values():
        copy.wait_send()
    for copy in later:
        copy.wait()


def turn(cid, part, x, g=None, gather=True, dtype=F32, parts=2, jobs=()):
    B, D = x.shape
    back = g is not None
    args = (part, x) + ((g,) if back and gather else ())
    in_specs = [hbm()] + [vmem()] * (len(args) - 1)
    shapes, specs = (out((B, D), dtype),), (vmem(),)
    if gather:
        shapes += (out((W * B, D), BF),)
        specs += (hbm(),)
    scratch = [
        pltpu.VMEM((B, D), BF),
        pltpu.VMEM((W - 1, B, D), BF),
        pltpu.VMEM((B, D), BF),
        dma(W - 1, parts), dma(W - 1, parts), pltpu.SemaphoreType.DMA,
        dma(W - 1, parts), dma(W - 1, parts), dma(parts),
    ]
    for job in jobs:
        args += job.inputs
        in_specs += job.in_specs
        shapes += job.shapes
        specs += job.specs
        scratch += job.scratch
    return pl.pallas_call(
        functools.partial(turn_body, back, gather, parts, jobs, (len(args), len(shapes))),
        out_shape=shapes,
        in_specs=in_specs,
        out_specs=specs,
        scratch_shapes=scratch,
        compiler_params=talk(cid),
        name="turn%d" % cid,
    )(*args)


def chain_body(T, back, jobs, counts, *refs):
    refs = list(refs)
    ins, outs = take(refs, counts[0]), take(refs, counts[1])
    v, a2 = take(ins, 2)
    (h,) = take(outs, 1)
    recv, ss, rs = take(refs, 3)
    t, p, c = here()
    sign = -1 if back else 1
    for k in range(1, T):
        source = t - sign * k

        @pl.when((source >= 0) & (source < T))
        def _():
            greet((lax.rem(source + T, T), p, c))

    made = started(jobs, ins, outs, refs)
    arrive_some(sum((m[0] for m in made), t if back else T - 1 - t))

    def send(k):
        to = lax.rem(t + sign * k + T, T)
        return remote(v, recv.at[k - 1], ss.at[k - 1], rs.at[k - 1], (to, p, c))

    for k in range(1, T):
        to = t + sign * k

        @pl.when((to >= 0) & (to < T))
        def _():
            send(k).start()

    for m in made:
        m[1]()
    h[...] = jnp.zeros_like(h)
    for k in range(T - 1, 0, -1):
        source = t - sign * k

        @pl.when((source >= 0) & (source < T))
        def _():
            send(k).wait_recv()
            decay = jnp.exp2(a2[...] * recv[k - 1, 16:17, :]) * recv[k - 1, 17:18, :]
            h[...] = recv[k - 1, 0:16, :] + decay * h[...]

    for k in range(1, T):
        to = t + sign * k

        @pl.when((to >= 0) & (to < T))
        def _():
            send(k).wait_send()

    for m in made:
        m[2]()


def chain(cid, T, back, v, a2, jobs=()):
    args, in_specs = (v, a2), [vmem(), vmem()]
    shapes, specs = (out(a2.shape),), (vmem(),)
    scratch = [pltpu.VMEM((T - 1,) + v.shape, F32), dma(T - 1), dma(T - 1)]
    for job in jobs:
        args += job.inputs
        in_specs += job.in_specs
        shapes += job.shapes
        specs += job.specs
        scratch += job.scratch
    return pl.pallas_call(
        functools.partial(chain_body, T, back, jobs, (len(args), len(shapes))),
        out_shape=shapes,
        in_specs=in_specs,
        out_specs=specs,
        scratch_shapes=scratch,
        compiler_params=talk(cid),
        name="chain%d" % cid,
    )(*args)


def rope(w, cosine, sine):
    return w * cosine + pltpu.roll(w, HD // 2, 1) * sine


def keys_body(T, hops, qkv, cosine, sine, ct, q, k_all, v_all, ct_out, ss, rs, s_g, r_g, s_l):
    t, p, c = here()
    CH = q.shape[0]
    width = q.shape[1]
    B = ct.shape[0]

    @pl.when(t > 0)
    def _():
        greet((lax.rem(t - 1 + T, T), p, c))

    for d in range(1, W):
        greet((t, flip(p, d), c))

    mine = pl.ds(hops * CH, CH)
    for h in range(width // HD):
        cols = pl.ds(h * HD, HD)
        k_all[mine, cols] = rope(
            qkv[:, pl.ds(width + h * HD, HD)], cosine[...], sine[...]
        ).astype(BF)
    v_all[mine, :] = qkv[:, pl.ds(2 * width, width)].astype(BF)

    @pl.when(t < T - 1)
    def _():
        arrive(W)

    @pl.when(t == T - 1)
    def _():
        arrive(W - 1)

    def send(a, d):
        ref = (k_all, v_all)[a]
        return remote(
            ref.at[pl.ds((hops - d + 1) * CH, CH)],
            ref.at[pl.ds((hops - d) * CH, CH)],
            ss.at[a, d - 1],
            rs.at[a, d - 1],
            (lax.rem(t + 1, T), p, c),
        )

    for d in range(1, hops + 1):
        goes = (t < T - 1) & (t >= d - 1)

        @pl.when(goes)
        def _():
            send(0, d).start()
            send(1, d).start()

        if d == 1:
            rows = ct_out.at[pl.ds(pl.multiple_of(p * B, B), B)]
            copies = [
                remote(ct, rows, s_g.at[e], r_g.at[e], (t, flip(p, e), c)) for e in range(1, W)
            ] + [pltpu.make_async_copy(ct, rows, s_l)]
            for copy in copies:
                copy.start()
            for h in range(width // HD):
                cols = pl.ds(h * HD, HD)
                q[:, cols] = rope(qkv[:, cols], cosine[...], sine[...]).astype(BF)

        @pl.when(t < d)
        def _():
            k_all[pl.ds((hops - d) * CH, CH), :] = jnp.zeros((CH, width), BF)
            v_all[pl.ds((hops - d) * CH, CH), :] = jnp.zeros((CH, width), BF)

        @pl.when(t >= d)
        def _():
            send(0, d).wait_recv()
            send(1, d).wait_recv()

    for d in range(1, hops + 1):
        goes = (t < T - 1) & (t >= d - 1)

        @pl.when(goes)
        def _():
            send(0, d).wait_send()
            send(1, d).wait_send()

    for copy in copies:
        copy.wait()


def keys_call(cid, T, hops, qkv, cosine, sine, ct):
    CH = qkv.shape[0]
    width = qkv.shape[1] // 3
    return pl.pallas_call(
        functools.partial(keys_body, T, hops),
        out_shape=(
            out((CH, width), BF),
            out(((hops + 1) * CH, width), BF),
            out(((hops + 1) * CH, width), BF),
            out((W * ct.shape[0], ct.shape[1]), BF),
        ),
        in_specs=[vmem()] * 3 + [hbm()],
        out_specs=(vmem(),) * 3 + (hbm(),),
        scratch_shapes=[
            dma(2, hops), dma(2, hops), dma(W), dma(W), pltpu.SemaphoreType.DMA,
        ],
        compiler_params=talk(cid),
        name="keys",
    )(qkv, cosine, sine, ct)


def keys_back_body(T, hops, jobs, counts, *refs):
    refs = list(refs)
    ins, outs = take(refs, counts[0]), take(refs, counts[1])
    dq, dk, dv, cosine, sine = take(ins, 5)
    (dqkv,) = take(outs, 1)
    sb, recv, ss, rs = take(refs, 4)
    t, p, c = here()
    CH = dq.shape[0]
    width = dq.shape[1]

    @pl.when(t < T - 1)
    def _():
        greet((lax.rem(t + 1, T), p, c))

    made = started(jobs, ins, outs, refs)
    extra = sum(m[0] for m in made)

    def send(a, d):
        return remote(
            sb.at[a, d - 1],
            recv.at[a, d - 1],
            ss.at[a, d - 1],
            rs.at[a, d - 1],
            (lax.rem(t - 1 + T, T), p, c),
        )

    for d in range(hops, 0, -1):
        rows = pl.ds((hops - d) * CH, CH)
        k_sum = dk[rows, :]
        v_sum = dv[rows, :]
        if d == hops:
            sb[0, d - 1] = k_sum.astype(BF)
            sb[1, d - 1] = v_sum.astype(BF)

            @pl.when(t > 0)
            def _():
                arrive(1 + extra)

            if extra:

                @pl.when(t == 0)
                def _():
                    arrive(extra)

        else:

            @pl.when((t < T - 1) & (t >= d))
            def _():
                send(0, d + 1).wait_recv()
                send(1, d + 1).wait_recv()

            @pl.when((t == T - 1) | (t < d))
            def _():
                recv[0, d] = jnp.zeros((CH, width), BF)
                recv[1, d] = jnp.zeros((CH, width), BF)

            sb[0, d - 1] = (k_sum + recv[0, d].astype(F32)).astype(BF)
            sb[1, d - 1] = (v_sum + recv[1, d].astype(F32)).astype(BF)

        @pl.when(t >= d)
        def _():
            send(0, d).start()
            send(1, d).start()

        if d == hops:
            for m in made:
                m[1]()
            for h in range(width // HD):
                cols = pl.ds(h * HD, HD)
                dqkv[:, cols] = rope(dq[:, cols], cosine[...], -sine[...]).astype(BF)

    @pl.when(t < T - 1)
    def _():
        send(0, 1).wait_recv()
        send(1, 1).wait_recv()

    @pl.when(t == T - 1)
    def _():
        recv[0, 0] = jnp.zeros((CH, width), BF)
        recv[1, 0] = jnp.zeros((CH, width), BF)

    mine = pl.ds(hops * CH, CH)
    for h in range(width // HD):
        cols = pl.ds(h * HD, HD)
        k_sum = dk[mine, cols] + recv[0, 0, :, cols].astype(F32)
        v_sum = dv[mine, cols] + recv[1, 0, :, cols].astype(F32)
        dqkv[:, pl.ds(width + h * HD, HD)] = rope(k_sum, cosine[...], -sine[...]).astype(BF)
        dqkv[:, pl.ds(2 * width + h * HD, HD)] = v_sum.astype(BF)
    for m in made:
        m[2]()
    for d in range(hops, 0, -1):

        @pl.when(t >= d)
        def _():
            send(0, d).wait_send()
            send(1, d).wait_send()


def keys_back_call(cid, T, hops, dq, dk, dv, cosine, sine, jobs=()):
    CH, width = dq.shape
    args, in_specs = (dq, dk, dv, cosine, sine), [vmem()] * 5
    shapes, specs = (out((CH, 3 * width), BF),), (vmem(),)
    scratch = [
        pltpu.VMEM((2, hops, CH, width), BF), pltpu.VMEM((2, hops, CH, width), BF),
        dma(2, hops), dma(2, hops),
    ]
    for job in jobs:
        args += job.inputs
        in_specs += job.in_specs
        shapes += job.shapes
        specs += job.specs
        scratch += job.scratch
    return pl.pallas_call(
        functools.partial(keys_back_body, T, hops, jobs, (len(args), len(shapes))),
        out_shape=shapes,
        in_specs=in_specs,
        out_specs=specs,
        scratch_shapes=scratch,
        compiler_params=talk(cid, 48),
        name="keys_back",
    )(*args)


def rim_body(T, x, o, recv, ss, rs):
    t, p, c = here()

    @pl.when(t < T - 1)
    def _():
        greet((lax.rem(t + 1, T), p, c))

    def send():
        return remote(x, recv, ss, rs, (lax.rem(t + T - 1, T), p, c))

    @pl.when(t > 0)
    def _():
        arrive(1)
        send().start()
        send().wait_send()

    o[...] = jnp.zeros_like(o)

    @pl.when(t < T - 1)
    def _():
        send().wait_recv()
        o[...] = recv[...]


def rim_back(cid, T, x):
    return pl.pallas_call(
        functools.partial(rim_body, T),
        out_shape=out(x.shape),
        in_specs=[vmem()],
        out_specs=vmem(),
        scratch_shapes=[pltpu.VMEM(x.shape, F32), pltpu.SemaphoreType.DMA, pltpu.SemaphoreType.DMA],
        compiler_params=talk(cid),
        name="rim_back",
    )(x)


def conv_sum(xz, mask, taps, lo, size):
    width = taps.shape[1]
    total = jnp.broadcast_to(taps[4:5, :], (size, width))
    for j in range(4):
        rows = xz[pl.ds(lo + HALO - 3 + j, size), pl.ds(0, width)]
        total = total + taps[j : j + 1, :] * rows * mask[pl.ds(lo, size), j : j + 1]
    return total


def conv_body(xz, mask, taps, proj, u, u_low, part):
    CH = u.shape[0]
    step = min(CH, 128)
    for lo in range(0, CH, step):
        cut = pl.ds(lo, step)
        c = conv_sum(xz, mask, taps, lo, step)
        value = c / (1.0 + jnp.exp(-c))
        u[cut, :] = value
        low = value.astype(BF)
        u_low[cut, :] = low
        part[cut, :] = jnp.dot(low, proj[...], preferred_element_type=F32)


def conv_call(xz, mask, taps, proj):
    CH = mask.shape[0]
    width = taps.shape[1]
    return pl.pallas_call(
        conv_body,
        out_shape=(out((CH, width)), out((CH, width), BF), out((CH, proj.shape[1]))),
        in_specs=[vmem()] * 4,
        out_specs=(vmem(),) * 3,
        compiler_params=alone(),
        name="conv",
    )(xz, mask, taps, proj)


def conv_back_body(xz, mask, taps, du, dxs, grads):
    CH, width = du.shape
    step = min(CH, 128)
    dxs[...] = jnp.zeros_like(dxs)
    sums = [jnp.zeros((1, width), F32) for _ in range(5)]
    for lo in range(0, CH, step):
        c = conv_sum(xz, mask, taps, lo, step)
        s = 1.0 / (1.0 + jnp.exp(-c))
        dc = du[pl.ds(lo, step), :] * (s * (1.0 + c * (1.0 - s)))
        sums[4] = sums[4] + jnp.sum(dc, axis=0, keepdims=True)
        for j in range(4):
            rows = pl.ds(lo + HALO - 3 + j, step)
            live = dc * mask[pl.ds(lo, step), j : j + 1]
            sums[j] = sums[j] + jnp.sum(live * xz[rows, pl.ds(0, width)], axis=0, keepdims=True)
            dxs[rows, :] = dxs[rows, :] + live * taps[j : j + 1, :]
    grads[...] = jnp.zeros_like(grads)
    for j in range(5):
        grads[j : j + 1, :] = sums[j]


def conv_back_call(xz, mask, taps, du):
    CH, width = du.shape
    return pl.pallas_call(
        conv_back_body,
        out_shape=(out((HALO + CH, width)), out((8, width))),
        in_specs=[vmem()] * 4,
        out_specs=(vmem(),) * 2,
        compiler_params=alone(),
        name="conv_back",
    )(xz, mask, taps, du)


def wide(block, width):
    return jnp.concatenate([block] * (width // 128), axis=1) if width > 128 else block


def fold(block):
    total = block[:, 0:128]
    for lo in range(128, block.shape[1], 128):
        total = total + block[:, lo : lo + 128]
    return total


def scan_one_body(delta, u, a2, brep, first, end):
    CH, width = delta.shape
    decay = a2[...]

    def group(g, h):
        lo = pl.multiple_of(g * 8, 8)
        d8 = delta[pl.ds(lo, 8), :]
        du8 = d8 * u[pl.ds(lo, 8), :]
        for i in range(8):
            d = d8[i : i + 1, :] + first[lo + i]
            b = wide(brep[pl.ds(pl.multiple_of(g * 128 + i * 16, 16), 16), :], width)
            h = jnp.exp2(d * decay) * h + du8[i : i + 1, :] * b
        return h

    end[...] = lax.fori_loop(0, CH // 8, group, jnp.zeros(decay.shape, F32))


def scan_one(delta, u, a2, brep, first):
    return pl.pallas_call(
        scan_one_body,
        out_shape=out(a2.shape),
        in_specs=[vmem()] * 4 + [smem()],
        out_specs=vmem(),
        compiler_params=alone(),
        name="scan_one",
    )(delta, u, a2, brep, first)


def scan_two_body(delta, u, a2, brep, crep, first, h_in, y, marks):
    CH, width = delta.shape
    decay = a2[...]
    row = lax.broadcasted_iota(jnp.int32, (8, width), 0)

    def group(g, h):
        lo = pl.multiple_of(g * 8, 8)

        @pl.when(lax.rem(g, SUB // 8) == 0)
        def _():
            marks[pl.ds(pl.multiple_of(lax.div(g, SUB // 8) * 16, 16), 16), :] = h

        d8 = delta[pl.ds(lo, 8), :]
        du8 = d8 * u[pl.ds(lo, 8), :]
        y8 = jnp.zeros((8, width), F32)
        for i in range(8):
            at = pl.ds(pl.multiple_of(g * 128 + i * 16, 16), 16)
            d = d8[i : i + 1, :] + first[lo + i]
            h = jnp.exp2(d * decay) * h + du8[i : i + 1, :] * wide(brep[at, :], width)
            total = jnp.sum(h * wide(crep[at, :], width), axis=0, keepdims=True)
            y8 = jnp.where(row == i, total, y8)
        y[pl.ds(lo, 8), :] = y8
        return h

    lax.fori_loop(0, CH // 8, group, h_in[...])


def scan_two(delta, u, a2, brep, crep, first, h_in):
    CH, width = delta.shape
    return pl.pallas_call(
        scan_two_body,
        out_shape=(out((CH, width)), out((CH // SUB * 16, width))),
        in_specs=[vmem()] * 5 + [smem(), vmem()],
        out_specs=(vmem(),) * 2,
        compiler_params=alone(),
        name="scan_two",
    )(delta, u, a2, brep, crep, first, h_in)


def scan_three_body(delta, dy, a2, crep, first, start):
    CH, width = delta.shape
    decay = a2[...]

    def group(step, carry):
        g = CH // 8 - 1 - step
        lo = pl.multiple_of(g * 8, 8)
        d8 = delta[pl.ds(lo, 8), :]
        dy8 = dy[pl.ds(lo, 8), :]
        for i in range(7, -1, -1):
            at = pl.ds(pl.multiple_of(g * 128 + i * 16, 16), 16)
            d = d8[i : i + 1, :] + first[lo + i]
            lam = dy8[i : i + 1, :] * wide(crep[at, :], width) + carry
            carry = jnp.exp2(d * decay) * lam
        return carry

    start[...] = lax.fori_loop(0, CH // 8, group, jnp.zeros(decay.shape, F32))


def scan_three(delta, dy, a2, crep, first):
    return pl.pallas_call(
        scan_three_body,
        out_shape=out(a2.shape),
        in_specs=[vmem()] * 4 + [smem()],
        out_specs=vmem(),
        compiler_params=alone(),
        name="scan_three",
    )(delta, dy, a2, crep, first)


def scan_four_body(
    delta, u, dy, skip, a2, brep, crep, first, marks, g_in,
    ddelta, du_out, db, dc, ga, keep_a, keep_w,
):
    CH, width = delta.shape
    decay = a2[...]
    rate = decay * (1.0 / LOG2E)
    row = lax.broadcasted_iota(jnp.int32, (8, width), 0)
    per = SUB // 8

    def block(step, carried):
        blk = CH // SUB - 1 - step

        def forward(k, h):
            g = blk * per + k
            lo = pl.multiple_of(g * 8, 8)
            d8 = delta[pl.ds(lo, 8), :]
            du8 = d8 * u[pl.ds(lo, 8), :]
            for i in range(8):
                at = pl.ds(pl.multiple_of(g * 128 + i * 16, 16), 16)
                put = pl.ds(pl.multiple_of(k * 128 + i * 16, 16), 16)
                d = d8[i : i + 1, :] + first[lo + i]
                a = jnp.exp2(d * decay)
                keep_a[put, :] = a
                w = a * h
                keep_w[put, :] = w
                h = w + du8[i : i + 1, :] * wide(brep[at, :], width)
            return h

        lax.fori_loop(0, per, forward, marks[pl.ds(pl.multiple_of(blk * 16, 16), 16), :])

        def backward(back, state):
            carry, total_a = state
            k = per - 1 - back
            g = blk * per + k
            lo = pl.multiple_of(g * 8, 8)
            d8 = delta[pl.ds(lo, 8), :]
            u8 = u[pl.ds(lo, 8), :]
            du8 = d8 * u8
            dy8 = dy[pl.ds(lo, 8), :]
            s1 = jnp.zeros((8, width), F32)
            s2 = jnp.zeros((8, width), F32)
            for i in range(7, -1, -1):
                at = pl.ds(pl.multiple_of(g * 128 + i * 16, 16), 16)
                put = pl.ds(pl.multiple_of(k * 128 + i * 16, 16), 16)
                b = wide(brep[at, :], width)
                du = du8[i : i + 1, :]
                dyi = dy8[i : i + 1, :]
                w = keep_w[put, :]
                lam = dyi * wide(crep[at, :], width) + carry
                lw = lam * w
                s1 = jnp.where(row == i, jnp.sum(lam * b, axis=0, keepdims=True), s1)
                s2 = jnp.where(row == i, jnp.sum(lw * rate, axis=0, keepdims=True), s2)
                total_a = total_a + lw * d8[i : i + 1, :]
                dc[at, :] = fold((w + du * b) * dyi)
                db[at, :] = fold(lam * du)
                carry = keep_a[put, :] * lam
            ddelta[pl.ds(lo, 8), :] = s2 + u8 * s1
            du_out[pl.ds(lo, 8), :] = d8 * s1 + skip[0:1, :] * dy8
            return carry, total_a

        return lax.fori_loop(0, per, backward, carried)

    carry, total_a = lax.fori_loop(
        0, CH // SUB, block, (g_in[...], jnp.zeros(decay.shape, F32))
    )
    ga[...] = total_a * rate


def scan_four(delta, u, dy, skip, a2, brep, crep, first, marks, g_in):
    CH, width = delta.shape
    return pl.pallas_call(
        scan_four_body,
        out_shape=(
            out((CH, width)),
            out((CH, width)),
            out((CH * 16, 128)),
            out((CH * 16, 128)),
            out(a2.shape),
        ),
        in_specs=[vmem()] * 7 + [smem(), vmem(), vmem()],
        out_specs=(vmem(),) * 5,
        scratch_shapes=[pltpu.VMEM((SUB * 16, width), F32), pltpu.VMEM((SUB * 16, width), F32)],
        compiler_params=alone(),
        name="scan_four",
    )(delta, u, dy, skip, a2, brep, crep, first, marks, g_in)


def nt(a, b):
    return lax.dot_general(a, b, (((1,), (1,)), ((), ())), preferred_element_type=F32)


def tn(a, b):
    return lax.dot_general(a, b, (((0,), (0,)), ((), ())), preferred_element_type=F32)


def nn(a, b):
    return jnp.dot(a, b, preferred_element_type=F32)


def attend_body(q, k, v, bias, o, lse):
    s = nt(q[...], k[...]) * (HD**-0.5) + bias[...].astype(F32)
    top = jnp.max(s, axis=-1, keepdims=True)
    e = jnp.exp(s - top)
    total = jnp.sum(e, axis=-1, keepdims=True)
    o[...] = nn((e / total).astype(BF), v[...]).astype(BF)
    lse[...] = jnp.broadcast_to(top + jnp.log(total), lse.shape)


def attend(q, k, v, bias):
    CH, width = q.shape
    NK = k.shape[0]
    tq = min(CH, 256)
    return pl.pallas_call(
        attend_body,
        grid=(width // HD, CH // tq),
        out_shape=(out((CH, width), BF), out((CH, width))),
        in_specs=[
            pl.BlockSpec((tq, HD), lambda h, i: (i, h)),
            pl.BlockSpec((NK, HD), lambda h, i: (0, h)),
            pl.BlockSpec((NK, HD), lambda h, i: (0, h)),
            pl.BlockSpec((tq, NK), lambda h, i: (i, 0)),
        ],
        out_specs=(
            pl.BlockSpec((tq, HD), lambda h, i: (i, h)),
            pl.BlockSpec((tq, HD), lambda h, i: (i, h)),
        ),
        compiler_params=alone(),
        name="attend",
    )(q, k, v, bias)


def attend_back_body(q, k, v, bias, lse, do, dq, dk, dv):
    scale = HD**-0.5
    first = pl.program_id(1) == 0
    s = nt(q[...], k[...]) * scale + bias[...].astype(F32)
    prob = jnp.exp(s - lse[:, 0:1])
    dp = nt(do[...], v[...])
    rowdot = jnp.sum(prob * dp, axis=-1, keepdims=True)
    ds = (prob * (dp - rowdot)).astype(BF)
    dq[...] = nn(ds, k[...]) * scale
    add_k = tn(ds, q[...]) * scale
    add_v = tn(prob.astype(BF), do[...])

    @pl.when(first)
    def _():
        dk[...] = add_k
        dv[...] = add_v

    @pl.when(jnp.logical_not(first))
    def _():
        dk[...] += add_k
        dv[...] += add_v


def attend_back(q, k, v, bias, lse, do):
    CH, width = q.shape
    NK = k.shape[0]
    tq = min(CH, 256)
    rows = pl.BlockSpec((tq, HD), lambda h, i: (i, h))
    keys = pl.BlockSpec((NK, HD), lambda h, i: (0, h))
    return pl.pallas_call(
        attend_back_body,
        grid=(width // HD, CH // tq),
        out_shape=(out((CH, width)), out((NK, width)), out((NK, width))),
        in_specs=[rows, keys, keys, pl.BlockSpec((tq, NK), lambda h, i: (i, 0)), rows, rows],
        out_specs=(rows, keys, keys),
        compiler_params=alone(),
        name="attend_back",
    )(q, k, v, bias, lse, do)


def gather_tc(x):
    return lax.all_gather(x.reshape(-1, x.shape[-1]), ("t", "c"), axis=0, tiled=True)


def blocks(x):
    return x.reshape(W, x.shape[0] // W, x.shape[1])


def together(*values):
    return lax.optimization_barrier(values)


def scatter_tc(x):
    return lax.psum_scatter(x, ("t", "c"), scatter_dimension=0, tiled=True)


def swiglu(a):
    width = a.shape[1] // 2
    return jax.nn.silu(a[:, :width]) * a[:, width:]


def swiglu_back(a, dh):
    width = a.shape[1] // 2
    gate, up = a[:, :width], a[:, width:]
    s = jax.nn.sigmoid(gate)
    return jnp.concatenate([dh * up * (s * (1.0 + gate * (1.0 - s))), dh * gate * s], axis=1).astype(BF)


def local(
    inputs, segment_ids, cotangent, norm_mixer, in_proj, conv_weight, conv_bias, state_proj,
    step_proj, step_bias, decay_log, skip_gain, mixer_out, norm_ffn_one, gate_up_one, down_one,
    norm_attn, qkv_proj, attn_out, norm_ffn_two, gate_up_two, down_two,
):
    T = lax.axis_size("t")
    t, p, c = here()
    B, D = inputs.shape[1:]
    CH = W * B
    total = CH * T
    seq_len = min(SEQ_MAX, total)
    CB = conv_bias.shape[0]
    DI = CB * W * T * 2
    FB = down_one.shape[0]
    R = step_proj.shape[0]
    N = decay_log.shape[1]
    NR = state_proj.shape[1]
    width = CB * 2 * T
    heads = H // W * HD
    most = min(WIN, total // 2)
    hops = -(-(most - 1) // CH)

    used = NR + R + N + 7
    rows_in = jnp.concatenate(
        [step_proj, conv_weight, conv_bias[None], step_bias[None], skip_gain[None]]
        + [jnp.zeros((1, CB), BF)],
        axis=0,
    )
    gains = jnp.stack([norm_mixer, norm_ffn_one, norm_attn, norm_ffn_two], axis=1).astype(F32)
    chunks = (2 * CB, 2 * FB, heads, 2 * FB)
    seg8 = jnp.broadcast_to(segment_ids, (8, B))
    x0 = inputs[0].astype(F32)
    nh1_ext, seg_all, par_all, w_in, gu1_mine, qkv_mine, gu2_mine = first_call(
        T, inputs[0], seg8, state_proj, rows_in, decay_log, gains,
        (in_proj, gate_up_one, qkv_proj, gate_up_two), chunks,
    )
    w_in = w_in.reshape(D, -1)
    nh1_ext, attn_late = together(nh1_ext, attn_out)
    devices = 2 * W * T
    pairs = []
    for d in range(devices):
        rest = d % (2 * T)
        pairs.append((d, (rest // 2) * 2 * W + (d // (2 * T)) * 2 + rest % 2))
    ao_mine = lax.ppermute(attn_late, ("t", "p", "c"), pairs)
    w_mix = gather_tc(mixer_out)
    w_gu1 = gather_tc(gu1_mine)
    w_d1 = gather_tc(down_one)
    w_qkv = gather_tc(qkv_mine)
    w_gu2 = gather_tc(gu2_mine)
    w_d2 = gather_tc(down_two)

    seg = seg_all[:, 0, :].reshape(total)
    pos = t * CH + jnp.arange(CH, dtype=jnp.int32)
    padded = jnp.pad(seg, (max(hops * CH, HALO), 0), constant_values=-1)
    lead = max(hops * CH, HALO)
    near = lax.dynamic_slice(padded, (t * CH + lead - HALO,), (CH + HALO,))
    own_seg = near[HALO:]
    conv_mask = jnp.stack(
        [
            (near[HALO - 3 + j : HALO - 3 + j + CH] == own_seg) & ((pos - 3 + j) // seq_len == pos // seq_len)
            & (pos - 3 + j >= 0)
            for j in range(4)
        ]
        + [jnp.zeros((CH,), jnp.bool_)] * 4,
        axis=1,
    ).astype(F32)
    starts = (pos % seq_len == 0) | (near[HALO - 1 : HALO - 1 + CH] != own_seg)
    first = jnp.where(starts, BIG, 0.0).astype(F32)
    alive = jnp.where(jnp.any(starts), 0.0, 1.0).astype(F32)
    NK = (hops + 1) * CH
    key_seg = lax.dynamic_slice(padded, (t * CH + lead - hops * CH,), (NK,))
    key_pos = t * CH - hops * CH + jnp.arange(NK, dtype=jnp.int32)
    away = pos[:, None] - key_pos[None, :]
    allowed = (
        (key_pos[None, :] >= 0) & (away >= 0) & (away < WIN) & (key_seg[None, :] == own_seg[:, None])
        & (key_pos[None, :] // seq_len == (pos // seq_len)[:, None])
    )
    bias = jnp.where(allowed, 0.0, NEG).astype(BF)
    half = HD // 2
    inverse = jnp.exp(jnp.arange(half, dtype=F32) * (-math.log(10000.0) * 2.0 / HD))
    angles = (pos % seq_len).astype(F32)[:, None] * inverse[None, :]
    cos_half, sin_half = jnp.cos(angles), jnp.sin(angles)
    cosine = jnp.concatenate([cos_half, cos_half], axis=1)
    sine = jnp.concatenate([-sin_half, sin_half], axis=1)

    par_all = par_all.reshape(width, 256)
    w_state = par_all[:, :NR]
    w_step = par_all[:, NR : NR + R].T
    side = par_all[:, NR + R : NR + R + 8 + N].astype(F32).T
    a2 = -jnp.exp(side[8:]) * LOG2E
    taps = side[:8]
    step_row = side[5:6]
    skip_row = side[6:7]

    xz = nn(nh1_ext, w_in)
    nh1 = nh1_ext[HALO:]
    u, u_low, part = conv_call(xz, conv_mask, taps, w_state)
    pr = plane_sum(3, part)
    dt_low = pr[:, :R].astype(BF)
    pre = nn(dt_low, w_step) + step_row
    delta = jax.nn.softplus(pre)

    def replicated(block):
        return jnp.broadcast_to(block[:, :, None], (CH, N, 128)).reshape(CH * N, 128)

    brep = replicated(pr[:, R : R + N])
    crep = replicated(pr[:, R + N :])
    sum_delta = jnp.sum(delta, axis=0, keepdims=True)

    def packed(state):
        return jnp.concatenate(
            [state, sum_delta, jnp.full((1, width), alive, F32), jnp.zeros((6, width), F32)], axis=0
        )

    end = scan_one(delta, u, a2, brep, first)
    (h_in,) = chain(4, T, False, packed(end), a2)
    y_scan, marks = scan_two(delta, u, a2, brep, crep, first, h_in)
    y = y_scan + skip_row * u
    zg = xz[HALO:, width:]
    gate_s = jax.nn.sigmoid(zg)
    gated = (y * zg * gate_s).astype(BF)
    x1, nh2 = turn(5, nn(gated, w_mix).astype(BF), x0)

    a_one = nn(nh2, w_gu1)
    h_one = swiglu(a_one).astype(BF)
    x2, nh3, w_ao = turn(6, nn(h_one, w_d1).astype(BF), x1, jobs=(gather_job(T, ao_mine),))
    w_ao = w_ao.reshape(-1, D)

    qkv = nn(nh3, w_qkv)
    q, k_all, v_all, gl4 = keys_call(7, T, hops, qkv, cosine, sine, cotangent[0])
    o, lse = attend(q, k_all, v_all, bias)
    x3, nh4 = turn(8, nn(o, w_ao).astype(BF), x2)

    a_two = nn(nh4, w_gu2)
    h_two = swiglu(a_two).astype(BF)
    last_part = nn(h_two, w_d2).astype(BF)

    g4 = cotangent[0].astype(F32)
    dw_d2 = tn(h_two, gl4).astype(BF)
    da_two = swiglu_back(a_two, nt(gl4, w_d2))
    part, dw_gu2 = together(nt(da_two, w_gu2).astype(BF), tn(nh4, da_two).astype(BF))
    raw_gu2 = scatter_tc(dw_gu2)
    g3, gl3 = turn(10, part, x3, g4)

    do, dw_ao = together(nt(gl3, w_ao).astype(BF), tn(o, gl3).astype(BF))
    dq, dk, dv = attend_back(q, k_all, v_all, bias, lse, do)
    dq, last_part, raw_gu2 = together(dq, last_part, raw_gu2)
    dqkv, final = keys_back_call(
        11, T, hops, dq, dk, dv, cosine, sine, jobs=(sum_job(last_part, x3, F32),)
    )
    dqkv, dw_d2 = together(dqkv, dw_d2)
    grad_d2 = scatter_tc(dw_d2)
    part, dw_qkv = together(nt(dqkv, w_qkv).astype(BF), tn(nh3, dqkv).astype(BF))
    raw_qkv = scatter_tc(dw_qkv)
    g2, gl2, raw_ao = turn(12, part, x2, g3, jobs=(scatter_job(T, dw_ao),))

    da_one, dw_d1 = together(swiglu_back(a_one, nt(gl2, w_d1)), tn(h_one, gl2).astype(BF))
    part, dw_gu1, grad_d2 = together(nt(da_one, w_gu1).astype(BF), tn(nh2, da_one).astype(BF), grad_d2)
    raw_gu1 = scatter_tc(dw_gu1)
    grad_d1 = scatter_tc(dw_d1)
    g1, gl1 = turn(13, part, x1, g2)
    gl1, raw_qkv = together(gl1, raw_qkv)

    dgate = nt(gl1, w_mix)
    dy = dgate * zg * gate_s
    dz_low = (dgate * y * gate_s * (1.0 + zg * (1.0 - gate_s))).astype(BF)
    dy, dw_mix, dw_z = together(dy, tn(gated, gl1).astype(BF), tn(nh1, dz_low).astype(BF))
    grad_mix = scatter_tc(dw_mix)
    begin = scan_three(delta, dy, a2, crep, first)
    g_in, gu2_b, qkv_b = chain(
        14, T, True, packed(begin), a2, jobs=(spread_job(True, (blocks(raw_gu2), blocks(raw_qkv))),)
    )
    g_in, grad_d1 = together(g_in, grad_d1)
    ddelta, du_scan, db, dc_mat, ga = scan_four(
        delta, u, dy, skip_row, a2, brep, crep, first, marks, g_in
    )
    dpre = ddelta * jax.nn.sigmoid(pre)
    dpre_low = dpre.astype(BF)
    part_back = jnp.concatenate(
        [
            nt(dpre_low, w_step),
            jnp.sum(db, axis=1).reshape(CH, N),
            jnp.sum(dc_mat, axis=1).reshape(CH, N),
        ],
        axis=1,
    )
    part_back, raw_gu1, dw_z = together(part_back, raw_gu1, dw_z)
    raw_z = scatter_tc(dw_z)
    dpr_low = plane_sum(15, part_back).astype(BF)
    du = du_scan + nt(dpr_low, w_state)
    dxs_ext, conv_grads = conv_back_call(xz, conv_mask, taps, du)
    rim = rim_back(16, T, dxs_ext[8:16])
    dxs_low = jnp.concatenate(
        [dxs_ext[HALO : HALO + CH - 8], dxs_ext[HALO + CH - 8 :] + rim], axis=0
    ).astype(BF)
    dxz = jnp.concatenate([dxs_low, dz_low], axis=1)
    dxz, dw_x, grad_mix, raw_ao = together(dxz, tn(nh1, dxs_low).astype(BF), grad_mix, raw_ao)
    raw_x = scatter_tc(dw_x)
    small = jnp.concatenate(
        [
            tn(u_low, dpr_low),
            tn(dpre_low, dt_low),
            ga.T,
            conv_grads[:5].T,
            jnp.sum(dpre, axis=0)[:, None],
            jnp.sum(dy * u, axis=0)[:, None],
        ],
        axis=1,
    )
    small = jnp.pad(small, ((0, 0), (0, 256 - used))).astype(BF).reshape(2 * T, CB, 256)
    grad_x, small, gu1_b, grad_n4, grad_gu2, grad_n3, grad_qkv = turn(
        17, nt(dxz, w_in).astype(BF), x0, g1, gather=False,
        jobs=(scatter_job(T, small.reshape(width, 256)), spread_job(True, (blocks(raw_gu1),)),
            finish_job((gu2_b,), gate_up_two, norm_ffn_two, chunks[3]),
            finish_job((qkv_b,), qkv_proj, norm_attn, chunks[2]),
        ),
    )
    raw_z, grad_x = together(raw_z, grad_x)
    grad_x = g1 + grad_x
    final = final.astype(BF)

    def scaled(value, gain):
        return value.astype(F32) * gain.astype(F32)[:, None]

    grad_gu2, grad_qkv = scaled(grad_gu2, norm_ffn_two), scaled(grad_qkv, norm_attn)
    z_b, grad_n2, grad_gu1 = run_jobs(
        22, spread_job(True, (blocks(raw_z),)),
        finish_job((gu1_b,), gate_up_one, norm_ffn_one, chunks[1]),
    )
    at = NR + R + N
    small_grads = (
        small[:, at : at + 4].T,
        small[:, at + 4],
        small[:, :NR],
        small[:, NR : NR + R].T,
        small[:, at + 5],
        small[:, NR + R : at],
        small[:, at + 6],
    )
    grad_gu1 = scaled(grad_gu1, norm_ffn_one)
    grad_n2, grad_n3, grad_n4 = grad_n2[:, 0], grad_n3[:, 0], grad_n4[:, 0]
    raw_x, z_b, small_grads = together(raw_x, z_b, small_grads)
    (x_b,) = run_jobs(20, spread_job(True, (blocks(raw_x),)))
    grad_ao = lax.ppermute(raw_ao.astype(BF), ("t", "p", "c"), [(b, a) for a, b in pairs]).astype(F32)

    grad_n1, grad_in = finish((x_b, z_b), in_proj, norm_mixer, chunks[0])
    return (
        final[None],
        grad_x[None],
        grad_n1,
        grad_in,
        *small_grads,
        grad_mix.astype(F32),
        grad_n2,
        grad_gu1,
        grad_d1.astype(F32),
        grad_n3,
        grad_qkv,
        grad_ao,
        grad_n4,
        grad_gu2,
        grad_d2.astype(F32),
    )


def solution(mesh):
    chunks = mesh.shape["seq"] // W
    view = Mesh(mesh.devices.reshape(chunks, W, mesh.shape["fsdp"]), ("t", "p", "c"))
    every = ("t", "p", "c")
    tokens = P("c", ("t", "p"), None)
    vector, rows, cols = P(every), P(every, None), P(None, every)
    placed = (
        tokens, P("c", ("t", "p")), tokens,
        vector, rows, cols, vector, rows, cols, vector, rows, vector, rows,
        vector, rows, rows, vector, rows, rows, vector, rows, rows,
    )
    return jax.shard_map(
        local,
        mesh=view,
        in_specs=placed,
        out_specs=(tokens, tokens) + placed[3:],
        check_vma=False,
    )
```

```python
import functools
import math

import jax
import jax.numpy as jnp
from jax import lax
from jax.experimental import pallas as pl
from jax.experimental.pallas import tpu as pltpu
from jax.sharding import Mesh
from jax.sharding import PartitionSpec as P

W = 4
H = 12
HD = 128
WIN = 2048
SEQ_MAX = 8192
EPS = 1e-05
NEG = -1e30
BIG = 1e30
LOG2E = 1.4426950408889634
BF = jnp.bfloat16
F32 = jnp.float32
MESH = pl.DeviceIdType.MESH
HALO = 16
SUB = 64
MIB = 1 << 20


def vmem():
    return pl.BlockSpec(memory_space=pltpu.VMEM)


def hbm():
    return pl.BlockSpec(memory_space=pl.ANY)


def smem():
    return pl.BlockSpec(memory_space=pltpu.SMEM)


def here():
    return lax.axis_index("t"), lax.axis_index("p"), lax.axis_index("c")


def greet(device):
    pl.semaphore_signal(
        pltpu.get_barrier_semaphore(), inc=1, device_id=device, device_id_type=MESH
    )


def arrive(count):
    pl.semaphore_wait(pltpu.get_barrier_semaphore(), count)


def arrive_some(count):
    @pl.when(count > 0)
    def _():
        arrive(count)


def remote(src, dst, send, recv, device):
    return pltpu.make_async_remote_copy(
        src_ref=src,
        dst_ref=dst,
        send_sem=send,
        recv_sem=recv,
        device_id=device,
        device_id_type=MESH,
    )


def flip(p, d):
    return lax.bitwise_xor(p, d)


def dma(*shape):
    return pltpu.SemaphoreType.DMA(shape)


def talk(cid, limit=40):
    return pltpu.CompilerParams(
        collective_id=cid, has_side_effects=True, vmem_limit_bytes=limit * MIB
    )


def alone(limit=56):
    return pltpu.CompilerParams(vmem_limit_bytes=limit * MIB)


def out(shape, dtype=F32):
    return jax.ShapeDtypeStruct(shape, dtype)


def unit(x):
    return x * lax.rsqrt(jnp.mean(x * x, axis=-1, keepdims=True) + EPS)


def column_blocks(w, gain, chunk, blocks):
    groups = w.shape[1] // (W * chunk)
    for q in range(W):
        pieces = [w[:, (k * W + q) * chunk : (k * W + q + 1) * chunk] for k in range(groups)]
        value = jnp.concatenate(pieces, axis=1) if groups > 1 else pieces[0]
        blocks[q] = (value.astype(F32) * gain).astype(BF)


def first_body(T, chunks, x, seg, state, rows_in, log_in, gains, *refs):
    n = len(chunks) - 1
    weights, refs = refs[: n + 1], refs[n + 1 :]
    nh, seg_out, par_out, w_in = refs[:4]
    dsts, refs = refs[4 : 4 + n], refs[4 + n :]
    win, srcs, par, refs = refs[0], refs[1 : n + 1], refs[n + 1], refs[n + 2 :]
    (nbuf, zbuf, s_n, r_n, s_h, r_h, s_s, r_s, s_p, r_p, s_w, r_w, s_z, r_z, s_c, r_c, s_l, s_o, r_o) = refs
    t, p, c = here()
    B = x.shape[0]
    count = 0
    for dt in range(T):
        tt = lax.rem(t + dt, T)
        for dp in range(W):
            pp = flip(p, dp)
            if dt or dp:
                greet((tt, pp, c))
                count += 1
            if dt == 0 or dp == 0:
                greet((tt, pp, 1 - c))
                count += 1
    column_blocks(weights[0], gains[:, 0:1], chunks[0], win)
    arrive(count)
    half = lax.div(p, 2)
    slot = lax.rem(p, 2) * 2 + c
    me = t * 2 + c

    def block(src, dst, send, recv, q):
        return remote(src.at[q], dst.at[slot], send.at[q], recv.at[slot], (t, q, half))

    def kept(src, dst, send, q):
        return pltpu.make_async_copy(src.at[q], dst.at[slot], send.at[q])

    def exchange(src, dst, send, recv):
        for q in range(W):
            mine = (p == q) & (half == c)

            @pl.when(jnp.logical_not(mine))
            def _():
                block(src, dst, send, recv, q).start()

            @pl.when(mine)
            def _():
                kept(src, dst, send, q).start()

    def exchanged(src, dst, send, recv, j):
        own = (half == c) & (slot == j)

        @pl.when(jnp.logical_not(own))
        def _():
            remote(src.at[0], dst.at[j], send.at[0], recv.at[j], (t, 0, half)).wait_recv()

    def sent(src, dst, send, recv):
        for q in range(W):
            mine = (p == q) & (half == c)

            @pl.when(jnp.logical_not(mine))
            def _():
                block(src, dst, send, recv, q).wait_send()

    landing = w_in.at[t * 2 + half]
    exchange(win, landing, s_w, r_w)
    nbuf[...] = unit(x[...].astype(F32)).astype(BF)
    zbuf[...] = jnp.zeros_like(zbuf)
    size = rows_in.shape[1]
    eye = (
        lax.broadcasted_iota(jnp.int32, (size, size), 0)
        == lax.broadcasted_iota(jnp.int32, (size, size), 1)
    ).astype(BF)
    lines = nt(eye, rows_in[...]).astype(BF)
    wide_at = state.shape[1]
    par[:, 0:wide_at] = state[...]
    par[:, wide_at:] = jnp.concatenate(
        [lines, log_in[...], jnp.zeros((size, 256 - wide_at - lines.shape[1] - log_in.shape[1]), BF)],
        axis=1,
    )
    rows = pl.ds(pl.multiple_of(HALO + p * B, HALO), B)
    copies = []
    for dt in range(T):
        for dc in range(2):
            if dt or dc:
                copies.append(
                    remote(
                        par, par_out.at[me], s_p.at[dt, dc], r_p.at[dt, dc],
                        (lax.rem(t + dt, T), p, flip(c, dc)),
                    )
                )
    for d in range(1, W):
        copies.append(remote(nbuf, nh.at[rows], s_n.at[d], r_n.at[d], (t, flip(p, d), c)))
    for dt in range(T):
        for dp in range(W):
            if dt or dp:
                copies.append(
                    remote(
                        seg, seg_out.at[t * W + p], s_s.at[dt, dp], r_s.at[dt, dp],
                        (lax.rem(t + dt, T), flip(p, dp), c),
                    )
                )
    copies += [
        pltpu.make_async_copy(nbuf, nh.at[rows], s_l.at[0]),
        pltpu.make_async_copy(par, par_out.at[me], s_l.at[1]),
        pltpu.make_async_copy(seg, seg_out.at[t * W + p], s_l.at[2]),
    ]
    for copy in copies:
        copy.start()
    last = (p == W - 1) & (t < T - 1)
    tail = nbuf.at[pl.ds(B - HALO, HALO)]
    head = nh.at[pl.ds(0, HALO)]

    def rim(q):
        return remote(tail, head, s_h.at[q], r_h, (lax.rem(t + 1, T), q, c))

    @pl.when(last)
    def _():
        for q in range(W):
            rim(q).start()

    @pl.when(t == 0)
    def _():
        clear = pltpu.make_async_copy(zbuf, head, s_l.at[3])
        clear.start()
        clear.wait()

    for i in range(n):
        column_blocks(weights[i + 1], gains[:, i + 1 : i + 2], chunks[i + 1], srcs[i])
        exchange(srcs[i], dsts[i], s_o.at[i], r_o.at[i])

    def on(way, d, j):
        step = 1 - 2 * way
        source = lax.rem(t - step * d + T, T) * 2 + c
        part = w_in.at[source, j]
        return remote(
            part, part, s_z.at[way, d, j], r_z.at[way, d + 1, j], (lax.rem(t + step + T, T), p, c)
        )

    def came(way, d, j):
        step = 1 - 2 * way
        part = w_in.at[lax.rem(t - step * d + T, T) * 2 + c, j]
        return remote(part, part, s_z.at[way, d, j], r_z.at[way, d, j], (lax.rem(t + step + T, T), p, c))

    def across(way, d, j):
        step = 1 - 2 * way
        part = w_in.at[lax.rem(t - step * d + T, T) * 2 + c, j]
        return remote(part, part, s_c.at[way, d, j], r_c.at[way, d, j], (t, p, 1 - c))

    def crossed(way, d, j):
        step = 1 - 2 * way
        part = w_in.at[lax.rem(t - step * d + T, T) * 2 + 1 - c, j]
        return remote(part, part, s_c.at[way, d, j], r_c.at[way, d, j], (t, p, 1 - c))

    def goes(way, d):
        if way == 0:
            return (t >= d) & (t < T - 1)
        return (t + d < T) & (t > 0)

    def arrives(way, d):
        return (t >= d) if way == 0 else (t + d < T)

    for j in range(W):
        mine = (half == c) & (slot == j)

        @pl.when(mine)
        def _():
            for q in range(W):

                @pl.when(p == q)
                def _():
                    kept(win, landing, s_w, q).wait()

        exchanged(win, w_in.at[me], s_w, r_w, j)
        across(0, 0, j).start()
        for way in range(2):

            @pl.when(goes(way, 0))
            def _():
                on(way, 0, j).start()

    for d in range(1, T):
        for j in range(W):
            for way in range(2):

                @pl.when(arrives(way, d))
                def _():
                    came(way, d, j).wait_recv()
                    across(way, d, j).start()

                @pl.when(goes(way, d))
                def _():
                    on(way, d, j).start()

    for copy in copies:
        copy.wait()

    @pl.when(last)
    def _():
        for q in range(W):
            rim(q).wait_send()

    @pl.when(t > 0)
    def _():
        rim(0).wait_recv()

    sent(win, landing, s_w, r_w)
    for i in range(n):
        sent(srcs[i], dsts[i], s_o.at[i], r_o.at[i])
        for q in range(W):
            mine = (p == q) & (half == c)

            @pl.when(mine)
            def _():
                kept(srcs[i], dsts[i], s_o.at[i], q).wait()

        for j in range(W):
            exchanged(srcs[i], dsts[i], s_o.at[i], r_o.at[i], j)
    for d in range(T):
        for j in range(W):
            for way in range(2):
                if d or way == 0:

                    @pl.when(arrives(way, d))
                    def _():
                        across(way, d, j).wait_send()
                        crossed(way, d, j).wait_recv()

                @pl.when(goes(way, d))
                def _():
                    on(way, d, j).wait_send()


def first_call(T, x, seg, state, rows_in, log_in, gains, weights, chunks):
    B, D = x.shape
    n = len(weights) - 1
    blocks = [(W, w.shape[0], w.shape[1] // W) for w in weights]
    return pl.pallas_call(
        functools.partial(first_body, T, chunks),
        out_shape=(
            out((HALO + W * B, D), BF),
            out((W * T,) + seg.shape, jnp.int32),
            out((2 * T, state.shape[0], 256), BF),
            out((2 * T,) + blocks[0], BF),
        )
        + tuple(out(b, BF) for b in blocks[1:]),
        in_specs=[vmem(), hbm()] + [vmem()] * (5 + n),
        out_specs=(hbm(),) * (4 + n),
        scratch_shapes=[pltpu.VMEM(b, BF) for b in blocks]
        + [
            pltpu.VMEM((state.shape[0], 256), BF),
            pltpu.VMEM((B, D), BF),
            pltpu.VMEM((HALO, D), BF),
            dma(W), dma(W), dma(W), pltpu.SemaphoreType.DMA,
            dma(T, W), dma(T, W), dma(T, 2), dma(T, 2), dma(W), dma(W),
            dma(2, T, W), dma(2, T + 1, W), dma(2, T, W), dma(2, T, W), dma(4),
            dma(n, W), dma(n, W),
        ],
        compiler_params=talk(0),
        name="first",
    )(x, seg, state, rows_in, log_in, gains, *weights)


class Job:
    def __init__(self, build, inputs, in_specs, shapes, specs, scratch):
        self.build, self.inputs, self.in_specs = build, tuple(inputs), list(in_specs)
        self.shapes, self.specs, self.scratch = tuple(shapes), tuple(specs), list(scratch)


def take(refs, count):
    head = refs[:count]
    del refs[:count]
    return head


def started(jobs, ins, outs, scratch):
    made = []
    for job in jobs:
        made.append(
            job.build(
                take(ins, len(job.inputs)), take(outs, len(job.shapes)), take(scratch, len(job.scratch))
            )
        )
    return made


def spread_build(n, back):
    def build(srcs, dsts, sems):
        s_w, r_w = sems
        t, p, c = here()
        half = lax.div(p, 2)
        pair = lax.rem(p, 2) * 2 + c
        both = half == c

        def there(q):
            if back:
                return (t, c * 2 + q // 2, jnp.int32(q % 2))
            return (t, jnp.int32(q), half)

        def comes(j):
            if back:
                return (t, jnp.int32(j), half)
            return (t, c * 2 + j // 2, jnp.int32(j % 2))

        slot = p if back else pair

        def own(q):
            return both & ((pair == q) if back else (p == q))

        def from_me(q):
            return both & ((p == q) if back else (pair == q))

        def away(a, q):
            return remote(
                srcs[a].at[q], dsts[a].at[slot], s_w.at[a, q], r_w.at[a, slot], there(q)
            )

        def kept(a, q):
            return pltpu.make_async_copy(srcs[a].at[q], dsts[a].at[slot], s_w.at[a, q])

        for q in range(W):
            source = comes(q)

            @pl.when(jnp.logical_not(from_me(q)))
            def _():
                greet(source)

        def begin():
            for a in range(n):
                for q in range(W):

                    @pl.when(jnp.logical_not(own(q)))
                    def _():
                        away(a, q).start()

                    @pl.when(own(q))
                    def _():
                        kept(a, q).start()

        def end():
            for a in range(n):
                for q in range(W):

                    @pl.when(jnp.logical_not(own(q)))
                    def _():
                        away(a, q).wait_send()

                    @pl.when(own(q))
                    def _():
                        kept(a, q).wait()

                    @pl.when(jnp.logical_not(from_me(q)))
                    def _():
                        remote(
                            srcs[a].at[q], dsts[a].at[q], s_w.at[a, q], r_w.at[a, q], there(q)
                        ).wait_recv()

        return W - both.astype(jnp.int32), begin, end

    return build


def spread_job(back, arrays):
    n = len(arrays)
    return Job(
        spread_build(n, back), arrays, [hbm()] * n,
        [out(a.shape, a.dtype) for a in arrays], [hbm()] * n, [dma(n, W), dma(n, W)],
    )


def finish_body(n, chunk, scaled, *refs):
    blocks, (w, gain, total, o) = refs[:n], refs[n:]
    acc = jnp.zeros((w.shape[0], 1), F32)
    at = 0
    for b in blocks:
        for k in range(b.shape[2] // chunk):
            pieces = [b[q, :, k * chunk : (k + 1) * chunk] for q in range(W)]
            value = jnp.concatenate(pieces, axis=1).astype(F32)
            cut = pl.ds(at, W * chunk)
            acc = acc + jnp.sum(w[:, cut].astype(F32) * value, axis=1, keepdims=True)
            o[:, cut] = value * gain[...] if scaled else value.astype(BF)
            at += W * chunk
    total[...] = jnp.broadcast_to(acc, total.shape)


def finish_job(blocks, w, gain, chunk, scaled=False):
    rows = w.shape[0]
    n = len(blocks)

    def build(ins, outs, scratch):
        return 0, lambda: finish_body(n, chunk, scaled, *ins, *outs), lambda: None

    return Job(
        build, tuple(blocks) + (w, gain.astype(F32).reshape(rows, 1)), [vmem()] * (n + 2),
        [out((rows, 128)), out(w.shape, F32 if scaled else BF)], [vmem(), vmem()], [],
    )


def finish(blocks, w, gain, chunk):
    job = finish_job(blocks, w, gain, chunk, True)
    total, grad = pl.pallas_call(
        functools.partial(finish_body, len(blocks), chunk, True),
        out_shape=job.shapes,
        in_specs=job.in_specs,
        out_specs=job.specs,
        compiler_params=alone(),
        name="finish",
    )(*job.inputs)
    return total[:, 0], grad


def jobs_body(counts, jobs, *refs):
    refs = list(refs)
    ins, outs = take(refs, counts[0]), take(refs, counts[1])
    made = started(jobs, ins, outs, refs)
    arrive(sum(m[0] for m in made))
    for m in made:
        m[1]()
    for m in made:
        m[2]()


def run_jobs(cid, *jobs):
    inputs = sum((j.inputs for j in jobs), ())
    shapes = sum((j.shapes for j in jobs), ())
    return pl.pallas_call(
        functools.partial(jobs_body, (len(inputs), len(shapes)), jobs),
        out_shape=shapes,
        in_specs=sum((j.in_specs for j in jobs), []),
        out_specs=sum((j.specs for j in jobs), ()),
        scratch_shapes=sum((j.scratch for j in jobs), []),
        compiler_params=talk(cid),
        name="jobs%d" % cid,
    )(*inputs)


def plane_sum_body(x, o, sb, recv, ss, rs):
    t, p, c = here()
    for d in range(1, W):
        greet((t, flip(p, d), c))
    sb[...] = x[...].astype(BF)
    arrive(W - 1)
    copies = [
        remote(sb, recv.at[d - 1], ss.at[d - 1], rs.at[d - 1], (t, flip(p, d), c))
        for d in range(1, W)
    ]
    for copy in copies:
        copy.start()
    for copy in copies:
        copy.wait()
    total = x[...]
    for d in range(W - 1):
        total = total + recv[d].astype(F32)
    o[...] = total


def plane_sum(cid, x):
    return pl.pallas_call(
        plane_sum_body,
        out_shape=out(x.shape),
        in_specs=[vmem()],
        out_specs=vmem(),
        scratch_shapes=[
            pltpu.VMEM(x.shape, BF),
            pltpu.VMEM((W - 1,) + x.shape, BF),
            dma(W - 1),
            dma(W - 1),
        ],
        compiler_params=talk(cid),
        name="plane_sum%d" % cid,
    )(x)


def gather_job(T, piece):
    def build(ins, outs, sems):
        (src,), (dst,) = ins, outs
        s_z, r_z, s_c, r_c, s_l = sems
        t, p, c = here()

        def part(dt, core):
            return dst.at[lax.rem(t - dt + T, T) * 2 + core]

        def out_to(dt):
            return remote(src, part(0, c), s_z.at[dt], r_z.at[dt], (lax.rem(t + dt, T), p, c))

        def across(dt):
            return remote(
                src if dt == 0 else part(dt, c), part(dt, c), s_c.at[dt], r_c.at[dt], (t, p, 1 - c)
            )

        keep = pltpu.make_async_copy(src, part(0, c), s_l)
        for dt in range(1, T):
            greet((lax.rem(t + dt, T), p, c))
        greet((t, p, 1 - c))

        def begin():
            for dt in range(1, T):
                out_to(dt).start()
            across(0).start()
            keep.start()

        def end():
            for dt in range(1, T):
                out_to(dt).wait_recv()
                across(dt).start()
            keep.wait()
            for dt in range(T):
                across(dt).wait_send()
                other = part(dt, 1 - c)
                remote(other, other, s_c.at[dt], r_c.at[dt], (t, p, 1 - c)).wait_recv()
            for dt in range(1, T):
                out_to(dt).wait_send()

        return T, begin, end

    return Job(
        build, [piece], [hbm()], [out((2 * T,) + piece.shape, BF)], [hbm()],
        [dma(T), dma(T), dma(T), dma(T), pltpu.SemaphoreType.DMA],
    )


def scatter_job(T, grad):
    grad = grad.reshape(2 * T, -1, grad.shape[-1])

    def build(ins, outs, scratch):
        (src,), (dst,) = ins, outs
        mine, other, recv, s_z, r_z, s_c, r_c, s_l = scratch
        t, p, c = here()

        def at(dt):
            return lax.rem(t + dt, T)

        def across(dt):
            return remote(
                src.at[at(dt) * 2 + 1 - c], other.at[dt], s_c.at[dt], r_c.at[dt], (t, p, 1 - c)
            )

        def load(dt):
            return pltpu.make_async_copy(src.at[at(dt) * 2 + c], mine.at[dt], s_l.at[dt])

        def out_to(dt):
            return remote(mine.at[dt], recv.at[dt - 1], s_z.at[dt], r_z.at[dt], (at(dt), p, c))

        order = list(range(1, T)) + [0]
        for dt in range(1, T):
            greet((at(dt), p, c))
        greet((t, p, 1 - c))

        def begin():
            for dt in order:
                across(dt).start()
                load(dt).start()
            for dt in order[:-1]:
                across(dt).wait_recv()
                load(dt).wait()
                mine[dt] = (mine[dt].astype(F32) + other[dt].astype(F32)).astype(BF)
                out_to(dt).start()

        def end():
            across(0).wait_recv()
            load(0).wait()
            total = mine[0].astype(F32) + other[0].astype(F32)
            for dt in range(1, T):
                out_to(dt).wait_recv()
                total = total + recv[dt - 1].astype(F32)
            dst[...] = total
            for dt in range(T):
                across(dt).wait_send()
            for dt in range(1, T):
                out_to(dt).wait_send()

        return T, begin, end

    shape = grad.shape[1:]
    return Job(
        build, [grad], [hbm()], [out(shape)], [vmem()],
        [
            pltpu.VMEM((T,) + shape, BF),
            pltpu.VMEM((T,) + shape, BF),
            pltpu.VMEM((T - 1,) + shape, BF),
            dma(T), dma(T), dma(T), dma(T), dma(T),
        ],
    )


def sum_job(part, x, dtype):
    B, D = x.shape

    def build(ins, outs, scratch):
        src, base = ins
        (o,) = outs
        own, recv, ss, rs, ls = scratch
        t, p, c = here()

        def copy(d):
            q = flip(p, d)
            return remote(
                src.at[pl.ds(pl.multiple_of(q * B, B), B)], recv.at[d - 1],
                ss.at[d - 1], rs.at[d - 1], (t, q, c),
            )

        local = pltpu.make_async_copy(src.at[pl.ds(pl.multiple_of(p * B, B), B)], own, ls)
        for d in range(1, W):
            greet((t, flip(p, d), c))

        def begin():
            for d in range(1, W):
                copy(d).start()
            local.start()

        def end():
            local.wait()
            total = base[...] + own[...].astype(F32)
            for d in range(1, W):
                copy(d).wait()
                total = total + recv[d - 1].astype(F32)
            o[...] = total.astype(o.dtype)

        return W - 1, begin, end

    return Job(
        build, [part, x], [hbm(), vmem()], [out((B, D), dtype)], [vmem()],
        [
            pltpu.VMEM((B, D), BF), pltpu.VMEM((W - 1, B, D), BF),
            dma(W - 1), dma(W - 1), pltpu.SemaphoreType.DMA,
        ],
    )


def turn_body(back, gather, parts, jobs, counts, *refs):
    refs = list(refs)
    ins, outs = take(refs, counts[0]), take(refs, counts[1])
    part, x = take(ins, 2)
    g = take(ins, 1)[0] if back and gather else None
    o = take(outs, 1)[0]
    gath = take(outs, 1)[0] if gather else None
    own, recv, sbuf, ss, rs, ls, ss2, rs2, ls2 = take(refs, 9)
    t, p, c = here()
    B = x.shape[0]
    rows = B // parts
    for d in range(1, W):
        greet((t, flip(p, d), c))
    made = started(jobs, ins, outs, refs)
    local = pltpu.make_async_copy(part.at[pl.ds(pl.multiple_of(p * B, B), B)], own, ls)
    local.start()
    arrive(sum((m[0] for m in made), W - 1))
    first = {}
    for k in range(parts):
        for d in range(1, W):
            q = flip(p, d)
            first[k, d] = remote(
                part.at[pl.ds(pl.multiple_of(q * B + k * rows, rows), rows)],
                recv.at[d - 1, pl.ds(k * rows, rows)],
                ss.at[d - 1, k],
                rs.at[d - 1, k],
                (t, q, c),
            )
            first[k, d].start()
    for m in made:
        m[1]()
    local.wait()
    later = []
    for k in range(parts):
        for d in range(1, W):
            first[k, d].wait_recv()
        cut = pl.ds(k * rows, rows)
        total = own[cut, :].astype(F32)
        for d in range(W - 1):
            total = total + recv[d, cut, :].astype(F32)
        value = x[cut, :]
        if back:
            r = lax.rsqrt(jnp.mean(value * value, axis=-1, keepdims=True) + EPS)
            hat = value * r
            new = r * (total - hat * jnp.mean(total * hat, axis=-1, keepdims=True))
            new = g[cut, :] + new if g is not None else new
        else:
            new = value + total
        o[cut, :] = new.astype(o.dtype)
        if gather:
            sbuf[cut, :] = (new if back else unit(new)).astype(BF)
            place = gath.at[pl.ds(pl.multiple_of(p * B + k * rows, rows), rows)]
            for d in range(1, W):
                later.append(
                    remote(sbuf.at[cut], place, ss2.at[d - 1, k], rs2.at[d - 1, k], (t, flip(p, d), c))
                )
            later.append(pltpu.make_async_copy(sbuf.at[cut], place, ls2.at[k]))
            for copy in later[-W:]:
                copy.start()
    for m in made:
        m[2]()
    for copy in first.values():
        copy.wait_send()
    for copy in later:
        copy.wait()


def turn(cid, part, x, g=None, gather=True, dtype=F32, parts=2, jobs=()):
    B, D = x.shape
    back = g is not None
    args = (part, x) + ((g,) if back and gather else ())
    in_specs = [hbm()] + [vmem()] * (len(args) - 1)
    shapes, specs = (out((B, D), dtype),), (vmem(),)
    if gather:
        shapes += (out((W * B, D), BF),)
        specs += (hbm(),)
    scratch = [
        pltpu.VMEM((B, D), BF),
        pltpu.VMEM((W - 1, B, D), BF),
        pltpu.VMEM((B, D), BF),
        dma(W - 1, parts), dma(W - 1, parts), pltpu.SemaphoreType.DMA,
        dma(W - 1, parts), dma(W - 1, parts), dma(parts),
    ]
    for job in jobs:
        args += job.inputs
        in_specs += job.in_specs
        shapes += job.shapes
        specs += job.specs
        scratch += job.scratch
    return pl.pallas_call(
        functools.partial(turn_body, back, gather, parts, jobs, (len(args), len(shapes))),
        out_shape=shapes,
        in_specs=in_specs,
        out_specs=specs,
        scratch_shapes=scratch,
        compiler_params=talk(cid),
        name="turn%d" % cid,
    )(*args)


def chain_body(T, back, jobs, counts, *refs):
    refs = list(refs)
    ins, outs = take(refs, counts[0]), take(refs, counts[1])
    v, a2 = take(ins, 2)
    (h,) = take(outs, 1)
    recv, ss, rs = take(refs, 3)
    t, p, c = here()
    sign = -1 if back else 1
    for k in range(1, T):
        source = t - sign * k

        @pl.when((source >= 0) & (source < T))
        def _():
            greet((lax.rem(source + T, T), p, c))

    made = started(jobs, ins, outs, refs)
    arrive_some(sum((m[0] for m in made), t if back else T - 1 - t))

    def send(k):
        to = lax.rem(t + sign * k + T, T)
        return remote(v, recv.at[k - 1], ss.at[k - 1], rs.at[k - 1], (to, p, c))

    for k in range(1, T):
        to = t + sign * k

        @pl.when((to >= 0) & (to < T))
        def _():
            send(k).start()

    for m in made:
        m[1]()
    h[...] = jnp.zeros_like(h)
    for k in range(T - 1, 0, -1):
        source = t - sign * k

        @pl.when((source >= 0) & (source < T))
        def _():
            send(k).wait_recv()
            decay = jnp.exp2(a2[...] * recv[k - 1, 16:17, :]) * recv[k - 1, 17:18, :]
            h[...] = recv[k - 1, 0:16, :] + decay * h[...]

    for k in range(1, T):
        to = t + sign * k

        @pl.when((to >= 0) & (to < T))
        def _():
            send(k).wait_send()

    for m in made:
        m[2]()


def chain(cid, T, back, v, a2, jobs=()):
    args, in_specs = (v, a2), [vmem(), vmem()]
    shapes, specs = (out(a2.shape),), (vmem(),)
    scratch = [pltpu.VMEM((T - 1,) + v.shape, F32), dma(T - 1), dma(T - 1)]
    for job in jobs:
        args += job.inputs
        in_specs += job.in_specs
        shapes += job.shapes
        specs += job.specs
        scratch += job.scratch
    return pl.pallas_call(
        functools.partial(chain_body, T, back, jobs, (len(args), len(shapes))),
        out_shape=shapes,
        in_specs=in_specs,
        out_specs=specs,
        scratch_shapes=scratch,
        compiler_params=talk(cid),
        name="chain%d" % cid,
    )(*args)


def rope(w, cosine, sine):
    return w * cosine + pltpu.roll(w, HD // 2, 1) * sine


def keys_body(T, hops, qkv, cosine, sine, ct, q, k_all, v_all, ct_out, ss, rs, s_g, r_g, s_l):
    t, p, c = here()
    CH = q.shape[0]
    width = q.shape[1]
    B = ct.shape[0]

    @pl.when(t > 0)
    def _():
        greet((lax.rem(t - 1 + T, T), p, c))

    for d in range(1, W):
        greet((t, flip(p, d), c))

    mine = pl.ds(hops * CH, CH)
    for h in range(width // HD):
        cols = pl.ds(h * HD, HD)
        k_all[mine, cols] = rope(
            qkv[:, pl.ds(width + h * HD, HD)], cosine[...], sine[...]
        ).astype(BF)
    v_all[mine, :] = qkv[:, pl.ds(2 * width, width)].astype(BF)

    @pl.when(t < T - 1)
    def _():
        arrive(W)

    @pl.when(t == T - 1)
    def _():
        arrive(W - 1)

    def send(a, d):
        ref = (k_all, v_all)[a]
        return remote(
            ref.at[pl.ds((hops - d + 1) * CH, CH)],
            ref.at[pl.ds((hops - d) * CH, CH)],
            ss.at[a, d - 1],
            rs.at[a, d - 1],
            (lax.rem(t + 1, T), p, c),
        )

    for d in range(1, hops + 1):
        goes = (t < T - 1) & (t >= d - 1)

        @pl.when(goes)
        def _():
            send(0, d).start()
            send(1, d).start()

        if d == 1:
            rows = ct_out.at[pl.ds(pl.multiple_of(p * B, B), B)]
            copies = [
                remote(ct, rows, s_g.at[e], r_g.at[e], (t, flip(p, e), c)) for e in range(1, W)
            ] + [pltpu.make_async_copy(ct, rows, s_l)]
            for copy in copies:
                copy.start()
            for h in range(width // HD):
                cols = pl.ds(h * HD, HD)
                q[:, cols] = rope(qkv[:, cols], cosine[...], sine[...]).astype(BF)

        @pl.when(t < d)
        def _():
            k_all[pl.ds((hops - d) * CH, CH), :] = jnp.zeros((CH, width), BF)
            v_all[pl.ds((hops - d) * CH, CH), :] = jnp.zeros((CH, width), BF)

        @pl.when(t >= d)
        def _():
            send(0, d).wait_recv()
            send(1, d).wait_recv()

    for d in range(1, hops + 1):
        goes = (t < T - 1) & (t >= d - 1)

        @pl.when(goes)
        def _():
            send(0, d).wait_send()
            send(1, d).wait_send()

    for copy in copies:
        copy.wait()


def keys_call(cid, T, hops, qkv, cosine, sine, ct):
    CH = qkv.shape[0]
    width = qkv.shape[1] // 3
    return pl.pallas_call(
        functools.partial(keys_body, T, hops),
        out_shape=(
            out((CH, width), BF),
            out(((hops + 1) * CH, width), BF),
            out(((hops + 1) * CH, width), BF),
            out((W * ct.shape[0], ct.shape[1]), BF),
        ),
        in_specs=[vmem()] * 3 + [hbm()],
        out_specs=(vmem(),) * 3 + (hbm(),),
        scratch_shapes=[
            dma(2, hops), dma(2, hops), dma(W), dma(W), pltpu.SemaphoreType.DMA,
        ],
        compiler_params=talk(cid),
        name="keys",
    )(qkv, cosine, sine, ct)


def keys_back_body(T, hops, jobs, counts, *refs):
    refs = list(refs)
    ins, outs = take(refs, counts[0]), take(refs, counts[1])
    dq, dk, dv, cosine, sine = take(ins, 5)
    (dqkv,) = take(outs, 1)
    sb, recv, ss, rs = take(refs, 4)
    t, p, c = here()
    CH = dq.shape[0]
    width = dq.shape[1]

    @pl.when(t < T - 1)
    def _():
        greet((lax.rem(t + 1, T), p, c))

    made = started(jobs, ins, outs, refs)
    extra = sum(m[0] for m in made)

    def send(a, d):
        return remote(
            sb.at[a, d - 1],
            recv.at[a, d - 1],
            ss.at[a, d - 1],
            rs.at[a, d - 1],
            (lax.rem(t - 1 + T, T), p, c),
        )

    for d in range(hops, 0, -1):
        rows = pl.ds((hops - d) * CH, CH)
        k_sum = dk[rows, :]
        v_sum = dv[rows, :]
        if d == hops:
            sb[0, d - 1] = k_sum.astype(BF)
            sb[1, d - 1] = v_sum.astype(BF)

            @pl.when(t > 0)
            def _():
                arrive(1 + extra)

            if extra:

                @pl.when(t == 0)
                def _():
                    arrive(extra)

        else:

            @pl.when((t < T - 1) & (t >= d))
            def _():
                send(0, d + 1).wait_recv()
                send(1, d + 1).wait_recv()

            @pl.when((t == T - 1) | (t < d))
            def _():
                recv[0, d] = jnp.zeros((CH, width), BF)
                recv[1, d] = jnp.zeros((CH, width), BF)

            sb[0, d - 1] = (k_sum + recv[0, d].astype(F32)).astype(BF)
            sb[1, d - 1] = (v_sum + recv[1, d].astype(F32)).astype(BF)

        @pl.when(t >= d)
        def _():
            send(0, d).start()
            send(1, d).start()

        if d == hops:
            for m in made:
                m[1]()
            for h in range(width // HD):
                cols = pl.ds(h * HD, HD)
                dqkv[:, cols] = rope(dq[:, cols], cosine[...], -sine[...]).astype(BF)

    @pl.when(t < T - 1)
    def _():
        send(0, 1).wait_recv()
        send(1, 1).wait_recv()

    @pl.when(t == T - 1)
    def _():
        recv[0, 0] = jnp.zeros((CH, width), BF)
        recv[1, 0] = jnp.zeros((CH, width), BF)

    mine = pl.ds(hops * CH, CH)
    for h in range(width // HD):
        cols = pl.ds(h * HD, HD)
        k_sum = dk[mine, cols] + recv[0, 0, :, cols].astype(F32)
        v_sum = dv[mine, cols] + recv[1, 0, :, cols].astype(F32)
        dqkv[:, pl.ds(width + h * HD, HD)] = rope(k_sum, cosine[...], -sine[...]).astype(BF)
        dqkv[:, pl.ds(2 * width + h * HD, HD)] = v_sum.astype(BF)
    for m in made:
        m[2]()
    for d in range(hops, 0, -1):

        @pl.when(t >= d)
        def _():
            send(0, d).wait_send()
            send(1, d).wait_send()


def keys_back_call(cid, T, hops, dq, dk, dv, cosine, sine, jobs=()):
    CH, width = dq.shape
    args, in_specs = (dq, dk, dv, cosine, sine), [vmem()] * 5
    shapes, specs = (out((CH, 3 * width), BF),), (vmem(),)
    scratch = [
        pltpu.VMEM((2, hops, CH, width), BF), pltpu.VMEM((2, hops, CH, width), BF),
        dma(2, hops), dma(2, hops),
    ]
    for job in jobs:
        args += job.inputs
        in_specs += job.in_specs
        shapes += job.shapes
        specs += job.specs
        scratch += job.scratch
    return pl.pallas_call(
        functools.partial(keys_back_body, T, hops, jobs, (len(args), len(shapes))),
        out_shape=shapes,
        in_specs=in_specs,
        out_specs=specs,
        scratch_shapes=scratch,
        compiler_params=talk(cid, 48),
        name="keys_back",
    )(*args)


def rim_body(T, x, o, recv, ss, rs):
    t, p, c = here()

    @pl.when(t < T - 1)
    def _():
        greet((lax.rem(t + 1, T), p, c))

    def send():
        return remote(x, recv, ss, rs, (lax.rem(t + T - 1, T), p, c))

    @pl.when(t > 0)
    def _():
        arrive(1)
        send().start()
        send().wait_send()

    o[...] = jnp.zeros_like(o)

    @pl.when(t < T - 1)
    def _():
        send().wait_recv()
        o[...] = recv[...]


def rim_back(cid, T, x):
    return pl.pallas_call(
        functools.partial(rim_body, T),
        out_shape=out(x.shape),
        in_specs=[vmem()],
        out_specs=vmem(),
        scratch_shapes=[pltpu.VMEM(x.shape, F32), pltpu.SemaphoreType.DMA, pltpu.SemaphoreType.DMA],
        compiler_params=talk(cid),
        name="rim_back",
    )(x)


def conv_sum(xz, mask, taps, lo, size):
    width = taps.shape[1]
    total = jnp.broadcast_to(taps[4:5, :], (size, width))
    for j in range(4):
        rows = xz[pl.ds(lo + HALO - 3 + j, size), pl.ds(0, width)]
        total = total + taps[j : j + 1, :] * rows * mask[pl.ds(lo, size), j : j + 1]
    return total


def conv_body(xz, mask, taps, proj, u, u_low, part):
    CH = u.shape[0]
    step = min(CH, 128)
    for lo in range(0, CH, step):
        cut = pl.ds(lo, step)
        c = conv_sum(xz, mask, taps, lo, step)
        value = c / (1.0 + jnp.exp(-c))
        u[cut, :] = value
        low = value.astype(BF)
        u_low[cut, :] = low
        part[cut, :] = jnp.dot(low, proj[...], preferred_element_type=F32)


def conv_call(xz, mask, taps, proj):
    CH = mask.shape[0]
    width = taps.shape[1]
    return pl.pallas_call(
        conv_body,
        out_shape=(out((CH, width)), out((CH, width), BF), out((CH, proj.shape[1]))),
        in_specs=[vmem()] * 4,
        out_specs=(vmem(),) * 3,
        compiler_params=alone(),
        name="conv",
    )(xz, mask, taps, proj)


def conv_back_body(xz, mask, taps, du, dxs, grads):
    CH, width = du.shape
    step = min(CH, 128)
    dxs[...] = jnp.zeros_like(dxs)
    sums = [jnp.zeros((1, width), F32) for _ in range(5)]
    for lo in range(0, CH, step):
        c = conv_sum(xz, mask, taps, lo, step)
        s = 1.0 / (1.0 + jnp.exp(-c))
        dc = du[pl.ds(lo, step), :] * (s * (1.0 + c * (1.0 - s)))
        sums[4] = sums[4] + jnp.sum(dc, axis=0, keepdims=True)
        for j in range(4):
            rows = pl.ds(lo + HALO - 3 + j, step)
            live = dc * mask[pl.ds(lo, step), j : j + 1]
            sums[j] = sums[j] + jnp.sum(live * xz[rows, pl.ds(0, width)], axis=0, keepdims=True)
            dxs[rows, :] = dxs[rows, :] + live * taps[j : j + 1, :]
    grads[...] = jnp.zeros_like(grads)
    for j in range(5):
        grads[j : j + 1, :] = sums[j]


def conv_back_call(xz, mask, taps, du):
    CH, width = du.shape
    return pl.pallas_call(
        conv_back_body,
        out_shape=(out((HALO + CH, width)), out((8, width))),
        in_specs=[vmem()] * 4,
        out_specs=(vmem(),) * 2,
        compiler_params=alone(),
        name="conv_back",
    )(xz, mask, taps, du)


def wide(block, width):
    return jnp.concatenate([block] * (width // 128), axis=1) if width > 128 else block


def fold(block):
    total = block[:, 0:128]
    for lo in range(128, block.shape[1], 128):
        total = total + block[:, lo : lo + 128]
    return total


def scan_one_body(delta, u, a2, brep, first, end):
    CH, width = delta.shape
    decay = a2[...]

    def group(g, h):
        lo = pl.multiple_of(g * 8, 8)
        d8 = delta[pl.ds(lo, 8), :]
        du8 = d8 * u[pl.ds(lo, 8), :]
        for i in range(8):
            d = d8[i : i + 1, :] + first[lo + i]
            b = wide(brep[pl.ds(pl.multiple_of(g * 128 + i * 16, 16), 16), :], width)
            h = jnp.exp2(d * decay) * h + du8[i : i + 1, :] * b
        return h

    end[...] = lax.fori_loop(0, CH // 8, group, jnp.zeros(decay.shape, F32))


def scan_one(delta, u, a2, brep, first):
    return pl.pallas_call(
        scan_one_body,
        out_shape=out(a2.shape),
        in_specs=[vmem()] * 4 + [smem()],
        out_specs=vmem(),
        compiler_params=alone(),
        name="scan_one",
    )(delta, u, a2, brep, first)


def scan_two_body(delta, u, a2, brep, crep, first, h_in, y, marks):
    CH, width = delta.shape
    decay = a2[...]
    row = lax.broadcasted_iota(jnp.int32, (8, width), 0)

    def group(g, h):
        lo = pl.multiple_of(g * 8, 8)

        @pl.when(lax.rem(g, SUB // 8) == 0)
        def _():
            marks[pl.ds(pl.multiple_of(lax.div(g, SUB // 8) * 16, 16), 16), :] = h

        d8 = delta[pl.ds(lo, 8), :]
        du8 = d8 * u[pl.ds(lo, 8), :]
        y8 = jnp.zeros((8, width), F32)
        for i in range(8):
            at = pl.ds(pl.multiple_of(g * 128 + i * 16, 16), 16)
            d = d8[i : i + 1, :] + first[lo + i]
            h = jnp.exp2(d * decay) * h + du8[i : i + 1, :] * wide(brep[at, :], width)
            total = jnp.sum(h * wide(crep[at, :], width), axis=0, keepdims=True)
            y8 = jnp.where(row == i, total, y8)
        y[pl.ds(lo, 8), :] = y8
        return h

    lax.fori_loop(0, CH // 8, group, h_in[...])


def scan_two(delta, u, a2, brep, crep, first, h_in):
    CH, width = delta.shape
    return pl.pallas_call(
        scan_two_body,
        out_shape=(out((CH, width)), out((CH // SUB * 16, width))),
        in_specs=[vmem()] * 5 + [smem(), vmem()],
        out_specs=(vmem(),) * 2,
        compiler_params=alone(),
        name="scan_two",
    )(delta, u, a2, brep, crep, first, h_in)


def scan_three_body(delta, dy, a2, crep, first, start):
    CH, width = delta.shape
    decay = a2[...]

    def group(step, carry):
        g = CH // 8 - 1 - step
        lo = pl.multiple_of(g * 8, 8)
        d8 = delta[pl.ds(lo, 8), :]
        dy8 = dy[pl.ds(lo, 8), :]
        for i in range(7, -1, -1):
            at = pl.ds(pl.multiple_of(g * 128 + i * 16, 16), 16)
            d = d8[i : i + 1, :] + first[lo + i]
            lam = dy8[i : i + 1, :] * wide(crep[at, :], width) + carry
            carry = jnp.exp2(d * decay) * lam
        return carry

    start[...] = lax.fori_loop(0, CH // 8, group, jnp.zeros(decay.shape, F32))


def scan_three(delta, dy, a2, crep, first):
    return pl.pallas_call(
        scan_three_body,
        out_shape=out(a2.shape),
        in_specs=[vmem()] * 4 + [smem()],
        out_specs=vmem(),
        compiler_params=alone(),
        name="scan_three",
    )(delta, dy, a2, crep, first)


def scan_four_body(
    delta, u, dy, skip, a2, brep, crep, first, marks, g_in,
    ddelta, du_out, db, dc, ga, keep_a, keep_w,
):
    CH, width = delta.shape
    decay = a2[...]
    rate = decay * (1.0 / LOG2E)
    row = lax.broadcasted_iota(jnp.int32, (8, width), 0)
    per = SUB // 8

    def block(step, carried):
        blk = CH // SUB - 1 - step

        def forward(k, h):
            g = blk * per + k
            lo = pl.multiple_of(g * 8, 8)
            d8 = delta[pl.ds(lo, 8), :]
            du8 = d8 * u[pl.ds(lo, 8), :]
            for i in range(8):
                at = pl.ds(pl.multiple_of(g * 128 + i * 16, 16), 16)
                put = pl.ds(pl.multiple_of(k * 128 + i * 16, 16), 16)
                d = d8[i : i + 1, :] + first[lo + i]
                a = jnp.exp2(d * decay)
                keep_a[put, :] = a
                w = a * h
                keep_w[put, :] = w
                h = w + du8[i : i + 1, :] * wide(brep[at, :], width)
            return h

        lax.fori_loop(0, per, forward, marks[pl.ds(pl.multiple_of(blk * 16, 16), 16), :])

        def backward(back, state):
            carry, total_a = state
            k = per - 1 - back
            g = blk * per + k
            lo = pl.multiple_of(g * 8, 8)
            d8 = delta[pl.ds(lo, 8), :]
            u8 = u[pl.ds(lo, 8), :]
            du8 = d8 * u8
            dy8 = dy[pl.ds(lo, 8), :]
            s1 = jnp.zeros((8, width), F32)
            s2 = jnp.zeros((8, width), F32)
            for i in range(7, -1, -1):
                at = pl.ds(pl.multiple_of(g * 128 + i * 16, 16), 16)
                put = pl.ds(pl.multiple_of(k * 128 + i * 16, 16), 16)
                b = wide(brep[at, :], width)
                du = du8[i : i + 1, :]
                dyi = dy8[i : i + 1, :]
                w = keep_w[put, :]
                lam = dyi * wide(crep[at, :], width) + carry
                lw = lam * w
                s1 = jnp.where(row == i, jnp.sum(lam * b, axis=0, keepdims=True), s1)
                s2 = jnp.where(row == i, jnp.sum(lw * rate, axis=0, keepdims=True), s2)
                total_a = total_a + lw * d8[i : i + 1, :]
                dc[at, :] = fold((w + du * b) * dyi)
                db[at, :] = fold(lam * du)
                carry = keep_a[put, :] * lam
            ddelta[pl.ds(lo, 8), :] = s2 + u8 * s1
            du_out[pl.ds(lo, 8), :] = d8 * s1 + skip[0:1, :] * dy8
            return carry, total_a

        return lax.fori_loop(0, per, backward, carried)

    carry, total_a = lax.fori_loop(
        0, CH // SUB, block, (g_in[...], jnp.zeros(decay.shape, F32))
    )
    ga[...] = total_a * rate


def scan_four(delta, u, dy, skip, a2, brep, crep, first, marks, g_in):
    CH, width = delta.shape
    return pl.pallas_call(
        scan_four_body,
        out_shape=(
            out((CH, width)),
            out((CH, width)),
            out((CH * 16, 128)),
            out((CH * 16, 128)),
            out(a2.shape),
        ),
        in_specs=[vmem()] * 7 + [smem(), vmem(), vmem()],
        out_specs=(vmem(),) * 5,
        scratch_shapes=[pltpu.VMEM((SUB * 16, width), F32), pltpu.VMEM((SUB * 16, width), F32)],
        compiler_params=alone(),
        name="scan_four",
    )(delta, u, dy, skip, a2, brep, crep, first, marks, g_in)


def nt(a, b):
    return lax.dot_general(a, b, (((1,), (1,)), ((), ())), preferred_element_type=F32)


def tn(a, b):
    return lax.dot_general(a, b, (((0,), (0,)), ((), ())), preferred_element_type=F32)


def nn(a, b):
    return jnp.dot(a, b, preferred_element_type=F32)


def attend_body(q, k, v, bias, o, lse):
    s = nt(q[...], k[...]) * (HD**-0.5) + bias[...].astype(F32)
    top = jnp.max(s, axis=-1, keepdims=True)
    e = jnp.exp(s - top)
    total = jnp.sum(e, axis=-1, keepdims=True)
    o[...] = nn((e / total).astype(BF), v[...]).astype(BF)
    lse[...] = jnp.broadcast_to(top + jnp.log(total), lse.shape)


def attend(q, k, v, bias):
    CH, width = q.shape
    NK = k.shape[0]
    tq = min(CH, 256)
    return pl.pallas_call(
        attend_body,
        grid=(width // HD, CH // tq),
        out_shape=(out((CH, width), BF), out((CH, width))),
        in_specs=[
            pl.BlockSpec((tq, HD), lambda h, i: (i, h)),
            pl.BlockSpec((NK, HD), lambda h, i: (0, h)),
            pl.BlockSpec((NK, HD), lambda h, i: (0, h)),
            pl.BlockSpec((tq, NK), lambda h, i: (i, 0)),
        ],
        out_specs=(
            pl.BlockSpec((tq, HD), lambda h, i: (i, h)),
            pl.BlockSpec((tq, HD), lambda h, i: (i, h)),
        ),
        compiler_params=alone(),
        name="attend",
    )(q, k, v, bias)


def attend_back_body(q, k, v, bias, lse, do, dq, dk, dv):
    scale = HD**-0.5
    first = pl.program_id(1) == 0
    s = nt(q[...], k[...]) * scale + bias[...].astype(F32)
    prob = jnp.exp(s - lse[:, 0:1])
    dp = nt(do[...], v[...])
    rowdot = jnp.sum(prob * dp, axis=-1, keepdims=True)
    ds = (prob * (dp - rowdot)).astype(BF)
    dq[...] = nn(ds, k[...]) * scale
    add_k = tn(ds, q[...]) * scale
    add_v = tn(prob.astype(BF), do[...])

    @pl.when(first)
    def _():
        dk[...] = add_k
        dv[...] = add_v

    @pl.when(jnp.logical_not(first))
    def _():
        dk[...] += add_k
        dv[...] += add_v


def attend_back(q, k, v, bias, lse, do):
    CH, width = q.shape
    NK = k.shape[0]
    tq = min(CH, 256)
    rows = pl.BlockSpec((tq, HD), lambda h, i: (i, h))
    keys = pl.BlockSpec((NK, HD), lambda h, i: (0, h))
    return pl.pallas_call(
        attend_back_body,
        grid=(width // HD, CH // tq),
        out_shape=(out((CH, width)), out((NK, width)), out((NK, width))),
        in_specs=[rows, keys, keys, pl.BlockSpec((tq, NK), lambda h, i: (i, 0)), rows, rows],
        out_specs=(rows, keys, keys),
        compiler_params=alone(),
        name="attend_back",
    )(q, k, v, bias, lse, do)


def gather_tc(x):
    return lax.all_gather(x.reshape(-1, x.shape[-1]), ("t", "c"), axis=0, tiled=True)


def blocks(x):
    return x.reshape(W, x.shape[0] // W, x.shape[1])


def together(*values):
    return lax.optimization_barrier(values)


def scatter_tc(x):
    return lax.psum_scatter(x, ("t", "c"), scatter_dimension=0, tiled=True)


def swiglu(a):
    width = a.shape[1] // 2
    return jax.nn.silu(a[:, :width]) * a[:, width:]


def swiglu_back(a, dh):
    width = a.shape[1] // 2
    gate, up = a[:, :width], a[:, width:]
    s = jax.nn.sigmoid(gate)
    return jnp.concatenate([dh * up * (s * (1.0 + gate * (1.0 - s))), dh * gate * s], axis=1).astype(BF)


def local(
    inputs, segment_ids, cotangent, norm_mixer, in_proj, conv_weight, conv_bias, state_proj,
    step_proj, step_bias, decay_log, skip_gain, mixer_out, norm_ffn_one, gate_up_one, down_one,
    norm_attn, qkv_proj, attn_out, norm_ffn_two, gate_up_two, down_two,
):
    T = lax.axis_size("t")
    t, p, c = here()
    B, D = inputs.shape[1:]
    CH = W * B
    total = CH * T
    seq_len = min(SEQ_MAX, total)
    CB = conv_bias.shape[0]
    DI = CB * W * T * 2
    FB = down_one.shape[0]
    R = step_proj.shape[0]
    N = decay_log.shape[1]
    NR = state_proj.shape[1]
    width = CB * 2 * T
    heads = H // W * HD
    most = min(WIN, total // 2)
    hops = -(-(most - 1) // CH)

    used = NR + R + N + 7
    rows_in = jnp.concatenate(
        [step_proj, conv_weight, conv_bias[None], step_bias[None], skip_gain[None]]
        + [jnp.zeros((1, CB), BF)],
        axis=0,
    )
    gains = jnp.stack([norm_mixer, norm_ffn_one, norm_attn, norm_ffn_two], axis=1).astype(F32)
    chunks = (2 * CB, 2 * FB, heads, 2 * FB)
    seg8 = jnp.broadcast_to(segment_ids, (8, B))
    x0 = inputs[0].astype(F32)
    nh1_ext, seg_all, par_all, w_in, gu1_mine, qkv_mine, gu2_mine = first_call(
        T, inputs[0], seg8, state_proj, rows_in, decay_log, gains,
        (in_proj, gate_up_one, qkv_proj, gate_up_two), chunks,
    )
    w_in = w_in.reshape(D, -1)
    nh1_ext, attn_late = together(nh1_ext, attn_out)
    devices = 2 * W * T
    pairs = []
    for d in range(devices):
        rest = d % (2 * T)
        pairs.append((d, (rest // 2) * 2 * W + (d // (2 * T)) * 2 + rest % 2))
    ao_mine = lax.ppermute(attn_late, ("t", "p", "c"), pairs)
    w_mix = gather_tc(mixer_out)
    w_gu1 = gather_tc(gu1_mine)
    w_d1 = gather_tc(down_one)
    w_qkv = gather_tc(qkv_mine)
    w_gu2 = gather_tc(gu2_mine)
    w_d2 = gather_tc(down_two)

    seg = seg_all[:, 0, :].reshape(total)
    pos = t * CH + jnp.arange(CH, dtype=jnp.int32)
    padded = jnp.pad(seg, (max(hops * CH, HALO), 0), constant_values=-1)
    lead = max(hops * CH, HALO)
    near = lax.dynamic_slice(padded, (t * CH + lead - HALO,), (CH + HALO,))
    own_seg = near[HALO:]
    conv_mask = jnp.stack(
        [
            (near[HALO - 3 + j : HALO - 3 + j + CH] == own_seg) & ((pos - 3 + j) // seq_len == pos // seq_len)
            & (pos - 3 + j >= 0)
            for j in range(4)
        ]
        + [jnp.zeros((CH,), jnp.bool_)] * 4,
        axis=1,
    ).astype(F32)
    starts = (pos % seq_len == 0) | (near[HALO - 1 : HALO - 1 + CH] != own_seg)
    first = jnp.where(starts, BIG, 0.0).astype(F32)
    alive = jnp.where(jnp.any(starts), 0.0, 1.0).astype(F32)
    NK = (hops + 1) * CH
    key_seg = lax.dynamic_slice(padded, (t * CH + lead - hops * CH,), (NK,))
    key_pos = t * CH - hops * CH + jnp.arange(NK, dtype=jnp.int32)
    away = pos[:, None] - key_pos[None, :]
    allowed = (
        (key_pos[None, :] >= 0) & (away >= 0) & (away < WIN) & (key_seg[None, :] == own_seg[:, None])
        & (key_pos[None, :] // seq_len == (pos // seq_len)[:, None])
    )
    bias = jnp.where(allowed, 0.0, NEG).astype(BF)
    half = HD // 2
    inverse = jnp.exp(jnp.arange(half, dtype=F32) * (-math.log(10000.0) * 2.0 / HD))
    angles = (pos % seq_len).astype(F32)[:, None] * inverse[None, :]
    cos_half, sin_half = jnp.cos(angles), jnp.sin(angles)
    cosine = jnp.concatenate([cos_half, cos_half], axis=1)
    sine = jnp.concatenate([-sin_half, sin_half], axis=1)

    par_all = par_all.reshape(width, 256)
    w_state = par_all[:, :NR]
    w_step = par_all[:, NR : NR + R].T
    side = par_all[:, NR + R : NR + R + 8 + N].astype(F32).T
    a2 = -jnp.exp(side[8:]) * LOG2E
    taps = side[:8]
    step_row = side[5:6]
    skip_row = side[6:7]

    xz = nn(nh1_ext, w_in)
    nh1 = nh1_ext[HALO:]
    u, u_low, part = conv_call(xz, conv_mask, taps, w_state)
    pr = plane_sum(3, part)
    dt_low = pr[:, :R].astype(BF)
    pre = nn(dt_low, w_step) + step_row
    delta = jax.nn.softplus(pre)

    def replicated(block):
        return jnp.broadcast_to(block[:, :, None], (CH, N, 128)).reshape(CH * N, 128)

    brep = replicated(pr[:, R : R + N])
    crep = replicated(pr[:, R + N :])
    sum_delta = jnp.sum(delta, axis=0, keepdims=True)

    def packed(state):
        return jnp.concatenate(
            [state, sum_delta, jnp.full((1, width), alive, F32), jnp.zeros((6, width), F32)], axis=0
        )

    end = scan_one(delta, u, a2, brep, first)
    (h_in,) = chain(4, T, False, packed(end), a2)
    y_scan, marks = scan_two(delta, u, a2, brep, crep, first, h_in)
    y = y_scan + skip_row * u
    zg = xz[HALO:, width:]
    gate_s = jax.nn.sigmoid(zg)
    gated = (y * zg * gate_s).astype(BF)
    x1, nh2 = turn(5, nn(gated, w_mix).astype(BF), x0)

    a_one = nn(nh2, w_gu1)
    h_one = swiglu(a_one).astype(BF)
    x2, nh3, w_ao = turn(6, nn(h_one, w_d1).astype(BF), x1, jobs=(gather_job(T, ao_mine),))
    w_ao = w_ao.reshape(-1, D)

    qkv = nn(nh3, w_qkv)
    q, k_all, v_all, gl4 = keys_call(7, T, hops, qkv, cosine, sine, cotangent[0])
    o, lse = attend(q, k_all, v_all, bias)
    x3, nh4 = turn(8, nn(o, w_ao).astype(BF), x2)

    a_two = nn(nh4, w_gu2)
    h_two = swiglu(a_two).astype(BF)
    last_part = nn(h_two, w_d2).astype(BF)

    g4 = cotangent[0].astype(F32)
    dw_d2 = tn(h_two, gl4).astype(BF)
    da_two = swiglu_back(a_two, nt(gl4, w_d2))
    part, dw_gu2 = together(nt(da_two, w_gu2).astype(BF), tn(nh4, da_two).astype(BF))
    raw_gu2 = scatter_tc(dw_gu2)
    g3, gl3 = turn(10, part, x3, g4)

    do, dw_ao = together(nt(gl3, w_ao).astype(BF), tn(o, gl3).astype(BF))
    dq, dk, dv = attend_back(q, k_all, v_all, bias, lse, do)
    dq, last_part, raw_gu2 = together(dq, last_part, raw_gu2)
    dqkv, final = keys_back_call(
        11, T, hops, dq, dk, dv, cosine, sine, jobs=(sum_job(last_part, x3, F32),)
    )
    dqkv, dw_d2 = together(dqkv, dw_d2)
    grad_d2 = scatter_tc(dw_d2)
    part, dw_qkv = together(nt(dqkv, w_qkv).astype(BF), tn(nh3, dqkv).astype(BF))
    raw_qkv = scatter_tc(dw_qkv)
    g2, gl2, raw_ao = turn(12, part, x2, g3, jobs=(scatter_job(T, dw_ao),))

    da_one, dw_d1 = together(swiglu_back(a_one, nt(gl2, w_d1)), tn(h_one, gl2).astype(BF))
    part, dw_gu1, grad_d2 = together(nt(da_one, w_gu1).astype(BF), tn(nh2, da_one).astype(BF), grad_d2)
    raw_gu1 = scatter_tc(dw_gu1)
    grad_d1 = scatter_tc(dw_d1)
    g1, gl1 = turn(13, part, x1, g2)
    gl1, raw_qkv = together(gl1, raw_qkv)

    dgate = nt(gl1, w_mix)
    dy = dgate * zg * gate_s
    dz_low = (dgate * y * gate_s * (1.0 + zg * (1.0 - gate_s))).astype(BF)
    dy, dw_mix, dw_z = together(dy, tn(gated, gl1).astype(BF), tn(nh1, dz_low).astype(BF))
    grad_mix = scatter_tc(dw_mix)
    begin = scan_three(delta, dy, a2, crep, first)
    g_in, gu2_b, qkv_b = chain(
        14, T, True, packed(begin), a2, jobs=(spread_job(True, (blocks(raw_gu2), blocks(raw_qkv))),)
    )
    g_in, grad_d1 = together(g_in, grad_d1)
    ddelta, du_scan, db, dc_mat, ga = scan_four(
        delta, u, dy, skip_row, a2, brep, crep, first, marks, g_in
    )
    dpre = ddelta * jax.nn.sigmoid(pre)
    dpre_low = dpre.astype(BF)
    part_back = jnp.concatenate(
        [
            nt(dpre_low, w_step),
            jnp.sum(db, axis=1).reshape(CH, N),
            jnp.sum(dc_mat, axis=1).reshape(CH, N),
        ],
        axis=1,
    )
    part_back, raw_gu1, dw_z = together(part_back, raw_gu1, dw_z)
    raw_z = scatter_tc(dw_z)
    dpr_low = plane_sum(15, part_back).astype(BF)
    du = du_scan + nt(dpr_low, w_state)
    dxs_ext, conv_grads = conv_back_call(xz, conv_mask, taps, du)
    rim = rim_back(16, T, dxs_ext[8:16])
    dxs_low = jnp.concatenate(
        [dxs_ext[HALO : HALO + CH - 8], dxs_ext[HALO + CH - 8 :] + rim], axis=0
    ).astype(BF)
    dxz = jnp.concatenate([dxs_low, dz_low], axis=1)
    dxz, dw_x, grad_mix, raw_ao = together(dxz, tn(nh1, dxs_low).astype(BF), grad_mix, raw_ao)
    grad_ao = lax.ppermute(raw_ao.astype(BF), ("t", "p", "c"), [(b, a) for a, b in pairs]).astype(F32)
    dxz, grad_ao = together(dxz, grad_ao)
    raw_x = scatter_tc(dw_x)
    small = jnp.concatenate(
        [
            tn(u_low, dpr_low),
            tn(dpre_low, dt_low),
            ga.T,
            conv_grads[:5].T,
            jnp.sum(dpre, axis=0)[:, None],
            jnp.sum(dy * u, axis=0)[:, None],
        ],
        axis=1,
    )
    small = jnp.pad(small, ((0, 0), (0, 256 - used))).astype(BF).reshape(2 * T, CB, 256)
    grad_x, small, gu1_b, grad_n4, grad_gu2, grad_n3, grad_qkv = turn(
        17, nt(dxz, w_in).astype(BF), x0, g1, gather=False,
        jobs=(scatter_job(T, small.reshape(width, 256)), spread_job(True, (blocks(raw_gu1),)),
            finish_job((gu2_b,), gate_up_two, norm_ffn_two, chunks[3]),
            finish_job((qkv_b,), qkv_proj, norm_attn, chunks[2]),
        ),
    )
    raw_z, grad_x = together(raw_z, grad_x)
    grad_x = g1 + grad_x
    final = final.astype(BF)

    def scaled(value, gain):
        return value.astype(F32) * gain.astype(F32)[:, None]

    grad_gu2, grad_qkv = scaled(grad_gu2, norm_ffn_two), scaled(grad_qkv, norm_attn)
    z_b, grad_n2, grad_gu1 = run_jobs(
        22, spread_job(True, (blocks(raw_z),)),
        finish_job((gu1_b,), gate_up_one, norm_ffn_one, chunks[1]),
    )
    at = NR + R + N
    small_grads = (
        small[:, at : at + 4].T,
        small[:, at + 4],
        small[:, :NR],
        small[:, NR : NR + R].T,
        small[:, at + 5],
        small[:, NR + R : at],
        small[:, at + 6],
    )
    grad_gu1 = scaled(grad_gu1, norm_ffn_one)
    grad_n2, grad_n3, grad_n4 = grad_n2[:, 0], grad_n3[:, 0], grad_n4[:, 0]
    raw_x, z_b, small_grads = together(raw_x, z_b, small_grads)
    (x_b,) = run_jobs(20, spread_job(True, (blocks(raw_x),)))

    grad_n1, grad_in = finish((x_b, z_b), in_proj, norm_mixer, chunks[0])
    return (
        final[None],
        grad_x[None],
        grad_n1,
        grad_in,
        *small_grads,
        grad_mix.astype(F32),
        grad_n2,
        grad_gu1,
        grad_d1.astype(F32),
        grad_n3,
        grad_qkv,
        grad_ao,
        grad_n4,
        grad_gu2,
        grad_d2.astype(F32),
    )


def solution(mesh):
    chunks = mesh.shape["seq"] // W
    view = Mesh(mesh.devices.reshape(chunks, W, mesh.shape["fsdp"]), ("t", "p", "c"))
    every = ("t", "p", "c")
    tokens = P("c", ("t", "p"), None)
    vector, rows, cols = P(every), P(every, None), P(None, every)
    placed = (
        tokens, P("c", ("t", "p")), tokens,
        vector, rows, cols, vector, rows, cols, vector, rows, vector, rows,
        vector, rows, rows, vector, rows, rows, vector, rows, rows,
    )
    return jax.shard_map(
        local,
        mesh=view,
        in_specs=placed,
        out_specs=(tokens, tokens) + placed[3:],
        check_vma=False,
    )
```
